32 devices in a mesh: row: 8 (over z, x), col: 4 (over y, core).
Axes of the slice: x: 2, y: 2, z: 4, core: 2. Of those that a mesh axis runs over, the one named last changes fastest.
Arguments:
- vectors: float32 [8192, 1024], P(('row', 'col')), may hold values from -6 to 6
- rotation: float32 [1024, 1024], P(None, 'col'), may hold values from -0.1875 to 0.1875
- blocks: bfloat16 [64, 16, 128, 128], P('row'), may hold values from -0.0625 to 0.0625
- cols: int32 [64, 16], P('row'), may hold values from 0 to 15, as said below
- lists: int32 [8, 2, 4], P('row'), may hold values from 0 to 7, as said below
- counts: int32 [8], P('row'), may hold values from 4 to 8, as said below
Outputs:
- filtered: float32 [1024, 8192], P('col', 'row')
The draws below stay inside these ranges and needn't reach their ends.
Inputs may be any that keep to these rules, and one draw needn't show every extreme that they name: `counts`: at least one group uses all 8 slots. Every entry of lists[r] is below counts[r], and lists[r, j, 0] = counts[r] - 1; entries may repeat. cols[t, 0] = 4 + t % 8, the block row itself; on valid block rows of group r every slot between 4 and 15 that names an own block row is below 4 + counts[r].
All inputs are finite; a program needn't handle non-finite values.
Results may differ from the reference program's by a relative error of at most 0.0065.
Values may be sent and summed in bfloat16 or wider, within the bound.
No kernel may reach another device: no remote copies, remote signals or barrier semaphores. Data moves between devices by JAX's collectives and lax.ppermute only.
A program may use at most 64 MiB of HBM per device.

```python
import jax
import jax.numpy as jnp
from jax import lax

NV = 1024
BS = 128
NBLK = 16
STEPS = 10
CAP = 8
NB = 4
TBR = 64
ROWS = 8192


def structure(key):
    base = jax.random.fold_in(key, 7)
    keys = jax.random.split(base, 6)
    groups = TBR // CAP
    lowest = max(1, CAP // 2)
    counts = jax.random.randint(keys[0], (groups,), lowest, CAP + 1)
    forced = jax.random.randint(keys[1], (), 0, groups)
    counts = jnp.where(jnp.arange(groups) == forced, CAP, counts).astype(jnp.int32)
    raw_lists = jax.random.randint(keys[2], (groups, 2, NB), 0, 1048576) % counts[:, None, None]
    lists = jnp.where(jnp.arange(NB)[None, None, :] == 0, counts[:, None, None] - 1, raw_lists).astype(jnp.int32)
    kinds = jax.random.randint(keys[3], (groups, CAP, NBLK), 0, 3)
    own_index = jax.random.randint(keys[4], (groups, CAP, NBLK), 0, 1048576) % counts[:, None, None]
    near_index = jax.random.randint(keys[5], (groups, CAP, NBLK), 0, NB)
    slots = jnp.where(kinds == 0, near_index, jnp.where(kinds == 1, NB + own_index, NB + CAP + near_index))
    diagonal = NB + jnp.arange(CAP)[None, :, None] + jnp.zeros((groups, CAP, NBLK), jnp.int32)
    slots = jnp.where(jnp.arange(NBLK)[None, None, :] == 0, diagonal, slots)
    return (counts, lists, slots.reshape(groups * CAP, NBLK).astype(jnp.int32))


def draw_counts(key, part):
    return structure(key)[0]


def draw_lists(key, part):
    return structure(key)[1]


def draw_cols(key, part):
    return structure(key)[2]


def levels(rng, dims, pieces, least, largest):
    level, own = 1.0, jax.random.fold_in(rng, 6)
    for axis_at, blocks in pieces:
        heights = jnp.exp(jax.random.uniform(jax.random.fold_in(own, axis_at), (blocks,), jnp.float32, least / len(pieces), largest / len(pieces)))
        level = level * jnp.repeat(heights, dims[axis_at] // blocks).reshape([-1 if axis == axis_at else 1 for axis in range(len(dims))])
    return level


def centred(key, dims, deviation, reach, cuts=(), kind=jnp.bfloat16):
    values = jax.random.normal(key, dims, jnp.float32) * deviation
    if len(cuts) > 0:
        values = levels(key, dims, cuts, -0.22, 0.18) * values
    return jnp.clip(values, min=-reach, max=reach).astype(kind)


def setup_inputs(seed: int = 0) -> dict:
    seeds = jax.random.split(jax.random.key(seed), 7)
    vectors = centred(seeds[0], (ROWS, NV), 1.0, 6.0, ((0, 32),), jnp.float32)
    rotation = centred(seeds[1], (NV, NV), NV ** -0.5, 0.1875, ((1, 4),), jnp.float32)
    blocks = centred(seeds[2], (TBR, NBLK, BS, BS), (4 * NBLK * BS) ** -0.5, 0.0625, ((0, 8),))
    cols = draw_cols(jax.random.fold_in(seeds[6], 71), 0)
    lists = draw_lists(jax.random.fold_in(seeds[6], 71), 0)
    counts = draw_counts(jax.random.fold_in(seeds[6], 71), 0)
    return {"vectors": vectors, "rotation": rotation, "blocks": blocks, "cols": cols, "lists": lists, "counts": counts}


def apply_blocks(zfield, blocks, cols, lists, valid):
    groups = lists.shape[0]
    cap = zfield.shape[1]
    up_rows = jax.vmap(lambda field, index: field[index])(zfield, lists[:, 0])
    down_rows = jax.vmap(lambda field, index: field[index])(zfield, lists[:, 1])
    zero = jnp.zeros((1,) + up_rows.shape[1:], zfield.dtype)
    before = jnp.concatenate([zero, up_rows[:-1]], axis=0)
    after = jnp.concatenate([down_rows[1:], zero], axis=0)
    source = jnp.concatenate([before, zfield, after], axis=1)
    blk = blocks.reshape((groups, cap) + blocks.shape[1:])
    slot = cols.reshape(groups, cap, cols.shape[1])

    def one_group(items):
        src, mats, where = items
        picked = src[where].astype(jnp.float32)
        return jnp.einsum('bkij,bkjn->bin', mats.astype(jnp.float32), picked, precision=lax.Precision.HIGHEST)

    result = lax.map(one_group, (source, blk, slot))
    return result * valid[:, :, None, None]


def reference(vectors, rotation, blocks, cols, lists, counts):
    groups = lists.shape[0]
    cap = blocks.shape[0] // groups
    width = blocks.shape[2]
    rotated = jnp.dot(vectors, rotation, precision=lax.Precision.HIGHEST, preferred_element_type=jnp.float32)
    valid = (jnp.arange(cap, dtype=jnp.int32)[None, :] < counts[:, None]).astype(jnp.float32)
    previous = rotated.reshape(groups, cap, width, rotated.shape[1]) * valid[:, :, None, None]
    current = apply_blocks(previous.astype(jnp.bfloat16), blocks, cols, lists, valid)
    for step in range(STEPS - 1):
        following = 2.0 * apply_blocks(current.astype(jnp.bfloat16), blocks, cols, lists, valid) - previous
        previous = current
        current = following
    return current.reshape(-1, current.shape[3]).T
```

```python
import functools

import jax
import jax.numpy as jnp
from jax import lax
from jax.experimental import pallas as pl
from jax.experimental.pallas import tpu as pltpu
from jax.sharding import PartitionSpec as P

STEPS = 10
AXES = ("row", "col")
F32, BF16 = jnp.float32, jnp.bfloat16
VMEM = pl.BlockSpec(memory_space=pltpu.VMEM)
SMEM = pl.BlockSpec(memory_space=pltpu.SMEM)
ANY = pl.BlockSpec(memory_space=pl.ANY)


def patterns(rows, cols):
    at = lambda r, c: r * cols + c
    every = [(r, c) for r in range(rows) for c in range(cols)]
    role = lambda r, c: (c % 2) ^ (r // 2 % 2)
    keeps = lambda r, c: role(r, c) == r % 2
    other = lambda r, c: (r ^ 1, c ^ 1)
    out = {}
    out["field"] = [
        (at(r, c), at(r - r % 2 + c % 2, c - c % 2 + ((r % 2) ^ (r // 2 % 2)))) for r, c in every
    ]
    out["back"] = [(d, s) for s, d in out["field"]]
    out["blocks"] = [(at(r, c), at(*other(r, c))) for r, c in every if not keeps(r, c)]
    out["meta"] = [
        (at(r, c), at(r, c) if keeps(r, c) else at(*other(r, c))) for r, c in every
    ]
    out["across"] = [(at(r, c), at(r, c ^ 2)) for r, c in every if not keeps(r, c)]
    out["near"] = [(at(r, c), at(r, c ^ 1)) for r, c in every]
    out["far"] = [
        (at(r, c), at(r + (2 if role(r, c) else -2), c))
        for r, c in every
        if 0 <= r + (2 if role(r, c) else -2) < rows
    ]
    return out


def call(kernel, outs, in_specs, out_specs, name, scratch=(), aliases={}, mib=24):
    return pl.pallas_call(
        kernel,
        out_shape=outs,
        in_specs=in_specs,
        out_specs=out_specs,
        scratch_shapes=scratch,
        input_output_aliases=aliases,
        compiler_params=pltpu.CompilerParams(vmem_limit_bytes=mib << 20),
        name=name,
    )


def rotate_kernel(places, width, info, rotation, *refs):
    pieces, out = refs[: len(places)], refs[len(places)]
    rot = rotation[...]
    high = rot.astype(BF16)
    low = (rot - high.astype(F32)).astype(BF16)
    mine, used = info[0], info[1] * width
    for place, piece in zip(places, pieces):
        rows = piece.shape[0]
        first = pl.multiple_of((mine ^ place) * rows, rows)
        x = piece[...]
        y = jnp.dot(x, high, preferred_element_type=F32) + jnp.dot(x, low, preferred_element_type=F32)
        at = first + lax.broadcasted_iota(jnp.int32, y.shape, 0)
        out[pl.ds(first, rows), :] = jnp.where(at < used, y, 0.0).astype(BF16)


def build_kernel(base, count, cap, nblk, width, meta, blocks, moved, *refs):
    near_out, far_out = refs[-7:-5]
    raw, total, near_buf, far_buf, sems = refs[-5:]
    role, keep, half, used = meta[0], meta[1], meta[2], meta[3]
    near_w, far_w = near_buf.shape[2], far_buf.shape[2]
    own = 4 * width

    def place(step):
        return lax.rem(base + step + half * (cap // 2), cap)

    def load(step, start):
        for flag, src in ((keep == 1, blocks.at[place(step)]), (keep == 0, moved.at[step])):
            @pl.when(flag)
            def _():
                copy = pltpu.make_async_copy(src, raw.at[step], sems.at[step])
                copy.start() if start else copy.wait()

    def stores(step):
        rows = pl.ds(pl.multiple_of(place(step) * width, width), width)
        return (
            pltpu.make_async_copy(near_buf.at[step], near_out.at[rows, :], sems.at[count + 2 * step]),
            pltpu.make_async_copy(far_buf.at[step], far_out.at[rows, :], sems.at[count + 2 * step + 1]),
        )

    for step in range(count):
        load(step, True)
    for step in range(count):
        load(step, False)
        t = place(step)
        total[...] = jnp.zeros_like(total)
        for k in range(nblk):
            slot = meta[4 + t * nblk + k]
            lanes = slot_place(slot, role, cap, nblk) * width
            lanes = pl.ds(pl.multiple_of(lanes, width), width)
            total[:, lanes] = total[:, lanes] + raw[step, k].astype(F32)
        scale = jnp.where(t < used, 1.0, 0.0).astype(F32)
        near_buf[step] = (total[:, :near_w] * scale).astype(BF16)
        far_buf[step] = (total[:, near_w:] * scale).astype(BF16)
        for copy in stores(step):
            copy.start()
    for step in range(count):
        for copy in stores(step):
            copy.wait()


def slot_place(slot, role, cap, slots):
    edge = (slots - cap) // 2
    first = jnp.where(slot < edge, slot + slots - edge, slot - edge)
    second = jnp.where(slot < edge, slot + cap, jnp.where(slot < edge + cap, slot - edge, slot))
    return jnp.where(role == 0, first, second)


def pack(lists, field, near_send, far_send, width):
    edge = near_send.shape[0] // width
    for i in range(edge):
        for which, send in ((0, near_send), (edge, far_send)):
            row = pl.multiple_of(lists[which + i] * width, width)
            send[i * width : (i + 1) * width, :] = field[pl.ds(row, width), :]


def pack_kernel(width, lists, field, near_send, far_send):
    pack(lists, field, near_send, far_send, width)


def local_kernel(near_op, field, near, acc):
    rows = field.shape[0]
    acc[...] = jnp.dot(near_op[:, :rows], field[...], preferred_element_type=F32) + jnp.dot(
        near_op[:, rows:], near[...], preferred_element_type=F32
    )


def finish_kernel(step, last, width, lists, acc, far_op, far, *refs):
    total = acc[...] + jnp.dot(far_op[...], far[...], preferred_element_type=F32)
    if step > 0:
        older, refs = refs[0], refs[1:]
        total = 2.0 * total - older[...].astype(F32)
    if last:
        refs[0][...] = total.T.astype(BF16)
        return
    value, field, near_send, far_send = refs
    value[...] = total
    field[...] = total.astype(BF16)
    pack(lists, field, near_send, far_send, width)


def body(vectors, rotation, blocks, cols, lists, counts):
    rows, columns = lax.axis_size("row"), lax.axis_size("col")
    ways = patterns(rows, columns)
    send = lambda x, way: lax.ppermute(x, AXES, ways[way])
    r, c = lax.axis_index("row"), lax.axis_index("col")
    cap, nblk, width = blocks.shape[0], blocks.shape[1], blocks.shape[2]
    edge = lists.shape[2]
    panel = rotation.shape[1]
    height = cap * width
    slots = cap + 2 * edge
    role = (c % 2) ^ (r // 2 % 2)
    keep = (role == r % 2).astype(jnp.int32)
    half = c // 2 % 2
    sds = jax.ShapeDtypeStruct

    meta = send(jnp.concatenate([counts, cols.reshape(-1), lists.reshape(-1)]), "meta")
    used, slot_table, tables = meta[:1], meta[1 : 1 + cap * nblk], meta[1 + cap * nblk :].reshape(2, edge)
    order = jnp.stack([role, 1 - role])
    send_lists = tables[order].reshape(-1)
    info = jnp.concatenate([jnp.stack([role, keep, half]), used, slot_table]).astype(jnp.int32)

    pieces = {0: vectors.astype(BF16)}
    bit = columns // 2
    while bit:
        for place in list(pieces):
            pieces[place ^ bit] = lax.ppermute(
                pieces[place], "col", [(k, k ^ bit) for k in range(columns)]
            )
        bit //= 2

    hc = cap // 2
    chunk = 2
    mine = lax.dynamic_slice_in_dim(blocks, half * hc, hc, 0)
    direct = [send(mine[k : k + chunk], "blocks") for k in range(0, hc, chunk)]
    relayed = [send(x, "across") for x in direct]

    field = call(
        functools.partial(rotate_kernel, tuple(pieces), width),
        sds((height, panel), BF16), [SMEM, VMEM] + [VMEM] * len(pieces), VMEM, "rotate",
    )(jnp.stack([c.astype(jnp.int32), counts[0]]), rotation, *pieces.values())
    field = send(field, "field")

    ops = ()
    op_shapes = (sds((height, height + edge * width), BF16), sds((height, edge * width), BF16))
    for k, moved in enumerate(direct + relayed):
        ops = call(
            functools.partial(build_kernel, k * chunk, chunk, cap, nblk, width),
            op_shapes, [SMEM, ANY, ANY] + [ANY] * len(ops), (ANY, ANY), "build",
            scratch=(
                pltpu.VMEM((chunk, nblk, width, width), BF16),
                pltpu.VMEM((width, slots * width), F32),
                pltpu.VMEM((chunk, width, height + edge * width), BF16),
                pltpu.VMEM((chunk, width, edge * width), BF16),
                pltpu.SemaphoreType.DMA((3 * chunk,)),
            ),
            aliases={3: 0, 4: 1} if ops else {},
        )(info, blocks, moved, *ops)
    near_op, far_op = ops

    sent = (sds((edge * width, panel), BF16),) * 2
    near_send, far_send = call(
        functools.partial(pack_kernel, width), sent, [SMEM, VMEM], (VMEM, VMEM), "pack"
    )(send_lists, field)
    older, newer = None, field
    for step in range(STEPS):
        far, near = send(far_send, "far"), send(near_send, "near")
        acc = call(local_kernel, sds((height, panel), F32), [VMEM] * 3, VMEM, "local")(near_op, field, near)
        last = step == STEPS - 1
        out = sds((panel, height), BF16) if last else (
            (sds((height, panel), F32), sds((height, panel), BF16)) + sent
        )
        extra = [] if older is None else [older]
        result = call(
            functools.partial(finish_kernel, step, last, width),
            out, [SMEM] + [VMEM] * (3 + len(extra)), VMEM if last else (VMEM,) * 4, "finish",
        )(send_lists, acc, far_op, far, *extra)
        if not last:
            older = newer
            newer, field, near_send, far_send = result
    return send(result, "back").astype(F32)


def solution(mesh):
    return jax.shard_map(
        body,
        mesh=mesh,
        in_specs=(
            P(("row", "col"), None),
            P(None, "col"),
            P("row", None, None, None),
            P("row", None),
            P("row", None, None),
            P("row"),
        ),
        out_specs=P("col", "row"),
        check_vma=False,
    )
```

```python
import functools

import jax
import jax.numpy as jnp
from jax import lax
from jax.experimental import pallas as pl
from jax.experimental.pallas import tpu as pltpu
from jax.sharding import PartitionSpec as P

STEPS = 10
AXES = ("row", "col")
F32, BF16 = jnp.float32, jnp.bfloat16
VMEM = pl.BlockSpec(memory_space=pltpu.VMEM)
SMEM = pl.BlockSpec(memory_space=pltpu.SMEM)
HBM = pl.BlockSpec(memory_space=pltpu.HBM)
ANY = pl.BlockSpec(memory_space=pl.ANY)


def patterns(rows, cols):
    every = [(r, c) for r in range(rows) for c in range(cols)]
    keeps = lambda r, c: r % 2 == c % 2

    def far(r, c):
        to = r + 2 if c % 2 else r - 2
        return (to, c ^ 1) if 0 <= to < rows else (r ^ 1, c)

    ways = {
        "trade": lambda r, c: (r ^ 2, c) if keeps(r, c) else (r ^ 1, c ^ 1),
        "across": lambda r, c: (r ^ 2, c) if keeps(r, c) else (r, c ^ 2),
        "near": lambda r, c: (r, c ^ 1),
        "far": far,
    }
    at = lambda place: place[0] * cols + place[1]
    return {name: [(at(p), at(way(*p))) for p in every] for name, way in ways.items()}


def call(kernel, outs, in_specs, out_specs, name, scratch=(), aliases={}, mib=12):
    return pl.pallas_call(
        kernel,
        out_shape=outs,
        in_specs=in_specs,
        out_specs=out_specs,
        scratch_shapes=scratch,
        input_output_aliases=aliases,
        compiler_params=pltpu.CompilerParams(vmem_limit_bytes=mib << 20),
        name=name,
    )


def rotate_kernel(places, width, info, rotation, *refs):
    pieces, out = refs[: len(places)], refs[len(places)]
    rot = rotation[...]
    high = rot.astype(BF16)
    low = (rot - high.astype(F32)).astype(BF16)
    mine, used = info[0], info[1] * width
    for place, piece in zip(places, pieces):
        rows = piece.shape[0]
        first = pl.multiple_of((mine ^ place) * rows, rows)
        x = piece[...]
        y = jnp.dot(x, high, preferred_element_type=F32) + jnp.dot(x, low, preferred_element_type=F32)
        at = first + lax.broadcasted_iota(jnp.int32, y.shape, 0)
        out[pl.ds(first, rows), :] = jnp.where(at < used, y, 0.0).astype(BF16)


def build_kernel(base, count, cap, nblk, width, meta, blocks, moved, *refs):
    near_out, far_out = refs[-7:-5]
    raw, total, near_buf, far_buf, sems = refs[-5:]
    role, keep, half, edge, used = meta[0], meta[1], meta[2], meta[3], meta[4]
    near_w, far_w = near_buf.shape[2], far_buf.shape[2]

    def place(step):
        return lax.rem(base + step + half * (cap // 2), cap)

    def load(step, start):
        for flag, src in ((keep == 1, blocks.at[place(step)]), (keep == 0, moved.at[step])):
            @pl.when(flag)
            def _():
                copy = pltpu.make_async_copy(src, raw.at[step], sems.at[step])
                copy.start() if start else copy.wait()

    def stores(step):
        rows = pl.ds(pl.multiple_of(place(step) * width, width), width)
        return (
            pltpu.make_async_copy(near_buf.at[step], near_out.at[rows, :], sems.at[count + 2 * step]),
            pltpu.make_async_copy(far_buf.at[step], far_out.at[rows, :], sems.at[count + 2 * step + 1]),
        )

    for step in range(count):
        load(step, True)
    for step in range(count):
        load(step, False)
        t = place(step)
        total[...] = jnp.zeros_like(total)
        for k in range(nblk):
            slot = meta[5 + t * nblk + k]
            lanes = slot_place(slot, role, cap, nblk) * width
            lanes = pl.ds(pl.multiple_of(lanes, width), width)
            total[:, lanes] = total[:, lanes] + raw[step, k].astype(F32)
        scale = jnp.where(t < used, 1.0, 0.0).astype(F32)
        near_buf[step] = (total[:, :near_w] * scale).astype(BF16)
        far_buf[step] = (total[:, near_w:] * jnp.where(edge == 1, 0.0, scale)).astype(BF16)
        for copy in stores(step):
            copy.start()
    for step in range(count):
        for copy in stores(step):
            copy.wait()


def slot_place(slot, role, cap, slots):
    edge = (slots - cap) // 2
    first = jnp.where(slot < edge, slot + slots - edge, slot - edge)
    second = jnp.where(slot < edge, slot + cap, jnp.where(slot < edge + cap, slot - edge, slot))
    return jnp.where(role == 0, first, second)


def pick(lists, first, edge, width):
    return [pl.ds(pl.multiple_of(lists[first + i] * width, width), width) for i in range(edge)]


def pack_kernel(width, edge, lists, own, moved, field, near_send, far_send):
    @pl.when(lists[2 * edge] == 1)
    def _():
        field[...] = own[...]

    @pl.when(lists[2 * edge] == 0)
    def _():
        field[...] = moved[...]

    for first, send in ((0, near_send), (edge, far_send)):
        for i, rows in enumerate(pick(lists, first, edge, width)):
            send[i * width : (i + 1) * width, :] = field[rows, :]


def local_kernel(near_op, field, near, acc):
    rows = field.shape[0]
    acc[...] = jnp.dot(near_op[:, :rows], field[...], preferred_element_type=F32) + jnp.dot(
        near_op[:, rows:], near[...], preferred_element_type=F32
    )


def ahead_kernel(width, edge, lists, acc, far_op, far, *refs):
    rows = pick(lists, edge, edge, width)
    join = lambda ref: jnp.concatenate([ref[r, :] for r in rows], axis=0)
    total = join(acc) + jnp.dot(join(far_op), far[...], preferred_element_type=F32)
    if len(refs) > 1:
        total = 2.0 * total - join(refs[0]).astype(F32)
    refs[-1][...] = total.astype(BF16)


def finish_kernel(first, last, width, edge, lists, acc, far_op, far, *refs):
    total = acc[...] + jnp.dot(far_op[...], far[...], preferred_element_type=F32)
    if not first:
        older, refs = refs[0], refs[1:]
        total = 2.0 * total - older[...].astype(F32)
    if last:
        refs[0][...] = total.T.astype(BF16)
        return
    value, field, near_send = refs
    value[...] = total
    field[...] = total.astype(BF16)
    for i, rows in enumerate(pick(lists, 0, edge, width)):
        near_send[i * width : (i + 1) * width, :] = field[rows, :]


def body(vectors, rotation, blocks, cols, lists, counts):
    rows, columns = lax.axis_size("row"), lax.axis_size("col")
    ways = patterns(rows, columns)
    send = lambda x, way: lax.ppermute(x, AXES, ways[way])
    r, c = lax.axis_index("row"), lax.axis_index("col")
    cap, nblk, width = blocks.shape[0], blocks.shape[1], blocks.shape[2]
    edge = lists.shape[2]
    panel = rotation.shape[1]
    height = cap * width
    slots = cap + 2 * edge
    role = c % 2
    keep = role == r % 2
    half = c // 2 % 2
    at_edge = jnp.where(role == 0, r < 2, r >= rows - 2)
    flag = lambda x: x.astype(jnp.int32)
    sds = jax.ShapeDtypeStruct

    own_meta = jnp.concatenate([counts, cols.reshape(-1), lists.reshape(-1)])
    meta = jnp.where(keep, own_meta, send(own_meta, "trade"))
    tables = meta[1 + cap * nblk :].reshape(2, edge)
    send_lists = jnp.where(role == 0, tables, tables[::-1]).reshape(-1)
    send_lists = jnp.concatenate([send_lists, flag(keep)[None]])
    info = jnp.concatenate([jnp.stack([flag(x) for x in (role, keep, half, at_edge)]), meta[: 1 + cap * nblk]])

    pieces = {0: vectors.astype(BF16)}
    bit = columns // 2
    while bit:
        for place in list(pieces):
            pieces[place ^ bit] = lax.ppermute(
                pieces[place], "col", [(k, k ^ bit) for k in range(columns)]
            )
        bit //= 2

    hc = cap // 2
    chunk = 1
    mine = lax.dynamic_slice_in_dim(blocks, half * hc, hc, 0)
    direct = [send(mine[k : k + chunk], "trade") for k in range(0, hc, chunk)]
    relayed = [send(x, "across") for x in direct]

    field = call(
        functools.partial(rotate_kernel, tuple(pieces), width),
        sds((height, panel), BF16), [SMEM, VMEM] + [VMEM] * len(pieces), VMEM, "rotate",
    )(jnp.stack([c.astype(jnp.int32), counts[0]]), rotation, *pieces.values())
    moved_field = send(field, "trade")

    held = pltpu.with_memory_space_constraint(blocks, pltpu.HBM)
    ops = ()
    op_shapes = (sds((height, height + edge * width), BF16), sds((height, edge * width), BF16))
    for k, moved in enumerate(direct + relayed):
        ops = call(
            functools.partial(build_kernel, k * chunk, chunk, cap, nblk, width),
            op_shapes, [SMEM, HBM, ANY] + [ANY] * len(ops), (ANY, ANY), "build",
            scratch=(
                pltpu.VMEM((chunk, nblk, width, width), BF16),
                pltpu.VMEM((width, slots * width), F32),
                pltpu.VMEM((chunk, width, height + edge * width), BF16),
                pltpu.VMEM((chunk, width, edge * width), BF16),
                pltpu.SemaphoreType.DMA((3 * chunk,)),
            ),
            aliases={3: 0, 4: 1} if ops else {},
        )(info, held, moved, *ops)
    near_op, far_op = ops

    sent = sds((edge * width, panel), BF16)
    wide = lambda kind: sds((height, panel), kind)
    field, near_send, far_send = call(
        functools.partial(pack_kernel, width, edge), (wide(BF16), sent, sent),
        [SMEM, VMEM, VMEM], (VMEM,) * 3, "pack",
    )(send_lists, field, moved_field)
    older, newer = (), field
    for step in range(STEPS):
        far, near = send(far_send, "far"), send(near_send, "near")
        acc = call(local_kernel, wide(F32), [VMEM] * 3, VMEM, "local")(near_op, field, near)
        last = step == STEPS - 1
        given = (send_lists, acc, far_op, far) + older
        specs = [SMEM] + [VMEM] * (len(given) - 1)
        if not last:
            far_send = call(functools.partial(ahead_kernel, width, edge), sent, specs, VMEM, "ahead")(*given)
        result = call(
            functools.partial(finish_kernel, step == 0, last, width, edge),
            sds((panel, height), BF16) if last else (wide(F32), wide(BF16), sent),
            specs, VMEM if last else (VMEM,) * 3, "finish",
        )(*given)
        if not last:
            older = (newer,)
            newer, field, near_send = result
    return jnp.where(keep, result, send(result, "trade")).astype(F32)


def solution(mesh):
    return jax.shard_map(
        body,
        mesh=mesh,
        in_specs=(
            P(("row", "col"), None),
            P(None, "col"),
            P("row", None, None, None),
            P("row", None),
            P("row", None, None),
            P("row"),
        ),
        out_specs=P("col", "row"),
        check_vma=False,
    )
```

```python
import functools

import jax
import jax.numpy as jnp
from jax import lax
from jax.experimental import pallas as pl
from jax.experimental.pallas import tpu as pltpu
from jax.sharding import PartitionSpec as P


STEPS = 10
AXES = ("row", "col")
F32, BF16 = jnp.float32, jnp.bfloat16
VMEM = pl.BlockSpec(memory_space=pltpu.VMEM)
SMEM = pl.BlockSpec(memory_space=pltpu.SMEM)
HBM = pl.BlockSpec(memory_space=pltpu.HBM)
ANY = pl.BlockSpec(memory_space=pl.ANY)


def patterns(rows, cols):
    every = [(r, c) for r in range(rows) for c in range(cols)]
    keeps = lambda r, c: r % 2 == c % 2

    def far(r, c):
        to = r + 2 if c % 2 else r - 2
        return (to, c ^ 1) if 0 <= to < rows else (r ^ 1, c)

    ways = {
        "trade": lambda r, c: (r ^ 2, c) if keeps(r, c) else (r ^ 1, c ^ 1),
        "across": lambda r, c: (r, c ^ 2),
        "near": lambda r, c: (r, c ^ 1),
        "far": far,
    }
    at = lambda place: place[0] * cols + place[1]
    pairs = {name: [(at(p), at(way(*p))) for p in every] for name, way in ways.items()}
    pairs["across"] = [(at(p), at(ways["across"](*p))) for p in every if not keeps(*p)]
    return pairs


def call(kernel, outs, in_specs, out_specs, scratch=(), aliases={}, mib=12):
    return pl.pallas_call(
        kernel,
        out_shape=outs,
        in_specs=in_specs,
        out_specs=out_specs,
        scratch_shapes=scratch,
        input_output_aliases=aliases,
        compiler_params=pltpu.CompilerParams(vmem_limit_bytes=mib << 20),
    )


def rotate_kernel(places, width, info, rotation, *refs):
    pieces, out = refs[: len(places)], refs[len(places)]
    rot = rotation[...]
    high = rot.astype(BF16)
    low = (rot - high.astype(F32)).astype(BF16)
    mine, used = info[0], info[1] * width
    for place, piece in zip(places, pieces):
        rows = piece.shape[0]
        first = pl.multiple_of((mine ^ place) * rows, rows)
        x = piece[...]
        y = jnp.dot(x, high, preferred_element_type=F32) + jnp.dot(x, low, preferred_element_type=F32)
        at = first + lax.broadcasted_iota(jnp.int32, y.shape, 0)
        out[pl.ds(first, rows), :] = jnp.where(at < used, y, 0.0).astype(BF16)


def build_kernel(step_at, direct, cap, nblk, width, meta, blocks, moved, *refs):
    near_out, far_out = refs[-7:-5]
    raw, total, near_buf, far_buf, sems = refs[-5:]
    role, keep, half, edge, used = meta[0], meta[1], meta[2], meta[3], meta[4]
    near_w = near_buf.shape[1]

    t = row_of(half, step_at, direct, cap)
    parts = 4
    piece = nblk // parts
    for flag, src in ((keep == 1, blocks.at[t]), (keep == 0, moved.at[0])):
        copies = [
            pltpu.make_async_copy(
                src.at[pl.ds(p * piece, piece)], raw.at[pl.ds(p * piece, piece)], sems.at[p]
            )
            for p in range(parts)
        ]

        @pl.when(flag)
        def _():
            for copy in copies:
                copy.start()

    total[...] = jnp.zeros_like(total)
    for copy in copies:
        copy.wait()
    for k in range(nblk):
        slot = meta[5 + t * nblk + k]
        lanes = slot_place(slot, role, cap, nblk) * width
        lanes = pl.ds(pl.multiple_of(lanes, width), width)
        total[:, lanes] = total[:, lanes] + raw[k].astype(F32)
    scale = jnp.where(t < used, 1.0, 0.0).astype(F32)
    near_buf[...] = (total[:, :near_w] * scale).astype(BF16)
    far_buf[...] = (total[:, near_w:] * jnp.where(edge == 1, 0.0, scale)).astype(BF16)
    rows = pl.ds(pl.multiple_of(t * width, width), width)
    stores = (
        pltpu.make_async_copy(near_buf, near_out.at[rows, :], sems.at[parts]),
        pltpu.make_async_copy(far_buf, far_out.at[rows, :], sems.at[parts + 1]),
    )
    for copy in stores:
        copy.start()
    for copy in stores:
        copy.wait()


def row_of(half, step, direct, cap):
    flip = half if direct else 1 - half
    return jnp.where(flip == 1, cap - 1 - step, step)


def stage_kernel(cap, half, blocks, *refs):
    outs, sems = refs[:-1], refs[-1]
    nblk = blocks.shape[1]
    piece = nblk // 4
    copies = [
        pltpu.make_async_copy(
            blocks.at[row_of(half[0], step, True, cap), pl.ds(p * piece, piece)],
            out.at[0, pl.ds(p * piece, piece)], sems.at[step, p],
        )
        for step, out in enumerate(outs) for p in range(4)
    ]
    for copy in copies:
        copy.start()
    for copy in copies:
        copy.wait()


def slot_place(slot, role, cap, slots):
    edge = (slots - cap) // 2
    first = jnp.where(slot < edge, slot + slots - edge, slot - edge)
    second = jnp.where(slot < edge, slot + cap, jnp.where(slot < edge + cap, slot - edge, slot))
    return jnp.where(role == 0, first, second)


def pick(lists, first, edge, width):
    return [pl.ds(pl.multiple_of(lists[first + i] * width, width), width) for i in range(edge)]


def pack_kernel(width, edge, lists, own, moved, field, near_send, far_send):
    @pl.when(lists[2 * edge] == 1)
    def _():
        field[...] = own[...]

    @pl.when(lists[2 * edge] == 0)
    def _():
        field[...] = moved[...]

    for first, send in ((0, near_send), (edge, far_send)):
        for i, rows in enumerate(pick(lists, first, edge, width)):
            send[i * width : (i + 1) * width, :] = field[rows, :]


def local_kernel(near_op, field, near, acc):
    rows = field.shape[0]
    acc[...] = jnp.dot(near_op[:, :rows], field[...], preferred_element_type=F32) + jnp.dot(
        near_op[:, rows:], near[...], preferred_element_type=F32
    )


def ahead_kernel(width, edge, lists, acc, far_op, far, *refs):
    rows = pick(lists, edge, edge, width)
    join = lambda ref: jnp.concatenate([ref[r, :] for r in rows], axis=0)
    total = join(acc) + jnp.dot(join(far_op), far[...], preferred_element_type=F32)
    if len(refs) > 1:
        total = 2.0 * total - join(refs[0]).astype(F32)
    refs[-1][...] = total.astype(BF16)


def finish_kernel(first, last, width, edge, lists, acc, far_op, far, *refs):
    total = acc[...] + jnp.dot(far_op[...], far[...], preferred_element_type=F32)
    if not first:
        older, refs = refs[0], refs[1:]
        total = 2.0 * total - older[...].astype(F32)
    if last:
        refs[0][...] = total.T.astype(BF16)
        return
    value, field, near_send = refs
    value[...] = total
    field[...] = total.astype(BF16)
    for i, rows in enumerate(pick(lists, 0, edge, width)):
        near_send[i * width : (i + 1) * width, :] = field[rows, :]


def body(vectors, rotation, blocks, cols, lists, counts):
    rows, columns = lax.axis_size("row"), lax.axis_size("col")
    ways = patterns(rows, columns)

    def send(x, way):
        return lax.ppermute(x, AXES, ways[way])

    r, c = lax.axis_index("row"), lax.axis_index("col")
    cap, nblk, width = blocks.shape[0], blocks.shape[1], blocks.shape[2]
    edge = lists.shape[2]
    panel = rotation.shape[1]
    height = cap * width
    slots = cap + 2 * edge
    role = c % 2
    keep = role == r % 2
    half = c // 2 % 2
    at_edge = jnp.where(role == 0, r < 2, r >= rows - 2)
    flag = lambda x: x.astype(jnp.int32)
    sds = jax.ShapeDtypeStruct

    own_meta = jnp.concatenate([counts, cols.reshape(-1), lists.reshape(-1)])
    meta = jnp.where(keep, own_meta, send(own_meta, "trade"))
    tables = meta[1 + cap * nblk :].reshape(2, edge)
    send_lists = jnp.where(role == 0, tables, tables[::-1]).reshape(-1)
    send_lists = jnp.concatenate([send_lists, flag(keep)[None]])
    info = jnp.concatenate([jnp.stack([flag(x) for x in (role, keep, half, at_edge)]), meta[: 1 + cap * nblk]])

    pieces = {0: vectors.astype(BF16)}
    bit = columns // 2
    while bit:
        for place in list(pieces):
            pieces[place ^ bit] = lax.ppermute(
                pieces[place], "col", [(k, k ^ bit) for k in range(columns)]
            )
        bit //= 2

    held = pltpu.with_memory_space_constraint(blocks, pltpu.HBM)
    relays = cap // 2 - 1
    straight = cap - relays
    row = sds((1, nblk, width, width), BF16)
    staged = call(
        functools.partial(stage_kernel, cap), (row,) * straight, [SMEM, HBM], (ANY,) * straight,
        scratch=(pltpu.SemaphoreType.DMA((straight, 4)),),
    )(flag(half)[None], held)
    moved = [(k, True, send(x, "trade")) for k, x in enumerate(staged)]
    moved[-1:-1] = [(k, False, send(moved[k][2], "across")) for k in range(relays)]

    field = call(
        functools.partial(rotate_kernel, tuple(pieces), width),
        sds((height, panel), BF16), [SMEM, VMEM] + [VMEM] * len(pieces), VMEM,
    )(jnp.stack([c.astype(jnp.int32), counts[0]]), rotation, *pieces.values())
    moved_field = send(field, "trade")

    ops = ()
    op_shapes = (sds((height, height + edge * width), BF16), sds((height, edge * width), BF16))
    for k, direct, rowk in moved:
        ops = call(
            functools.partial(build_kernel, k, direct, cap, nblk, width),
            op_shapes, [SMEM, HBM, ANY] + [ANY] * len(ops), (ANY, ANY),
            scratch=(
                pltpu.VMEM((nblk, width, width), BF16),
                pltpu.VMEM((width, slots * width), F32),
                pltpu.VMEM((width, height + edge * width), BF16),
                pltpu.VMEM((width, edge * width), BF16),
                pltpu.SemaphoreType.DMA((6,)),
            ),
            aliases={3: 0, 4: 1} if ops else {},
        )(info, held, rowk, *ops)
    near_op, far_op = ops

    sent = sds((edge * width, panel), BF16)
    wide = lambda kind: sds((height, panel), kind)
    field, near_send, far_send = call(
        functools.partial(pack_kernel, width, edge), (wide(BF16), sent, sent),
        [SMEM, VMEM, VMEM], (VMEM,) * 3,
    )(send_lists, field, moved_field)
    older, newer = (), field
    for step in range(STEPS):
        far, near = send(far_send, "far"), send(near_send, "near")
        acc = call(local_kernel, wide(F32), [VMEM] * 3, VMEM)(near_op, field, near)
        last = step == STEPS - 1
        given = (send_lists, acc, far_op, far) + older
        specs = [SMEM] + [VMEM] * (len(given) - 1)
        if not last:
            far_send = call(functools.partial(ahead_kernel, width, edge), sent, specs, VMEM)(*given)
        result = call(
            functools.partial(finish_kernel, step == 0, last, width, edge),
            sds((panel, height), BF16) if last else (wide(F32), wide(BF16), sent),
            specs, VMEM if last else (VMEM,) * 3,
        )(*given)
        if not last:
            older = (newer,)
            newer, field, near_send = result
    return jnp.where(keep, result, send(result, "trade")).astype(F32)


def solution(mesh):
    return jax.shard_map(
        body,
        mesh=mesh,
        in_specs=(
            P(("row", "col"), None),
            P(None, "col"),
            P("row", None, None, None),
            P("row", None),
            P("row", None, None),
            P("row"),
        ),
        out_specs=P("col", "row"),
        check_vma=False,
    )
```

```python
import functools

import jax
import jax.numpy as jnp
from jax import lax
from jax.experimental import pallas as pl
from jax.experimental.pallas import tpu as pltpu
from jax.sharding import PartitionSpec as P


STEPS = 10
AXES = ("row", "col")
F32, BF16 = jnp.float32, jnp.bfloat16
VMEM = pl.BlockSpec(memory_space=pltpu.VMEM)
SMEM = pl.BlockSpec(memory_space=pltpu.SMEM)
HBM = pl.BlockSpec(memory_space=pltpu.HBM)
ANY = pl.BlockSpec(memory_space=pl.ANY)


def patterns(rows, cols):
    every = [(r, c) for r in range(rows) for c in range(cols)]
    keeps = lambda r, c: r % 2 == c % 2

    def far(r, c):
        to = r + 2 if c % 2 else r - 2
        return (to, c ^ 1) if 0 <= to < rows else (r ^ 1, c)

    ways = {
        "trade": lambda r, c: (r ^ 2, c) if keeps(r, c) else (r ^ 1, c ^ 1),
        "across": lambda r, c: (r, c ^ 2),
        "near": lambda r, c: (r, c ^ 1),
        "far": far,
    }
    at = lambda place: place[0] * cols + place[1]
    pairs = {name: [(at(p), at(way(*p))) for p in every] for name, way in ways.items()}
    pairs["across"] = [(at(p), at(ways["across"](*p))) for p in every if not keeps(*p)]
    return pairs


def call(kernel, outs, in_specs, out_specs, scratch=(), aliases={}, mib=12):
    return pl.pallas_call(
        kernel,
        out_shape=outs,
        in_specs=in_specs,
        out_specs=out_specs,
        scratch_shapes=scratch,
        input_output_aliases=aliases,
        compiler_params=pltpu.CompilerParams(vmem_limit_bytes=mib << 20),
    )


def rotate_kernel(places, width, flags, counts, rotation, *refs):
    pieces, out = refs[: len(places)], refs[len(places)]
    rot = rotation[...]
    high = rot.astype(BF16)
    low = (rot - high.astype(F32)).astype(BF16)
    mine, used = flags[4], counts[0] * width
    for place, piece in zip(places, pieces):
        rows = piece.shape[0]
        first = pl.multiple_of((mine ^ place) * rows, rows)
        x = piece[...]
        y = jnp.dot(x, high, preferred_element_type=F32) + jnp.dot(x, low, preferred_element_type=F32)
        at = first + lax.broadcasted_iota(jnp.int32, y.shape, 0)
        out[pl.ds(first, rows), :] = jnp.where(at < used, y, 0.0).astype(BF16)


def build_kernel(steps, cap, nblk, width, info, blocks, *refs):
    moved, refs = refs[: len(steps)], refs[len(steps) :]
    near_out, far_out = refs[-7:-5]
    raw, total, near_buf, far_buf, sems = refs[-5:]
    role, keep, half, edge, used = (info[i] for i in range(5))
    near_w = near_buf.shape[2]
    parts = 4
    piece = nblk // parts
    rows = [row_of(half, step, direct, cap) for step, direct in steps]

    def loads(n, src):
        cut = lambda p: pl.ds(p * piece, piece)
        return [
            pltpu.make_async_copy(src.at[cut(p)], raw.at[n, cut(p)], sems.at[n, p]) for p in range(parts)
        ]

    for flag in (1, 0):
        @pl.when(keep == flag)
        def _():
            for n, t in enumerate(rows):
                for copy in loads(n, blocks.at[t] if flag else moved[n].at[0]):
                    copy.start()

    stores = []
    for n, t in enumerate(rows):
        total[...] = jnp.zeros_like(total)
        for copy in loads(n, moved[n].at[0]):
            copy.wait()
        for k in range(nblk):
            slot = info[5 + t * nblk + k]
            lanes = slot_place(slot, role, cap, nblk) * width
            lanes = pl.ds(pl.multiple_of(lanes, width), width)
            total[:, lanes] = total[:, lanes] + raw[n, k].astype(F32)
        scale = jnp.where(t < used, 1.0, 0.0).astype(F32)
        near_buf[n] = (total[:, :near_w] * scale).astype(BF16)
        far_buf[n] = (total[:, near_w:] * jnp.where(edge == 1, 0.0, scale)).astype(BF16)
        at = pl.ds(pl.multiple_of(t * width, width), width)
        stores.append(pltpu.make_async_copy(near_buf.at[n], near_out.at[at, :], sems.at[n, parts]))
        stores.append(pltpu.make_async_copy(far_buf.at[n], far_out.at[at, :], sems.at[n, parts + 1]))
        stores[-2].start()
        stores[-1].start()
    for copy in stores:
        copy.wait()


def gather_kernel(counts, cols, lists, out):
    out[0] = counts[0]
    at = 1
    for t in range(cols.shape[0]):
        for k in range(cols.shape[1]):
            out[at] = cols[t, k]
            at += 1
    for way in range(lists.shape[1]):
        for i in range(lists.shape[2]):
            out[at] = lists[0, way, i]
            at += 1


def tables_kernel(flags, own, moved, info, send_lists):
    keep = flags[1] == 1
    get = lambda i: jnp.where(keep, own[i], moved[i])
    for i in range(4):
        info[i] = flags[i]
    slots = info.shape[0] - 4
    for i in range(slots):
        info[4 + i] = get(i)
    edge = (send_lists.shape[0] - 1) // 2
    for i in range(edge):
        up, down = get(slots + i), get(slots + edge + i)
        send_lists[i] = jnp.where(flags[0] == 0, up, down)
        send_lists[edge + i] = jnp.where(flags[0] == 0, down, up)
    send_lists[2 * edge] = flags[1]


def row_of(half, step, direct, cap):
    flip = half if direct else 1 - half
    return jnp.where(flip == 1, cap - 1 - step, step)


def stage_kernel(steps, cap, flags, blocks, *refs):
    outs, sems = refs[:-1], refs[-1]
    piece = blocks.shape[1] // 4
    copies = [
        pltpu.make_async_copy(
            blocks.at[row_of(flags[2], step, True, cap), pl.ds(p * piece, piece)],
            out.at[0, pl.ds(p * piece, piece)], sems.at[n, p],
        )
        for n, (step, out) in enumerate(zip(steps, outs)) for p in range(4)
    ]
    for copy in copies:
        copy.start()
    for copy in copies:
        copy.wait()


def slot_place(slot, role, cap, slots):
    edge = (slots - cap) // 2
    first = jnp.where(slot < edge, slot + slots - edge, slot - edge)
    second = jnp.where(slot < edge, slot + cap, jnp.where(slot < edge + cap, slot - edge, slot))
    return jnp.where(role == 0, first, second)


def pick(lists, first, edge, width):
    return [pl.ds(pl.multiple_of(lists[first + i] * width, width), width) for i in range(edge)]


def pack_kernel(width, edge, lists, own, moved, field, near_send, far_send):
    @pl.when(lists[2 * edge] == 1)
    def _():
        field[...] = own[...]

    @pl.when(lists[2 * edge] == 0)
    def _():
        field[...] = moved[...]

    for first, send in ((0, near_send), (edge, far_send)):
        for i, rows in enumerate(pick(lists, first, edge, width)):
            send[i * width : (i + 1) * width, :] = field[rows, :]


def local_kernel(near_op, field, near, acc):
    rows = field.shape[0]
    acc[...] = jnp.dot(near_op[:, :rows], field[...], preferred_element_type=F32) + jnp.dot(
        near_op[:, rows:], near[...], preferred_element_type=F32
    )


def ahead_kernel(width, edge, lists, acc, far_op, far, *refs):
    rows = pick(lists, edge, edge, width)
    join = lambda ref: jnp.concatenate([ref[r, :] for r in rows], axis=0)
    total = join(acc) + jnp.dot(join(far_op), far[...], preferred_element_type=F32)
    if len(refs) > 1:
        total = 2.0 * total - join(refs[0]).astype(F32)
    refs[-1][...] = total.astype(BF16)


def finish_kernel(first, last, width, edge, lists, acc, far_op, far, *refs):
    total = acc[...] + jnp.dot(far_op[...], far[...], preferred_element_type=F32)
    if not first:
        older, refs = refs[0], refs[1:]
        total = 2.0 * total - older[...].astype(F32)
    if last:
        refs[0][...] = total.T.astype(BF16)
        return
    value, field, near_send = refs
    value[...] = total
    field[...] = total.astype(BF16)
    for i, rows in enumerate(pick(lists, 0, edge, width)):
        near_send[i * width : (i + 1) * width, :] = field[rows, :]


def body(vectors, rotation, blocks, cols, lists, counts):
    rows, columns = lax.axis_size("row"), lax.axis_size("col")
    ways = patterns(rows, columns)

    def send(x, way):
        return lax.ppermute(x, AXES, ways[way])

    r, c = lax.axis_index("row"), lax.axis_index("col")
    cap, nblk, width = blocks.shape[0], blocks.shape[1], blocks.shape[2]
    edge = lists.shape[2]
    panel = rotation.shape[1]
    height = cap * width
    slots = cap + 2 * edge
    role = c % 2
    keep = role == r % 2
    half = c // 2 % 2
    at_edge = jnp.where(role == 0, r < 2, r >= rows - 2)
    flag = lambda x: x.astype(jnp.int32)
    sds = jax.ShapeDtypeStruct

    ints = lambda n: sds((n,), jnp.int32)
    flags = jnp.stack([flag(x) for x in (role, keep, half, at_edge, c)])

    pieces = {0: vectors.astype(BF16)}
    bit = columns // 2
    while bit:
        for place in list(pieces):
            pieces[place ^ bit] = lax.ppermute(
                pieces[place], "col", [(k, k ^ bit) for k in range(columns)]
            )
        bit //= 2

    held = pltpu.with_memory_space_constraint(blocks, pltpu.HBM)
    relays = cap // 2 - 1
    straight = cap - relays
    row = sds((1, nblk, width, width), BF16)

    def stage(*steps):
        return call(
            functools.partial(stage_kernel, steps, cap), (row,) * len(steps), [SMEM, HBM], (VMEM,) * len(steps),
            scratch=(pltpu.SemaphoreType.DMA((len(steps), 4)),),
        )(flags, held)

    staged = stage(0) + stage(*range(1, straight - 1)) + stage(straight - 1)
    direct = [send(x, "trade") for x in staged]
    relayed = [send(x, "across") for x in direct[:relays]]

    n_slots = 1 + cap * nblk
    own = call(gather_kernel, ints(n_slots + 2 * edge), [SMEM] * 3, SMEM)(counts, cols, lists)
    info, send_lists = call(
        tables_kernel, (ints(4 + n_slots), ints(2 * edge + 1)), [SMEM] * 3, (SMEM, SMEM)
    )(flags, own, send(own, "trade"))

    field = call(
        functools.partial(rotate_kernel, tuple(pieces), width),
        sds((height, panel), BF16), [SMEM, SMEM, VMEM] + [VMEM] * len(pieces), VMEM,
    )(flags, counts, rotation, *pieces.values())
    moved_field = send(field, "trade")

    ops = ()
    op_shapes = (sds((height, height + edge * width), BF16), sds((height, edge * width), BF16))
    arrived = {(k, True): x for k, x in enumerate(direct)}
    arrived.update({(k, False): x for k, x in enumerate(relayed)})
    lots = [
        [(k, True) for k in range(straight - 1)],
        [(k, False) for k in range(relays - 1)],
        [(relays - 1, False)],
        [(straight - 1, True)],
    ]
    for lot in lots:
        n = len(lot)
        ops = call(
            functools.partial(build_kernel, tuple(lot), cap, nblk, width),
            op_shapes, [SMEM, HBM] + [ANY] * (n + len(ops)), (ANY, ANY),
            scratch=(
                pltpu.VMEM((n, nblk, width, width), BF16),
                pltpu.VMEM((width, slots * width), F32),
                pltpu.VMEM((n, width, height + edge * width), BF16),
                pltpu.VMEM((n, width, edge * width), BF16),
                pltpu.SemaphoreType.DMA((n, 6)),
            ),
            aliases={2 + n: 0, 3 + n: 1} if ops else {},
        )(info, held, *(arrived[key] for key in lot), *ops)
    near_op, far_op = ops

    sent = sds((edge * width, panel), BF16)
    wide = lambda kind: sds((height, panel), kind)
    field, near_send, far_send = call(
        functools.partial(pack_kernel, width, edge), (wide(BF16), sent, sent),
        [SMEM, VMEM, VMEM], (VMEM,) * 3,
    )(send_lists, field, moved_field)
    older, newer = (), field
    for step in range(STEPS):
        far, near = send(far_send, "far"), send(near_send, "near")
        acc = call(local_kernel, wide(F32), [VMEM] * 3, VMEM)(near_op, field, near)
        last = step == STEPS - 1
        given = (send_lists, acc, far_op, far) + older
        specs = [SMEM] + [VMEM] * (len(given) - 1)
        if not last:
            far_send = call(functools.partial(ahead_kernel, width, edge), sent, specs, VMEM)(*given)
        result = call(
            functools.partial(finish_kernel, step == 0, last, width, edge),
            sds((panel, height), BF16) if last else (wide(F32), wide(BF16), sent),
            specs, VMEM if last else (VMEM,) * 3,
        )(*given)
        if not last:
            older = (newer,)
            newer, field, near_send = result
    return jnp.where(keep, result, send(result, "trade")).astype(F32)


def solution(mesh):
    return jax.shard_map(
        body,
        mesh=mesh,
        in_specs=(
            P(("row", "col"), None),
            P(None, "col"),
            P("row", None, None, None),
            P("row", None),
            P("row", None, None),
            P("row"),
        ),
        out_specs=P("col", "row"),
        check_vma=False,
    )
```

```python
import functools

import jax
import jax.numpy as jnp
from jax import lax
from jax.experimental import pallas as pl
from jax.experimental.pallas import tpu as pltpu
from jax.sharding import PartitionSpec as P


STEPS = 10
AXES = ("row", "col")
F32, BF16 = jnp.float32, jnp.bfloat16
VMEM = pl.BlockSpec(memory_space=pltpu.VMEM)
SMEM = pl.BlockSpec(memory_space=pltpu.SMEM)
HBM = pl.BlockSpec(memory_space=pltpu.HBM)
ANY = pl.BlockSpec(memory_space=pl.ANY)


def patterns(rows, cols):
    every = [(r, c) for r in range(rows) for c in range(cols)]
    keeps = lambda r, c: r % 2 == c % 2

    def far(r, c):
        to = r + 2 if c % 2 else r - 2
        return (to, c ^ 1) if 0 <= to < rows else (r ^ 1, c)

    ways = {
        "trade": lambda r, c: (r ^ 2, c) if keeps(r, c) else (r ^ 1, c ^ 1),
        "across": lambda r, c: (r, c ^ 2),
        "near": lambda r, c: (r, c ^ 1),
        "far": far,
    }
    at = lambda place: place[0] * cols + place[1]
    pairs = {name: [(at(p), at(way(*p))) for p in every] for name, way in ways.items()}
    pairs["across"] = [(at(p), at(ways["across"](*p))) for p in every if not keeps(*p)]
    return pairs


def call(kernel, outs, in_specs, out_specs, scratch=(), aliases={}, mib=12):
    return pl.pallas_call(
        kernel,
        out_shape=outs,
        in_specs=in_specs,
        out_specs=out_specs,
        scratch_shapes=scratch,
        input_output_aliases=aliases,
        compiler_params=pltpu.CompilerParams(vmem_limit_bytes=mib << 20),
    )


def here():
    r, c = lax.axis_index("row"), lax.axis_index("col")
    role = lax.rem(c, 2)
    keep = role == lax.rem(r, 2)
    half = lax.rem(lax.div(c, 2), 2)
    edge = jnp.where(role == 0, r < 2, r >= lax.axis_size("row") - 2)
    return role, keep, half, edge, c


def rotate_kernel(places, width, counts, rotation, *refs):
    pieces, out = refs[: len(places)], refs[len(places)]
    rot = rotation[...]
    high = rot.astype(BF16)
    low = (rot - high.astype(F32)).astype(BF16)
    mine, used = here()[4], counts[0] * width
    for place, piece in zip(places, pieces):
        rows = piece.shape[0]
        first = pl.multiple_of((mine ^ place) * rows, rows)
        x = piece[...]
        y = jnp.dot(x, high, preferred_element_type=F32) + jnp.dot(x, low, preferred_element_type=F32)
        at = first + lax.broadcasted_iota(jnp.int32, y.shape, 0)
        out[pl.ds(first, rows), :] = jnp.where(at < used, y, 0.0).astype(BF16)


def build_kernel(steps, cap, nblk, width, info, blocks, *refs):
    moved, refs = refs[: len(steps)], refs[len(steps) :]
    near_out, far_out, raw, total, sems = refs[-5:]
    role, keep, half, at_edge, _ = here()
    slots = total.shape[0]
    near_slots = near_out.shape[1] // width
    parts = 4
    piece = nblk // parts
    rows = [row_of(half, step, direct, cap) for step, direct in steps]

    def loads(n, t):
        cut = lambda p: pl.ds(p * piece, piece)
        return [
            pltpu.make_async_copy(blocks.at[t, cut(p)], raw.at[n, cut(p)], sems.at[n, p])
            for p in range(parts)
        ]

    def add(source, t):
        total[...] = jnp.zeros_like(total)
        for k in range(nblk):
            slot = slot_place(info[1 + t * nblk + k], role, cap, slots)
            total[slot] = total[slot] + source(k).astype(F32)

    @pl.when(keep)
    def _():
        for n, t in enumerate(rows):
            for copy in loads(n, t):
                copy.start()

    for n, t in enumerate(rows):
        @pl.when(keep)
        def _():
            for copy in loads(n, t):
                copy.wait()
            add(lambda k: raw[n, k], t)

        @pl.when(jnp.logical_not(keep))
        def _():
            add(lambda k: moved[n][0, k], t)

        scale = jnp.where(t < info[0], 2.0, 0.0).astype(F32)
        far_scale = jnp.where(at_edge, 0.0, scale)
        at = pl.ds(pl.multiple_of(t * width, width), width)
        for slot in range(slots):
            near = slot < near_slots
            lane = (slot if near else slot - near_slots) * width
            value = total[slot] * (scale if near else far_scale)
            (near_out if near else far_out)[at, lane : lane + width] = value.astype(BF16)


def gather_kernel(counts, cols, lists, out):
    out[0] = counts[0]
    at = 1
    for t in range(cols.shape[0]):
        for k in range(cols.shape[1]):
            out[at] = cols[t, k]
            at += 1
    for way in range(lists.shape[1]):
        for i in range(lists.shape[2]):
            out[at] = lists[0, way, i]
            at += 1


def tables_kernel(own, moved, info, send_lists):
    role, keep = here()[:2]
    get = lambda i: jnp.where(keep, own[i], moved[i])
    slots = info.shape[0]
    for i in range(slots):
        info[i] = get(i)
    edge = send_lists.shape[0] // 2
    for i in range(edge):
        up, down = get(slots + i), get(slots + edge + i)
        send_lists[i] = jnp.where(role == 0, up, down)
        send_lists[edge + i] = jnp.where(role == 0, down, up)


def row_of(half, step, direct, cap):
    flip = half if direct else 1 - half
    return jnp.where(flip == 1, cap - 1 - step, step)


def stage_kernel(steps, cap, blocks, *refs):
    outs, sems = refs[:-1], refs[-1]
    half = here()[2]
    piece = blocks.shape[1] // 4
    copies = [
        pltpu.make_async_copy(
            blocks.at[row_of(half, step, True, cap), pl.ds(p * piece, piece)],
            out.at[0, pl.ds(p * piece, piece)], sems.at[n, p],
        )
        for n, (step, out) in enumerate(zip(steps, outs)) for p in range(4)
    ]
    for copy in copies:
        copy.start()
    for copy in copies:
        copy.wait()


def slot_place(slot, role, cap, slots):
    edge = (slots - cap) // 2
    first = jnp.where(slot < edge, slot + slots - edge, slot - edge)
    second = jnp.where(slot < edge, slot + cap, jnp.where(slot < edge + cap, slot - edge, slot))
    return jnp.where(role == 0, first, second)


def pick(lists, first, edge, width):
    return [pl.ds(pl.multiple_of(lists[first + i] * width, width), width) for i in range(edge)]


def pack_kernel(width, edge, lists, own, moved, field, near_send, far_send):
    keep = here()[1]

    @pl.when(keep)
    def _():
        field[...] = own[...]

    @pl.when(jnp.logical_not(keep))
    def _():
        field[...] = moved[...]

    for first, send in ((0, near_send), (edge, far_send)):
        for i, rows in enumerate(pick(lists, first, edge, width)):
            send[i * width : (i + 1) * width, :] = field[rows, :]


def local_kernel(width, edge, lists, near_op, field, near, *refs):
    first = len(refs) == 4
    rows = field.shape[0]
    total = jnp.dot(near_op[:, :rows], field[...], preferred_element_type=F32) + jnp.dot(
        near_op[:, rows:], near[...], preferred_element_type=F32
    )
    acc = refs[1]
    acc[...] = total if first else total - refs[0][...].astype(F32)
    for i, at in enumerate(pick(lists, edge, edge, width)):
        if len(refs) > 2:
            refs[2][i * width : (i + 1) * width, :] = acc[at, :]
        if first:
            refs[3][i * width : (i + 1) * width, :] = refs[0][at, :]


def result_of(first, acc, far_op, far):
    total = acc[...] + jnp.dot(far_op[...], far[...], preferred_element_type=F32)
    return 0.5 * total if first else total


def ahead_kernel(first, acc, far_op, far, out):
    out[...] = result_of(first, acc, far_op, far).astype(BF16)


def finish_kernel(first, width, edge, lists, acc, far_op, far, *refs):
    field, near_send = refs[-2:]
    total = result_of(first, acc, far_op, far)
    if len(refs) > 2:
        refs[0][...] = total
    field[...] = total.astype(BF16)
    for i, rows in enumerate(pick(lists, 0, edge, width)):
        near_send[i * width : (i + 1) * width, :] = field[rows, :]


def last_kernel(acc, far_op, far, out):
    out[...] = result_of(False, acc, far_op, far).T.astype(BF16)


def body(vectors, rotation, blocks, cols, lists, counts):
    rows, columns = lax.axis_size("row"), lax.axis_size("col")
    ways = patterns(rows, columns)

    def send(x, way):
        return lax.ppermute(x, AXES, ways[way])

    r, c = lax.axis_index("row"), lax.axis_index("col")
    cap, nblk, width = blocks.shape[0], blocks.shape[1], blocks.shape[2]
    edge = lists.shape[2]
    panel = rotation.shape[1]
    height = cap * width
    slots = cap + 2 * edge
    sds = jax.ShapeDtypeStruct

    ints = lambda n: sds((n,), jnp.int32)

    pieces = {0: vectors.astype(BF16)}
    bit = columns // 2
    while bit:
        for place in list(pieces):
            pieces[place ^ bit] = lax.ppermute(
                pieces[place], "col", [(k, k ^ bit) for k in range(columns)]
            )
        bit //= 2

    held = pltpu.with_memory_space_constraint(blocks, pltpu.HBM)
    relays = cap // 2 - 1
    straight = cap - relays
    row = sds((1, nblk, width, width), BF16)

    def stage(*steps):
        return call(
            functools.partial(stage_kernel, steps, cap), (row,) * len(steps), [HBM], (VMEM,) * len(steps),
            scratch=(pltpu.SemaphoreType.DMA((len(steps), 4)),),
        )(held)

    staged = stage(0) + stage(*range(1, straight))
    direct = [send(x, "trade") for x in staged]
    relayed = [send(x, "across") for x in direct[:relays]]

    n_slots = 1 + cap * nblk
    own = call(gather_kernel, ints(n_slots + 2 * edge), [SMEM] * 3, SMEM)(counts, cols, lists)
    info, send_lists = call(
        tables_kernel, (ints(n_slots), ints(2 * edge)), [SMEM] * 2, (SMEM, SMEM)
    )(own, send(own, "trade"))

    field = call(
        functools.partial(rotate_kernel, tuple(pieces), width),
        sds((height, panel), BF16), [SMEM, VMEM] + [VMEM] * len(pieces), VMEM,
    )(counts, rotation, *pieces.values())
    moved_field = send(field, "trade")

    ops = ()
    op_shapes = (sds((height, height + edge * width), BF16), sds((height, edge * width), BF16))
    arrived = {(k, True): x for k, x in enumerate(direct)}
    arrived.update({(k, False): x for k, x in enumerate(relayed)})
    keys = [(k, True) for k in range(straight - 1)]
    cut = len(keys) // 2
    lots = [keys[:cut], keys[cut:], [(k, False) for k in range(relays - 1)]]
    lots += [[(relays - 1, False)], [(straight - 1, True)]]
    for lot in lots:
        n = len(lot)
        ops = call(
            functools.partial(build_kernel, tuple(lot), cap, nblk, width),
            op_shapes, [SMEM, HBM] + [VMEM] * (n + len(ops)), (VMEM, VMEM),
            scratch=(
                pltpu.VMEM((n, nblk, width, width), BF16),
                pltpu.VMEM((slots, width, width), F32),
                pltpu.SemaphoreType.DMA((n, 4)),
            ),
            aliases={2 + n: 0, 3 + n: 1} if ops else {},
        )(info, held, *(arrived[key] for key in lot), *ops)
    near_op, far_op = ops

    sent = sds((edge * width, panel), BF16)
    wide = lambda kind: sds((height, panel), kind)
    field, near_send, far_send = call(
        functools.partial(pack_kernel, width, edge), (wide(BF16), sent, sent),
        [SMEM, VMEM, VMEM], (VMEM,) * 3,
    )(send_lists, field, moved_field)
    older, newer = (), field
    part = sds((edge * width, panel), F32)
    for step in range(STEPS):
        far, near = send(far_send, "far"), send(near_send, "near")
        first, last = step == 0, step == STEPS - 1
        extra = (far_op,) if first else older
        outs = (wide(F32),) if last else (wide(F32), part)
        if first:
            outs += (sds((edge * width, edge * width), BF16),)
        mine = call(
            functools.partial(local_kernel, width, edge), outs,
            [SMEM] + [VMEM] * 4, (VMEM,) * len(outs),
        )(send_lists, near_op, field, near, *extra)
        if first:
            far_part = mine[2]
        if last:
            result = call(last_kernel, sds((panel, height), BF16), [VMEM] * 3, VMEM)(mine[0], far_op, far)
            continue
        far_send = call(
            functools.partial(ahead_kernel, first), sent, [VMEM] * 3, VMEM
        )(mine[1], far_part, far)
        outs = (wide(BF16), sent) if step == STEPS - 2 else (wide(F32), wide(BF16), sent)
        result = call(
            functools.partial(finish_kernel, first, width, edge), outs,
            [SMEM] + [VMEM] * 3, (VMEM,) * len(outs),
        )(send_lists, mine[0], far_op, far)
        older, newer = (newer,), result[0]
        field, near_send = result[-2:]
    keep = c % 2 == r % 2
    return jnp.where(keep, result, send(result, "trade")).astype(F32)


def solution(mesh):
    return jax.shard_map(
        body,
        mesh=mesh,
        in_specs=(
            P(("row", "col"), None),
            P(None, "col"),
            P("row", None, None, None),
            P("row", None),
            P("row", None, None),
            P("row"),
        ),
        out_specs=P("col", "row"),
        check_vma=False,
    )
```

```python
import functools

import jax
import jax.numpy as jnp
from jax import lax
from jax.experimental import pallas as pl
from jax.experimental.pallas import tpu as pltpu
from jax.sharding import PartitionSpec as P


STEPS = 10
PLAIN = 2
AXES = ("row", "col")
F32, BF16 = jnp.float32, jnp.bfloat16
VMEM = pl.BlockSpec(memory_space=pltpu.VMEM)
SMEM = pl.BlockSpec(memory_space=pltpu.SMEM)
HBM = pl.BlockSpec(memory_space=pltpu.HBM)
ANY = pl.BlockSpec(memory_space=pl.ANY)


def patterns(rows, cols):
    every = [(r, c) for r in range(rows) for c in range(cols)]
    keeps = lambda r, c: r % 2 == c % 2

    def far(r, c):
        to = r + 2 if c % 2 else r - 2
        return (to, c ^ 1) if 0 <= to < rows else (r ^ 1, c)

    ways = {
        "trade": lambda r, c: (r ^ 2, c) if keeps(r, c) else (r ^ 1, c ^ 1),
        "across": lambda r, c: (r, c ^ 2),
        "near": lambda r, c: (r, c ^ 1),
        "far": far,
    }
    at = lambda place: place[0] * cols + place[1]
    pairs = {name: [(at(p), at(way(*p))) for p in every] for name, way in ways.items()}
    pairs["across"] = [(at(p), at(ways["across"](*p))) for p in every if not keeps(*p)]
    return pairs


def call(kernel, outs, in_specs, out_specs, scratch=(), aliases={}, mib=12):
    return pl.pallas_call(
        kernel,
        out_shape=outs,
        in_specs=in_specs,
        out_specs=out_specs,
        scratch_shapes=scratch,
        input_output_aliases=aliases,
        compiler_params=pltpu.CompilerParams(vmem_limit_bytes=mib << 20),
    )


def here():
    r, c = lax.axis_index("row"), lax.axis_index("col")
    role = lax.rem(c, 2)
    keep = role == lax.rem(r, 2)
    half = lax.rem(lax.div(c, 2), 2)
    edge = jnp.where(role == 0, r < 2, r >= lax.axis_size("row") - 2)
    return role, keep, half, edge, c


def rotate_kernel(places, width, counts, rotation, *refs):
    pieces, out = refs[: len(places)], refs[len(places)]
    rot = rotation[...]
    high = rot.astype(BF16)
    low = (rot - high.astype(F32)).astype(BF16)
    mine, used = here()[4], counts[0] * width
    for place, piece in zip(places, pieces):
        rows = piece.shape[0]
        first = pl.multiple_of((mine ^ place) * rows, rows)
        x = piece[...]
        y = jnp.dot(x, high, preferred_element_type=F32) + jnp.dot(x, low, preferred_element_type=F32)
        at = first + lax.broadcasted_iota(jnp.int32, y.shape, 0)
        out[pl.ds(first, rows), :] = jnp.where(at < used, y, 0.0).astype(BF16)


def build_kernel(steps, cap, nblk, width, info, blocks, *refs):
    moved, refs = refs[: len(steps)], refs[len(steps) :]
    near_out, far_out, raw, total, sems = refs[-5:]
    role, keep, half, at_edge, _ = here()
    slots = total.shape[0]
    near_slots = near_out.shape[1] // width
    parts = 4
    piece = nblk // parts
    rows = [row_of(half, step, direct, cap) for step, direct in steps]

    def loads(n, t):
        cut = lambda p: pl.ds(p * piece, piece)
        return [
            pltpu.make_async_copy(blocks.at[t, cut(p)], raw.at[n, cut(p)], sems.at[n, p])
            for p in range(parts)
        ]

    def add(source, t):
        total[...] = jnp.zeros_like(total)
        for k in range(nblk):
            slot = slot_place(info[1 + t * nblk + k], role, cap, slots)
            total[slot] = total[slot] + source(k).astype(F32)

    @pl.when(keep)
    def _():
        for n, t in enumerate(rows):
            for copy in loads(n, t):
                copy.start()

    for n, t in enumerate(rows):
        @pl.when(keep)
        def _():
            for copy in loads(n, t):
                copy.wait()
            add(lambda k: raw[n, k], t)

        @pl.when(jnp.logical_not(keep))
        def _():
            add(lambda k: moved[n][0, k], t)

        scale = jnp.where(t < info[0], 2.0, 0.0).astype(F32)
        far_scale = jnp.where(at_edge, 0.0, scale)
        at = pl.ds(pl.multiple_of(t * width, width), width)
        for slot in range(slots):
            near = slot < near_slots
            lane = (slot if near else slot - near_slots) * width
            value = total[slot] * (scale if near else far_scale)
            (near_out if near else far_out)[at, lane : lane + width] = value.astype(BF16)


def gather_kernel(counts, cols, lists, out):
    out[0] = counts[0]
    at = 1
    for t in range(cols.shape[0]):
        for k in range(cols.shape[1]):
            out[at] = cols[t, k]
            at += 1
    for way in range(lists.shape[1]):
        for i in range(lists.shape[2]):
            out[at] = lists[0, way, i]
            at += 1


def tables_kernel(own, moved, info, send_lists):
    role, keep = here()[:2]
    get = lambda i: jnp.where(keep, own[i], moved[i])
    slots = info.shape[0]
    for i in range(slots):
        info[i] = get(i)
    edge = send_lists.shape[0] // 2
    for i in range(edge):
        up, down = get(slots + i), get(slots + edge + i)
        send_lists[i] = jnp.where(role == 0, up, down)
        send_lists[edge + i] = jnp.where(role == 0, down, up)


def row_of(half, step, direct, cap):
    flip = half if direct else 1 - half
    return jnp.where(flip == 1, cap - 1 - step, step)


def stage_kernel(steps, cap, blocks, *refs):
    outs, sems = refs[:-1], refs[-1]
    half = here()[2]
    piece = blocks.shape[1] // 4
    copies = [
        pltpu.make_async_copy(
            blocks.at[row_of(half, step, True, cap), pl.ds(p * piece, piece)],
            out.at[0, pl.ds(p * piece, piece)], sems.at[n, p],
        )
        for n, (step, out) in enumerate(zip(steps, outs)) for p in range(4)
    ]
    for copy in copies:
        copy.start()
    for copy in copies:
        copy.wait()


def slot_place(slot, role, cap, slots):
    edge = (slots - cap) // 2
    first = jnp.where(slot < edge, slot + slots - edge, slot - edge)
    second = jnp.where(slot < edge, slot + cap, jnp.where(slot < edge + cap, slot - edge, slot))
    return jnp.where(role == 0, first, second)


def pick(lists, first, edge, width):
    return [pl.ds(pl.multiple_of(lists[first + i] * width, width), width) for i in range(edge)]


def pack_kernel(width, edge, lists, own, moved, field, near_send, far_send):
    keep = here()[1]

    @pl.when(keep)
    def _():
        field[...] = own[...]

    @pl.when(jnp.logical_not(keep))
    def _():
        field[...] = moved[...]

    for first, send in ((0, near_send), (edge, far_send)):
        for i, rows in enumerate(pick(lists, first, edge, width)):
            send[i * width : (i + 1) * width, :] = field[rows, :]


def fetch(lists, table, sem):
    return pltpu.make_async_copy(lists, table, sem)


def local_kernel(width, edge, less, gives, lists, near_op, field, near, *refs):
    table, sem = refs[-2:]
    refs = list(refs[:-2])
    copy = fetch(lists, table, sem)
    copy.start()
    rows = field.shape[0]
    older = refs.pop(0) if less else None
    far_op = refs.pop(0) if gives == "both" else None
    acc = refs.pop(0)
    total = jnp.dot(near_op[:, :rows], field[...], preferred_element_type=F32) + jnp.dot(
        near_op[:, rows:], near[...], preferred_element_type=F32
    )
    acc[...] = total - older[...].astype(F32) if less else total
    copy.wait()
    if not gives:
        return
    part = refs.pop(0)
    for i, at in enumerate(pick(table, edge, edge, width)):
        part[i * width : (i + 1) * width, :] = acc[at, :].astype(part.dtype)
        if gives == "both":
            half, place = divmod(i, edge // 2)
            refs[half][place * width : (place + 1) * width, :] = far_op[at, :]


def result_of(first, acc, far_op, far):
    total = acc[...] + jnp.dot(far_op[...], far, preferred_element_type=F32)
    return 0.5 * total if first else total


def ahead_kernel(first, acc, low, high, far, out):
    far_op = jnp.concatenate([low[...], high[...]], axis=0)
    total = acc[...] + jnp.dot(far_op, far[...], preferred_element_type=F32)
    out[...] = (0.5 * total if first else total).astype(BF16)


def far_rows(part, low, high, sent):
    op = jnp.concatenate([low[...], high[...]], axis=0)
    total = part[...].astype(F32) + jnp.dot(op, sent[...], preferred_element_type=F32)
    return total.astype(BF16)


def finish_kernel(first, apart, wants, width, edge, lists, acc, far_op, *refs):
    table, sem = refs[-2:]
    refs = list(refs[:-2])
    copy = fetch(lists, table, sem)
    copy.start()
    if apart:
        far = far_rows(*refs[:4])
        refs = refs[4:]
    else:
        far = refs.pop(0)[...]
    total = result_of(first, acc, far_op, far)
    value, part = wants
    if value:
        refs.pop(0)[...] = total
    field, near_send = refs[:2]
    field[...] = total.astype(BF16)
    copy.wait()
    sends = [(0, near_send)] + ([(edge, refs[2])] if part else [])
    for begin, send in sends:
        for i, rows in enumerate(pick(table, begin, edge, width)):
            send[i * width : (i + 1) * width, :] = field[rows, :]


def last_kernel(acc, far_op, part, low, high, sent, out):
    out[...] = result_of(False, acc, far_op, far_rows(part, low, high, sent)).T.astype(BF16)


def body(vectors, rotation, blocks, cols, lists, counts):
    rows, columns = lax.axis_size("row"), lax.axis_size("col")
    ways = patterns(rows, columns)

    def send(x, way):
        return lax.ppermute(x, AXES, ways[way])

    r, c = lax.axis_index("row"), lax.axis_index("col")
    cap, nblk, width = blocks.shape[0], blocks.shape[1], blocks.shape[2]
    edge = lists.shape[2]
    panel = rotation.shape[1]
    height = cap * width
    slots = cap + 2 * edge
    sds = jax.ShapeDtypeStruct

    ints = lambda n: sds((n,), jnp.int32)

    pieces = {0: vectors.astype(BF16)}
    bit = columns // 2
    while bit:
        for place in list(pieces):
            pieces[place ^ bit] = lax.ppermute(
                pieces[place], "col", [(k, k ^ bit) for k in range(columns)]
            )
        bit //= 2

    held = pltpu.with_memory_space_constraint(blocks, pltpu.HBM)
    relays = cap // 2 - 1
    straight = cap - relays
    row = sds((1, nblk, width, width), BF16)

    def stage(*steps):
        return call(
            functools.partial(stage_kernel, steps, cap), (row,) * len(steps), [HBM], (VMEM,) * len(steps),
            scratch=(pltpu.SemaphoreType.DMA((len(steps), 4)),),
        )(held)

    staged = stage(0) + stage(*range(1, straight))
    direct = [send(x, "trade") for x in staged]
    relayed = [send(x, "across") for x in direct[:relays]]

    n_slots = 1 + cap * nblk
    own = call(gather_kernel, ints(n_slots + 2 * edge), [SMEM] * 3, SMEM)(counts, cols, lists)
    info, send_lists = call(
        tables_kernel, (ints(n_slots), ints(2 * edge)), [SMEM] * 2, (SMEM, SMEM)
    )(own, send(own, "trade"))

    field = call(
        functools.partial(rotate_kernel, tuple(pieces), width),
        sds((height, panel), BF16), [SMEM, VMEM] + [VMEM] * len(pieces), VMEM,
    )(counts, rotation, *pieces.values())
    moved_field = send(field, "trade")

    ops = ()
    op_shapes = (sds((height, height + edge * width), BF16), sds((height, edge * width), BF16))
    arrived = {(k, True): x for k, x in enumerate(direct)}
    arrived.update({(k, False): x for k, x in enumerate(relayed)})
    keys = [(k, True) for k in range(straight - 1)]
    cut = len(keys) // 2
    lots = [keys[:cut], keys[cut:], [(k, False) for k in range(relays - 1)]]
    lots += [[(relays - 1, False)], [(straight - 1, True)]]
    for lot in lots:
        n = len(lot)
        ops = call(
            functools.partial(build_kernel, tuple(lot), cap, nblk, width),
            op_shapes, [SMEM, HBM] + [VMEM] * (n + len(ops)), (VMEM, VMEM),
            scratch=(
                pltpu.VMEM((n, nblk, width, width), BF16),
                pltpu.VMEM((slots, width, width), F32),
                pltpu.SemaphoreType.DMA((n, 4)),
            ),
            aliases={2 + n: 0, 3 + n: 1} if ops else {},
        )(info, held, *(arrived[key] for key in lot), *ops)
    near_op, far_op = ops

    sent = sds((edge * width, panel), BF16)
    wide = lambda kind: sds((height, panel), kind)
    field, near_send, far_send = call(
        functools.partial(pack_kernel, width, edge), (wide(BF16), sent, sent),
        [SMEM, VMEM, VMEM], (VMEM,) * 3,
    )(send_lists, field, moved_field)
    older, newer = (), field
    part = lambda kind: sds((edge * width, panel), kind)
    square = sds((edge // 2 * width, edge * width), BF16)
    table = (pltpu.SMEM((2 * edge,), jnp.int32), pltpu.SemaphoreType.DMA)
    lists_at = pltpu.with_memory_space_constraint(send_lists, pltpu.HBM)
    moved_part, sent_rows, theirs = None, {}, []
    for step in range(STEPS):
        plain = step <= PLAIN
        first, last = step == 0, step == STEPS - 1
        near = send(near_send, "near")
        if plain:
            far = send(far_send, "far")
            sent_rows[step] = far_send
        if 0 < step <= 2:
            theirs.append(send(far_part[step - 1], "far"))
        gives = "both" if first else "" if last else "one"
        kind = F32 if step < PLAIN else BF16
        outs = (wide(F32),) + ((part(kind),) if gives else ()) + ((square,) * 2 if first else ())
        given = (lists_at, near_op, field, near) + older + ((far_op,) if first else ())
        mine = call(
            functools.partial(local_kernel, width, edge, not first, gives), outs,
            [HBM] + [VMEM] * (len(given) - 1), (VMEM,) * len(outs), scratch=table,
        )(*given)
        acc = mine[0]
        if first:
            far_part = mine[2:]
        arrived_part, moved_part = moved_part, None
        if PLAIN <= step and not last:
            moved_part = send(mine[1], "far")
        if last:
            result = call(last_kernel, sds((panel, height), BF16), [VMEM] * 6, VMEM)(
                acc, far_op, arrived_part, *theirs, sent_rows[step - 1]
            )
            continue
        if step < PLAIN:
            far_send = call(
                functools.partial(ahead_kernel, first), sent, [VMEM] * 4, VMEM
            )(mine[1], *far_part, far)
        wants = (step < STEPS - 2, PLAIN <= step < STEPS - 2)
        outs = ((wide(F32),) if wants[0] else ()) + (wide(BF16), sent) + ((sent,) if wants[1] else ())
        given = (far,) if plain else (arrived_part, *theirs, sent_rows[step - 1])
        result = call(
            functools.partial(finish_kernel, first, not plain, wants, width, edge), outs,
            [HBM] + [VMEM] * (2 + len(given)), (VMEM,) * len(outs), scratch=table,
        )(lists_at, acc, far_op, *given)
        result = list(result)
        older, newer = (newer,), result.pop(0) if wants[0] else None
        field, near_send = result[:2]
        if wants[1]:
            sent_rows[step + 1] = result[2]
    keep = c % 2 == r % 2
    return jnp.where(keep, result, send(result, "trade")).astype(F32)


def solution(mesh):
    return jax.shard_map(
        body,
        mesh=mesh,
        in_specs=(
            P(("row", "col"), None),
            P(None, "col"),
            P("row", None, None, None),
            P("row", None),
            P("row", None, None),
            P("row"),
        ),
        out_specs=P("col", "row"),
        check_vma=False,
    )
```

```python
import functools

import jax
import jax.numpy as jnp
from jax import lax
from jax.experimental import pallas as pl
from jax.experimental.pallas import tpu as pltpu
from jax.sharding import PartitionSpec as P


STEPS = 10
PLAIN = 2
AXES = ("row", "col")
F32, BF16 = jnp.float32, jnp.bfloat16
VMEM = pl.BlockSpec(memory_space=pltpu.VMEM)
SMEM = pl.BlockSpec(memory_space=pltpu.SMEM)
HBM = pl.BlockSpec(memory_space=pltpu.HBM)
ANY = pl.BlockSpec(memory_space=pl.ANY)


def patterns(rows, cols):
    every = [(r, c) for r in range(rows) for c in range(cols)]
    keeps = lambda r, c: r % 2 == c % 2

    def far(r, c):
        to = r + 2 if c % 2 else r - 2
        return (to, c ^ 1) if 0 <= to < rows else (r ^ 1, c)

    ways = {
        "trade": lambda r, c: (r ^ 2, c) if keeps(r, c) else (r ^ 1, c ^ 1),
        "across": lambda r, c: (r, c ^ 2),
        "near": lambda r, c: (r, c ^ 1),
        "far": far,
    }
    at = lambda place: place[0] * cols + place[1]
    pairs = {name: [(at(p), at(way(*p))) for p in every] for name, way in ways.items()}
    pairs["across"] = [(at(p), at(ways["across"](*p))) for p in every if not keeps(*p)]
    return pairs


def call(kernel, outs, in_specs, out_specs, scratch=(), aliases={}, mib=12):
    return pl.pallas_call(
        kernel,
        out_shape=outs,
        in_specs=in_specs,
        out_specs=out_specs,
        scratch_shapes=scratch,
        input_output_aliases=aliases,
        compiler_params=pltpu.CompilerParams(vmem_limit_bytes=mib << 20),
    )


def here():
    r, c = lax.axis_index("row"), lax.axis_index("col")
    role = lax.rem(c, 2)
    keep = role == lax.rem(r, 2)
    half = lax.rem(lax.div(c, 2), 2)
    edge = jnp.where(role == 0, r < 2, r >= lax.axis_size("row") - 2)
    return role, keep, half, edge, c


def rotate_kernel(places, width, counts, rotation, *refs):
    pieces, out = refs[: len(places)], refs[len(places)]
    rot = rotation[...]
    high = rot.astype(BF16)
    low = (rot - high.astype(F32)).astype(BF16)
    mine, used = here()[4], counts[0] * width
    for place, piece in zip(places, pieces):
        rows = piece.shape[0]
        first = pl.multiple_of((mine ^ place) * rows, rows)
        x = piece[...]
        y = jnp.dot(x, high, preferred_element_type=F32) + jnp.dot(x, low, preferred_element_type=F32)
        at = first + lax.broadcasted_iota(jnp.int32, y.shape, 0)
        out[pl.ds(first, rows), :] = jnp.where(at < used, y, 0.0).astype(BF16)


def build_kernel(lot, held, cap, nblk, width, info, blocks, *refs):
    count = sum(pieces for _, _, pieces in lot)
    moved, refs = list(refs[:count]), refs[count:]
    near_out, far_out, raw, total, sems = refs[-5:]
    role, keep, half, at_edge, _ = here()
    slots = total.shape[0]
    near_slots = near_out.shape[1] // width
    parts = 4
    piece = nblk // parts
    place = lambda step, direct: row_of(half, step, direct, cap)

    def build(source, t):
        total[...] = jnp.zeros_like(total)
        for k in range(nblk):
            slot = slot_place(info[1 + t * nblk + k], role, cap, slots)
            total[slot] = total[slot] + source(k).astype(F32)
        scale = jnp.where(t < info[0], 2.0, 0.0).astype(F32)
        far_scale = jnp.where(at_edge, 0.0, scale)
        at = pl.ds(pl.multiple_of(t * width, width), width)
        for slot in range(slots):
            near = slot < near_slots
            lane = (slot if near else slot - near_slots) * width
            value = total[slot] * (scale if near else far_scale)
            (near_out if near else far_out)[at, lane : lane + width] = value.astype(BF16)

    def loads(n, t):
        cut = lambda p: pl.ds(p * piece, piece)
        return [
            pltpu.make_async_copy(blocks.at[t, cut(p)], raw.at[n, cut(p)], sems.at[n, p])
            for p in range(parts)
        ]

    if held:
        @pl.when(keep)
        def _():
            for n, row in enumerate(held):
                for copy in loads(n, place(*row)):
                    copy.start()

            def one(n, carry):
                steps = sum(jnp.where(n == at, step, 0) for at, (step, _) in enumerate(held))
                direct = sum(jnp.where(n == at, int(direct), 0) for at, (_, direct) in enumerate(held))
                t = place(steps, direct)
                for copy in loads(n, t):
                    copy.wait()
                build(lambda k: raw[n, k], t)
                return carry

            lax.fori_loop(0, len(held), one, 0)

    @pl.when(jnp.logical_not(keep))
    def _():
        for step, direct, pieces in lot:
            arrays = [moved.pop(0) for _ in range(pieces)]
            each = nblk // pieces
            build(lambda k: arrays[k // each][0, k % each], place(step, direct))


def gather_kernel(counts, cols, lists, out):
    out[0] = counts[0]
    at = 1
    for t in range(cols.shape[0]):
        for k in range(cols.shape[1]):
            out[at] = cols[t, k]
            at += 1
    for way in range(lists.shape[1]):
        for i in range(lists.shape[2]):
            out[at] = lists[0, way, i]
            at += 1


def tables_kernel(own, moved, info, send_lists):
    role, keep = here()[:2]
    get = lambda i: jnp.where(keep, own[i], moved[i])
    slots = info.shape[0]
    for i in range(slots):
        info[i] = get(i)
    edge = send_lists.shape[0] // 2
    for i in range(edge):
        up, down = get(slots + i), get(slots + edge + i)
        send_lists[i] = jnp.where(role == 0, up, down)
        send_lists[edge + i] = jnp.where(role == 0, down, up)


def row_of(half, step, direct, cap):
    flip = jnp.where(direct == 1, half, 1 - half)
    return jnp.where(flip == 1, cap - 1 - step, step)


def stage_kernel(cuts, cap, blocks, *refs):
    outs, sems = refs[:-1], refs[-1]
    half = here()[2]
    copies = []
    for n, ((step, first, count), out) in enumerate(zip(cuts, outs)):
        piece = count // 2
        for p in range(2):
            copies.append(
                pltpu.make_async_copy(
                    blocks.at[row_of(half, step, 1, cap), pl.ds(first + p * piece, piece)],
                    out.at[0, pl.ds(p * piece, piece)], sems.at[n, p],
                )
            )
    for copy in copies:
        copy.start()
    for copy in copies:
        copy.wait()


def slot_place(slot, role, cap, slots):
    edge = (slots - cap) // 2
    first = jnp.where(slot < edge, slot + slots - edge, slot - edge)
    second = jnp.where(slot < edge, slot + cap, jnp.where(slot < edge + cap, slot - edge, slot))
    return jnp.where(role == 0, first, second)


def pick(lists, first, edge, width):
    return [pl.ds(pl.multiple_of(lists[first + i] * width, width), width) for i in range(edge)]


def pack_kernel(width, edge, lists, own, moved, field, near_send, far_send):
    keep = here()[1]

    @pl.when(keep)
    def _():
        field[...] = own[...]

    @pl.when(jnp.logical_not(keep))
    def _():
        field[...] = moved[...]

    for first, send in ((0, near_send), (edge, far_send)):
        for i, rows in enumerate(pick(lists, first, edge, width)):
            send[i * width : (i + 1) * width, :] = field[rows, :]


def fetch(lists, table, sem):
    return pltpu.make_async_copy(lists, table, sem)


def local_kernel(width, edge, less, gives, lists, near_op, field, near, *refs):
    table, sem = refs[-2:]
    refs = list(refs[:-2])
    copy = fetch(lists, table, sem)
    copy.start()
    rows = field.shape[0]
    older = refs.pop(0) if less else None
    far_op = refs.pop(0) if gives == "both" else None
    acc = refs.pop(0)
    total = jnp.dot(near_op[:, :rows], field[...], preferred_element_type=F32) + jnp.dot(
        near_op[:, rows:], near[...], preferred_element_type=F32
    )
    acc[...] = total - older[...].astype(F32) if less else total
    copy.wait()
    if not gives:
        return
    part = refs.pop(0)
    for i, at in enumerate(pick(table, edge, edge, width)):
        part[i * width : (i + 1) * width, :] = acc[at, :].astype(part.dtype)
        if gives == "both":
            half, place = divmod(i, edge // 2)
            refs[half][place * width : (place + 1) * width, :] = far_op[at, :]


def result_of(first, acc, far_op, far):
    total = acc[...] + jnp.dot(far_op[...], far, preferred_element_type=F32)
    return 0.5 * total if first else total


def ahead_kernel(first, acc, low, high, far, out):
    far_op = jnp.concatenate([low[...], high[...]], axis=0)
    total = acc[...] + jnp.dot(far_op, far[...], preferred_element_type=F32)
    out[...] = (0.5 * total if first else total).astype(BF16)


def far_rows(part, low, high, sent):
    op = jnp.concatenate([low[...], high[...]], axis=0)
    total = part[...].astype(F32) + jnp.dot(op, sent[...], preferred_element_type=F32)
    return total.astype(BF16)


def finish_kernel(first, apart, wants, width, edge, lists, acc, far_op, *refs):
    table, sem = refs[-2:]
    refs = list(refs[:-2])
    copy = fetch(lists, table, sem)
    copy.start()
    if apart:
        far = far_rows(*refs[:4])
        refs = refs[4:]
    else:
        far = refs.pop(0)[...]
    total = result_of(first, acc, far_op, far)
    value, part = wants
    if value:
        refs.pop(0)[...] = total
    field, near_send = refs[:2]
    field[...] = total.astype(BF16)
    copy.wait()
    sends = [(0, near_send)] + ([(edge, refs[2])] if part else [])
    for begin, send in sends:
        for i, rows in enumerate(pick(table, begin, edge, width)):
            send[i * width : (i + 1) * width, :] = field[rows, :]


def last_kernel(begin, acc, far_op, part, low, high, sent, out):
    rows = pl.ds(begin, out.shape[1])
    far = far_rows(part, low, high, sent)
    total = acc[rows, :] + jnp.dot(far_op[rows, :], far, preferred_element_type=F32)
    out[...] = total.T.astype(BF16)


def merge_kernel(begin, own, moved, *refs):
    out, wide, sem = refs[-3:]
    keep = here()[1]

    @pl.when(keep)
    def _():
        wide[...] = own[...].astype(F32)

    @pl.when(jnp.logical_not(keep))
    def _():
        wide[...] = moved[...].astype(F32)

    copy = pltpu.make_async_copy(wide, out.at[:, pl.ds(begin, wide.shape[1])], sem)
    copy.start()
    copy.wait()


def body(vectors, rotation, blocks, cols, lists, counts):
    rows, columns = lax.axis_size("row"), lax.axis_size("col")
    ways = patterns(rows, columns)

    def send(x, way):
        return lax.ppermute(x, AXES, ways[way])

    cap, nblk, width = blocks.shape[0], blocks.shape[1], blocks.shape[2]
    edge = lists.shape[2]
    panel = rotation.shape[1]
    height = cap * width
    slots = cap + 2 * edge
    sds = jax.ShapeDtypeStruct

    ints = lambda n: sds((n,), jnp.int32)

    pieces = {0: vectors.astype(BF16)}
    bit = columns // 2
    while bit:
        for place in list(pieces):
            pieces[place ^ bit] = lax.ppermute(
                pieces[place], "col", [(k, k ^ bit) for k in range(columns)]
            )
        bit //= 2

    held = pltpu.with_memory_space_constraint(blocks, pltpu.HBM)
    middle, part_blocks = cap // 2, nblk // 2
    block_rows = lambda count: sds((1, count, width, width), BF16)

    def stage(*cuts):
        return call(
            functools.partial(stage_kernel, cuts, cap), tuple(block_rows(cut[2]) for cut in cuts),
            [HBM], (VMEM,) * len(cuts), scratch=(pltpu.SemaphoreType.DMA((len(cuts), 2)),),
        )(held)

    staged = stage((0, 0, nblk))
    staged += stage(
        *((k, 0, nblk) for k in range(1, middle - 1)),
        (middle - 1, part_blocks, part_blocks), (middle - 1, 0, part_blocks), (middle, 0, part_blocks),
    )
    direct = [send(x, "trade") for x in staged]
    relayed = [send(x, "across") for x in direct[:middle]]

    n_slots = 1 + cap * nblk
    own = call(gather_kernel, ints(n_slots + 2 * edge), [SMEM] * 3, SMEM)(counts, cols, lists)
    info, send_lists = call(
        tables_kernel, (ints(n_slots), ints(2 * edge)), [SMEM] * 2, (SMEM, SMEM)
    )(own, send(own, "trade"))

    field = call(
        functools.partial(rotate_kernel, tuple(pieces), width),
        sds((height, panel), BF16), [SMEM, VMEM] + [VMEM] * len(pieces), VMEM,
    )(counts, rotation, *pieces.values())
    moved_field = send(field, "trade")

    ops = ()
    op_shapes = (sds((height, height + edge * width), BF16), sds((height, edge * width), BF16))
    low, high, extra = direct[middle], direct[middle - 1], direct[middle + 1]
    cut = middle // 2
    lots = [
        [(k, 1, (direct[k],)) for k in range(cut)],
        [(k, 1, (direct[k],)) for k in range(cut, middle - 1)] + [(middle - 1, 1, (low, high))],
        [(k, 0, (relayed[k],)) for k in range(middle - 2)],
        [(middle - 2, 0, (relayed[middle - 2],))],
        [(middle, 1, (extra, relayed[middle - 1]))],
    ]
    whole = [[row[:2] for row in lot] for lot in lots]
    holds = [whole[0], sum(whole[1:], []), [], [], []]
    for lot, hold in zip(lots, holds):
        given = [x for row in lot for x in row[2]]
        n = len(given)
        ops = call(
            functools.partial(build_kernel, [(*row[:2], len(row[2])) for row in lot], hold, cap, nblk, width),
            op_shapes, [SMEM, HBM] + [VMEM] * (n + len(ops)), (VMEM, VMEM),
            scratch=(
                pltpu.VMEM((max(1, len(hold)), nblk, width, width), BF16),
                pltpu.VMEM((slots, width, width), F32),
                pltpu.SemaphoreType.DMA((max(1, len(hold)), 4)),
            ),
            aliases={2 + n: 0, 3 + n: 1} if ops else {}, mib=20,
        )(info, held, *given, *ops)
    near_op, far_op = ops

    sent = sds((edge * width, panel), BF16)
    wide = lambda kind: sds((height, panel), kind)
    field, near_send, far_send = call(
        functools.partial(pack_kernel, width, edge), (wide(BF16), sent, sent),
        [SMEM, VMEM, VMEM], (VMEM,) * 3,
    )(send_lists, field, moved_field)
    older, newer = (), field
    part = lambda kind: sds((edge * width, panel), kind)
    square = sds((edge // 2 * width, edge * width), BF16)
    table = (pltpu.SMEM((2 * edge,), jnp.int32), pltpu.SemaphoreType.DMA)
    lists_at = pltpu.with_memory_space_constraint(send_lists, pltpu.HBM)
    moved_part, sent_rows, theirs = None, {}, []
    for step in range(STEPS):
        plain = step <= PLAIN
        first, last = step == 0, step == STEPS - 1
        near = send(near_send, "near")
        if plain:
            far = send(far_send, "far")
            sent_rows[step] = far_send
        if 0 < step <= 2:
            theirs.append(send(far_part[step - 1], "far"))
        gives = "both" if first else "" if last else "one"
        kind = F32 if step < PLAIN else BF16
        outs = (wide(F32),) + ((part(kind),) if gives else ()) + ((square,) * 2 if first else ())
        given = (lists_at, near_op, field, near) + older + ((far_op,) if first else ())
        mine = call(
            functools.partial(local_kernel, width, edge, not first, gives), outs,
            [HBM] + [VMEM] * (len(given) - 1), (VMEM,) * len(outs), scratch=table,
        )(*given)
        acc = mine[0]
        if first:
            far_part = mine[2:]
        arrived_part, moved_part = moved_part, None
        if PLAIN <= step and not last:
            moved_part = send(mine[1], "far")
        if last:
            cut = height // 2
            ends = [
                call(
                    functools.partial(last_kernel, begin), sds((panel, cut), BF16), [VMEM] * 6, VMEM
                )(acc, far_op, arrived_part, *theirs, sent_rows[step - 1])
                for begin in (0, cut)
            ]
            backs = [send(x, "trade") for x in ends]
            out = ()
            for at, (own, back) in enumerate(zip(ends, backs)):
                out = (
                    call(
                        functools.partial(merge_kernel, at * cut), sds((panel, height), F32),
                        [VMEM] * 2 + [HBM] * len(out), HBM,
                        scratch=(pltpu.VMEM((panel, cut), F32), pltpu.SemaphoreType.DMA),
                        aliases={2: 0} if out else {},
                    )(own, back, *out),
                )
            return out[0]
        if step < PLAIN:
            far_send = call(functools.partial(ahead_kernel, first), sent, [VMEM] * 4, VMEM)(mine[1], *far_part, far)
        wants = (step < STEPS - 2, PLAIN <= step < STEPS - 2)
        outs = ((wide(F32),) if wants[0] else ()) + (wide(BF16), sent) + ((sent,) if wants[1] else ())
        given = (far,) if plain else (arrived_part, *theirs, sent_rows[step - 1])
        result = call(
            functools.partial(finish_kernel, first, not plain, wants, width, edge), outs,
            [HBM] + [VMEM] * (2 + len(given)), (VMEM,) * len(outs), scratch=table,
        )(lists_at, acc, far_op, *given)
        result = list(result)
        older, newer = (newer,), result.pop(0) if wants[0] else None
        field, near_send = result[:2]
        if wants[1]:
            sent_rows[step + 1] = result[2]


def solution(mesh):
    return jax.shard_map(
        body,
        mesh=mesh,
        in_specs=(
            P(("row", "col"), None),
            P(None, "col"),
            P("row", None, None, None),
            P("row", None),
            P("row", None, None),
            P("row"),
        ),
        out_specs=P("col", "row"),
        check_vma=False,
    )
```

```python
import functools

import jax
import jax.numpy as jnp
from jax import lax
from jax.experimental import pallas as pl
from jax.experimental.pallas import tpu as pltpu
from jax.sharding import PartitionSpec as P


STEPS = 10
PLAIN = 2
AXES = ("row", "col")
F32, BF16 = jnp.float32, jnp.bfloat16
VMEM = pl.BlockSpec(memory_space=pltpu.VMEM)
SMEM = pl.BlockSpec(memory_space=pltpu.SMEM)
HBM = pl.BlockSpec(memory_space=pltpu.HBM)
ANY = pl.BlockSpec(memory_space=pl.ANY)


def patterns(rows, cols):
    every = [(r, c) for r in range(rows) for c in range(cols)]
    keeps = lambda r, c: r % 2 == c % 2

    def far(r, c):
        to = r + 2 if c % 2 else r - 2
        return (to, c ^ 1) if 0 <= to < rows else (r ^ 1, c)

    ways = {
        "trade": lambda r, c: (r ^ 2, c) if keeps(r, c) else (r ^ 1, c ^ 1),
        "across": lambda r, c: (r, c ^ 2),
        "near": lambda r, c: (r, c ^ 1),
        "far": far,
    }
    at = lambda place: place[0] * cols + place[1]
    pairs = {name: [(at(p), at(way(*p))) for p in every] for name, way in ways.items()}
    pairs["across"] = [(at(p), at(ways["across"](*p))) for p in every if not keeps(*p)]
    return pairs


def call(kernel, outs, in_specs, out_specs, scratch=(), aliases={}, mib=12):
    return pl.pallas_call(
        kernel,
        out_shape=outs,
        in_specs=in_specs,
        out_specs=out_specs,
        scratch_shapes=scratch,
        input_output_aliases=aliases,
        compiler_params=pltpu.CompilerParams(vmem_limit_bytes=mib << 20),
    )


def here():
    r, c = lax.axis_index("row"), lax.axis_index("col")
    role = lax.rem(c, 2)
    keep = role == lax.rem(r, 2)
    half = lax.rem(lax.div(c, 2), 2)
    edge = jnp.where(role == 0, r < 2, r >= lax.axis_size("row") - 2)
    return role, keep, half, edge, c


def rotate_kernel(places, width, counts, rotation, *refs):
    pieces, out = refs[: len(places)], refs[len(places)]
    rot = rotation[...]
    high = rot.astype(BF16)
    low = (rot - high.astype(F32)).astype(BF16)
    mine, used = here()[4], counts[0] * width
    for place, piece in zip(places, pieces):
        rows = piece.shape[0]
        first = pl.multiple_of((mine ^ place) * rows, rows)
        x = piece[...]
        y = jnp.dot(x, high, preferred_element_type=F32) + jnp.dot(x, low, preferred_element_type=F32)
        at = first + lax.broadcasted_iota(jnp.int32, y.shape, 0)
        out[pl.ds(first, rows), :] = jnp.where(at < used, y, 0.0).astype(BF16)


def build_kernel(lot, held, cap, nblk, width, info, blocks, *refs):
    count = sum(pieces for _, _, pieces in lot)
    moved, refs = list(refs[:count]), refs[count:]
    near_out, far_out, raw, total, sems = refs[-5:]
    role, keep, half, at_edge, _ = here()
    slots = total.shape[0]
    near_slots = near_out.shape[1] // width
    parts = 4
    piece = nblk // parts
    place = lambda step, direct: row_of(half, step, direct, cap)

    def build(source, t):
        total[...] = jnp.zeros_like(total)
        for k in range(nblk):
            slot = slot_place(info[1 + t * nblk + k], role, cap, slots)
            total[slot] = total[slot] + source(k).astype(F32)
        scale = jnp.where(t < info[0], 2.0, 0.0).astype(F32)
        far_scale = jnp.where(at_edge, 0.0, scale)
        at = pl.ds(pl.multiple_of(t * width, width), width)
        for slot in range(slots):
            near = slot < near_slots
            lane = (slot if near else slot - near_slots) * width
            value = total[slot] * (scale if near else far_scale)
            (near_out if near else far_out)[at, lane : lane + width] = value.astype(BF16)

    def loads(n, t):
        cut = lambda p: pl.ds(p * piece, piece)
        return [
            pltpu.make_async_copy(blocks.at[t, cut(p)], raw.at[n, cut(p)], sems.at[n, p])
            for p in range(parts)
        ]

    if held:
        @pl.when(keep)
        def _():
            for n, row in enumerate(held):
                for copy in loads(n, place(*row)):
                    copy.start()

            def one(n, carry):
                steps = sum(jnp.where(n == at, step, 0) for at, (step, _) in enumerate(held))
                direct = sum(jnp.where(n == at, int(direct), 0) for at, (_, direct) in enumerate(held))
                t = place(steps, direct)
                for copy in loads(n, t):
                    copy.wait()
                build(lambda k: raw[n, k], t)
                return carry

            lax.fori_loop(0, len(held), one, 0)

    @pl.when(jnp.logical_not(keep))
    def _():
        for step, direct, pieces in lot:
            arrays = [moved.pop(0) for _ in range(pieces)]
            each = nblk // pieces
            build(lambda k: arrays[k // each][0, k % each], place(step, direct))


def gather_kernel(counts, cols, lists, out):
    out[0] = counts[0]
    at = 1
    for t in range(cols.shape[0]):
        for k in range(cols.shape[1]):
            out[at] = cols[t, k]
            at += 1
    for way in range(lists.shape[1]):
        for i in range(lists.shape[2]):
            out[at] = lists[0, way, i]
            at += 1


def tables_kernel(own, moved, info, send_lists):
    role, keep = here()[:2]
    get = lambda i: jnp.where(keep, own[i], moved[i])
    slots = info.shape[0]
    for i in range(slots):
        info[i] = get(i)
    edge = send_lists.shape[0] // 2
    for i in range(edge):
        up, down = get(slots + i), get(slots + edge + i)
        send_lists[i] = jnp.where(role == 0, up, down)
        send_lists[edge + i] = jnp.where(role == 0, down, up)


def row_of(half, step, direct, cap):
    flip = jnp.where(direct == 1, half, 1 - half)
    return jnp.where(flip == 1, cap - 1 - step, step)


def stage_kernel(cuts, cap, blocks, *refs):
    outs, sems = refs[:-1], refs[-1]
    half = here()[2]
    copies = []
    for n, ((step, first, count), out) in enumerate(zip(cuts, outs)):
        piece = count // 2
        for p in range(2):
            copies.append(
                pltpu.make_async_copy(
                    blocks.at[row_of(half, step, 1, cap), pl.ds(first + p * piece, piece)],
                    out.at[0, pl.ds(p * piece, piece)], sems.at[n, p],
                )
            )
    for copy in copies:
        copy.start()
    for copy in copies:
        copy.wait()


def slot_place(slot, role, cap, slots):
    edge = (slots - cap) // 2
    first = jnp.where(slot < edge, slot + slots - edge, slot - edge)
    second = jnp.where(slot < edge, slot + cap, jnp.where(slot < edge + cap, slot - edge, slot))
    return jnp.where(role == 0, first, second)


def pick(lists, first, edge, width):
    return [pl.ds(pl.multiple_of(lists[first + i] * width, width), width) for i in range(edge)]


def pack_kernel(width, edge, lists, own, moved, field, near_send, far_send):
    keep = here()[1]

    @pl.when(keep)
    def _():
        field[...] = own[...]

    @pl.when(jnp.logical_not(keep))
    def _():
        field[...] = moved[...]

    for first, send in ((0, near_send), (edge, far_send)):
        for i, rows in enumerate(pick(lists, first, edge, width)):
            send[i * width : (i + 1) * width, :] = field[rows, :]


def fetch(lists, table, sem):
    return pltpu.make_async_copy(lists, table, sem)


def local_kernel(width, edge, less, gives, lists, near_op, field, near, *refs):
    table, sem = refs[-2:]
    refs = list(refs[:-2])
    copy = fetch(lists, table, sem)
    copy.start()
    rows = field.shape[0]
    older = refs.pop(0) if less else None
    far_op = refs.pop(0) if gives == "both" else None
    acc = refs.pop(0)
    total = jnp.dot(near_op[:, :rows], field[...], preferred_element_type=F32) + jnp.dot(
        near_op[:, rows:], near[...], preferred_element_type=F32
    )
    acc[...] = total - older[...].astype(F32) if less else total
    copy.wait()
    if not gives:
        return
    part = refs.pop(0)
    for i, at in enumerate(pick(table, edge, edge, width)):
        part[i * width : (i + 1) * width, :] = acc[at, :].astype(part.dtype)
        if gives == "both":
            half, place = divmod(i, edge // 2)
            refs[half][place * width : (place + 1) * width, :] = far_op[at, :]


def result_of(first, acc, far_op, far):
    total = acc[...] + jnp.dot(far_op[...], far, preferred_element_type=F32)
    return 0.5 * total if first else total


def ahead_kernel(first, acc, low, high, far, out):
    far_op = jnp.concatenate([low[...], high[...]], axis=0)
    total = acc[...] + jnp.dot(far_op, far[...], preferred_element_type=F32)
    out[...] = (0.5 * total if first else total).astype(BF16)


def far_rows(part, low, high, sent):
    op = jnp.concatenate([low[...], high[...]], axis=0)
    total = part[...].astype(F32) + jnp.dot(op, sent[...], preferred_element_type=F32)
    return total.astype(BF16)


def finish_kernel(first, apart, wants, width, edge, lists, acc, far_op, *refs):
    table, sem = refs[-2:]
    refs = list(refs[:-2])
    copy = fetch(lists, table, sem)
    copy.start()
    if apart:
        far = far_rows(*refs[:4])
        refs = refs[4:]
    else:
        far = refs.pop(0)[...]
    total = result_of(first, acc, far_op, far)
    value, part = wants
    if value:
        refs.pop(0)[...] = total
    field, near_send = refs[:2]
    field[...] = total.astype(BF16)
    copy.wait()
    sends = [(0, near_send)] + ([(edge, refs[2])] if part else [])
    for begin, send in sends:
        for i, rows in enumerate(pick(table, begin, edge, width)):
            send[i * width : (i + 1) * width, :] = field[rows, :]


def last_kernel(begin, acc, far_op, part, low, high, sent, out):
    rows = pl.ds(begin, out.shape[1])
    far = far_rows(part, low, high, sent)
    total = acc[rows, :] + jnp.dot(far_op[rows, :], far, preferred_element_type=F32)
    out[...] = total.T.astype(BF16)


def merge_kernel(begin, own, moved, *refs):
    out, wide, sem = refs[-3:]
    keep = here()[1]

    @pl.when(keep)
    def _():
        wide[...] = own[...].astype(F32)

    @pl.when(jnp.logical_not(keep))
    def _():
        wide[...] = moved[...].astype(F32)

    copy = pltpu.make_async_copy(wide, out.at[:, pl.ds(begin, wide.shape[1])], sem)
    copy.start()
    copy.wait()


def body(vectors, rotation, blocks, cols, lists, counts):
    rows, columns = lax.axis_size("row"), lax.axis_size("col")
    ways = patterns(rows, columns)

    def send(x, way):
        return lax.ppermute(x, AXES, ways[way])

    cap, nblk, width = blocks.shape[0], blocks.shape[1], blocks.shape[2]
    edge = lists.shape[2]
    panel = rotation.shape[1]
    height = cap * width
    slots = cap + 2 * edge
    sds = jax.ShapeDtypeStruct

    ints = lambda n: sds((n,), jnp.int32)

    pieces = {0: vectors.astype(BF16)}
    bit = columns // 2
    while bit:
        for place in list(pieces):
            pieces[place ^ bit] = lax.ppermute(
                pieces[place], "col", [(k, k ^ bit) for k in range(columns)]
            )
        bit //= 2

    held = pltpu.with_memory_space_constraint(blocks, pltpu.HBM)
    middle, part_blocks = cap // 2, nblk // 2
    block_rows = lambda count: sds((1, count, width, width), BF16)

    def stage(*cuts):
        return call(
            functools.partial(stage_kernel, cuts, cap), tuple(block_rows(cut[2]) for cut in cuts),
            [HBM], (VMEM,) * len(cuts), scratch=(pltpu.SemaphoreType.DMA((len(cuts), 2)),),
        )(held)

    staged = stage((0, 0, nblk))
    staged += stage(
        *((k, 0, nblk) for k in range(1, middle - 1)),
        (middle - 1, part_blocks, part_blocks), (middle - 1, 0, part_blocks), (middle, 0, part_blocks),
    )
    direct = [send(x, "trade") for x in staged]
    relayed = [send(x, "across") for x in direct[:middle]]

    n_slots = 1 + cap * nblk
    own = call(gather_kernel, ints(n_slots + 2 * edge), [SMEM] * 3, SMEM)(counts, cols, lists)
    info, send_lists = call(
        tables_kernel, (ints(n_slots), ints(2 * edge)), [SMEM] * 2, (SMEM, SMEM)
    )(own, send(own, "trade"))

    field = call(
        functools.partial(rotate_kernel, tuple(pieces), width),
        sds((height, panel), BF16), [SMEM, VMEM] + [VMEM] * len(pieces), VMEM,
    )(counts, rotation, *pieces.values())
    moved_field = send(field, "trade")

    ops = ()
    op_shapes = (sds((height, height + edge * width), BF16), sds((height, edge * width), BF16))
    low, high, extra = direct[middle], direct[middle - 1], direct[middle + 1]
    cut = middle // 2
    lots = [
        [(k, 1, (direct[k],)) for k in range(cut)],
        [(k, 1, (direct[k],)) for k in range(cut, middle - 1)],
        [(k, 0, (relayed[k],)) for k in range(middle - 2)],
        [(middle - 2, 0, (relayed[middle - 2],)), (middle - 1, 1, (low, high))],
        [(middle, 1, (extra, relayed[middle - 1]))],
    ]
    whole = sum([[row[:2] for row in lot] for lot in lots], [])
    holds = [whole[: cap // 2], whole[cap // 2 :], [], [], []]
    for lot, hold in zip(lots, holds):
        given = [x for row in lot for x in row[2]]
        n = len(given)
        ops = call(
            functools.partial(build_kernel, [(*row[:2], len(row[2])) for row in lot], hold, cap, nblk, width),
            op_shapes, [SMEM, HBM] + [VMEM] * (n + len(ops)), (VMEM, VMEM),
            scratch=(
                pltpu.VMEM((max(1, len(hold)), nblk, width, width), BF16),
                pltpu.VMEM((slots, width, width), F32),
                pltpu.SemaphoreType.DMA((max(1, len(hold)), 4)),
            ),
            aliases={2 + n: 0, 3 + n: 1} if ops else {}, mib=20,
        )(info, held, *given, *ops)
    near_op, far_op = ops

    sent = sds((edge * width, panel), BF16)
    wide = lambda kind: sds((height, panel), kind)
    field, near_send, far_send = call(
        functools.partial(pack_kernel, width, edge), (wide(BF16), sent, sent),
        [SMEM, VMEM, VMEM], (VMEM,) * 3,
    )(send_lists, field, moved_field)
    older, newer = (), field
    part = lambda kind: sds((edge * width, panel), kind)
    square = sds((edge // 2 * width, edge * width), BF16)
    table = (pltpu.SMEM((2 * edge,), jnp.int32), pltpu.SemaphoreType.DMA)
    lists_at = pltpu.with_memory_space_constraint(send_lists, pltpu.HBM)
    moved_part, sent_rows, theirs = None, {}, []
    for step in range(STEPS):
        plain = step <= PLAIN
        first, last = step == 0, step == STEPS - 1
        near = send(near_send, "near")
        if plain:
            far = send(far_send, "far")
            sent_rows[step] = far_send
        if 0 < step <= 2:
            theirs.append(send(far_part[step - 1], "far"))
        gives = "both" if first else "" if last else "one"
        kind = F32 if step < PLAIN else BF16
        outs = (wide(F32),) + ((part(kind),) if gives else ()) + ((square,) * 2 if first else ())
        given = (lists_at, near_op, field, near) + older + ((far_op,) if first else ())
        mine = call(
            functools.partial(local_kernel, width, edge, not first, gives), outs,
            [HBM] + [VMEM] * (len(given) - 1), (VMEM,) * len(outs), scratch=table,
        )(*given)
        acc = mine[0]
        if first:
            far_part = mine[2:]
        arrived_part, moved_part = moved_part, None
        if PLAIN <= step and not last:
            moved_part = send(mine[1], "far")
        if last:
            cut = height // 2
            ends = [
                call(
                    functools.partial(last_kernel, begin), sds((panel, cut), BF16), [VMEM] * 6, VMEM
                )(acc, far_op, arrived_part, *theirs, sent_rows[step - 1])
                for begin in (0, cut)
            ]
            backs = [send(x, "trade") for x in ends]
            out = ()
            for at, (own, back) in enumerate(zip(ends, backs)):
                out = (
                    call(
                        functools.partial(merge_kernel, at * cut), sds((panel, height), F32),
                        [VMEM] * 2 + [HBM] * len(out), HBM,
                        scratch=(pltpu.VMEM((panel, cut), F32), pltpu.SemaphoreType.DMA),
                        aliases={2: 0} if out else {},
                    )(own, back, *out),
                )
            return out[0]
        if step < PLAIN:
            far_send = call(functools.partial(ahead_kernel, first), sent, [VMEM] * 4, VMEM)(mine[1], *far_part, far)
        wants = (step < STEPS - 2, PLAIN <= step < STEPS - 2)
        outs = ((wide(F32),) if wants[0] else ()) + (wide(BF16), sent) + ((sent,) if wants[1] else ())
        given = (far,) if plain else (arrived_part, *theirs, sent_rows[step - 1])
        result = call(
            functools.partial(finish_kernel, first, not plain, wants, width, edge), outs,
            [HBM] + [VMEM] * (2 + len(given)), (VMEM,) * len(outs), scratch=table,
        )(lists_at, acc, far_op, *given)
        result = list(result)
        older, newer = (newer,), result.pop(0) if wants[0] else None
        field, near_send = result[:2]
        if wants[1]:
            sent_rows[step + 1] = result[2]


def solution(mesh):
    return jax.shard_map(
        body,
        mesh=mesh,
        in_specs=(
            P(("row", "col"), None),
            P(None, "col"),
            P("row", None, None, None),
            P("row", None),
            P("row", None, None),
            P("row"),
        ),
        out_specs=P("col", "row"),
        check_vma=False,
    )
```

```python
import functools

import jax
import jax.numpy as jnp
from jax import lax
from jax.experimental import pallas as pl
from jax.experimental.pallas import tpu as pltpu
from jax.sharding import PartitionSpec as P


STEPS = 10
PLAIN = 1
AXES = ("row", "col")
F32, BF16 = jnp.float32, jnp.bfloat16
VMEM = pl.BlockSpec(memory_space=pltpu.VMEM)
SMEM = pl.BlockSpec(memory_space=pltpu.SMEM)
HBM = pl.BlockSpec(memory_space=pltpu.HBM)
ANY = pl.BlockSpec(memory_space=pl.ANY)


def patterns(rows, cols):
    every = [(r, c) for r in range(rows) for c in range(cols)]
    keeps = lambda r, c: r % 2 == c % 2

    def far(r, c):
        to = r + 2 if c % 2 else r - 2
        return (to, c ^ 1) if 0 <= to < rows else (r ^ 1, c)

    ways = {
        "trade": lambda r, c: (r ^ 2, c) if keeps(r, c) else (r ^ 1, c ^ 1),
        "across": lambda r, c: (r, c ^ 2),
        "near": lambda r, c: (r, c ^ 1),
        "far": far,
    }
    at = lambda place: place[0] * cols + place[1]
    pairs = {name: [(at(p), at(way(*p))) for p in every] for name, way in ways.items()}
    pairs["across"] = [(at(p), at(ways["across"](*p))) for p in every if not keeps(*p)]
    return pairs


def call(kernel, outs, in_specs, out_specs, scratch=(), aliases={}, mib=12):
    return pl.pallas_call(
        kernel,
        out_shape=outs,
        in_specs=in_specs,
        out_specs=out_specs,
        scratch_shapes=scratch,
        input_output_aliases=aliases,
        compiler_params=pltpu.CompilerParams(vmem_limit_bytes=mib << 20),
    )


def here():
    r, c = lax.axis_index("row"), lax.axis_index("col")
    role = lax.rem(c, 2)
    keep = role == lax.rem(r, 2)
    half = lax.rem(lax.div(c, 2), 2)
    edge = jnp.where(role == 0, r < 2, r >= lax.axis_size("row") - 2)
    return role, keep, half, edge, c


def rotate_kernel(places, width, counts, rotation, *refs):
    pieces, out = refs[: len(places)], refs[len(places)]
    rot = rotation[...]
    high = rot.astype(BF16)
    low = (rot - high.astype(F32)).astype(BF16)
    mine, used = here()[4], counts[0] * width
    for place, piece in zip(places, pieces):
        rows = piece.shape[0]
        first = pl.multiple_of((mine ^ place) * rows, rows)
        x = piece[...]
        y = jnp.dot(x, high, preferred_element_type=F32) + jnp.dot(x, low, preferred_element_type=F32)
        at = first + lax.broadcasted_iota(jnp.int32, y.shape, 0)
        out[pl.ds(first, rows), :] = jnp.where(at < used, y, 0.0).astype(BF16)


def build_kernel(lot, held, cap, nblk, width, info, blocks, *refs):
    count = sum(pieces for _, _, pieces in lot)
    moved, refs = list(refs[:count]), refs[count:]
    near_out, far_out, raw, total, sems = refs[-5:]
    role, keep, half, at_edge, _ = here()
    slots = total.shape[0]
    near_slots = near_out.shape[1] // width
    parts = 4
    piece = nblk // parts
    place = lambda step, direct: row_of(half, step, direct, cap)

    def build(source, t):
        total[...] = jnp.zeros_like(total)
        for k in range(nblk):
            slot = slot_place(info[1 + t * nblk + k], role, cap, slots)
            total[slot] = total[slot] + source(k).astype(F32)
        scale = jnp.where(t < info[0], 2.0, 0.0).astype(F32)
        far_scale = jnp.where(at_edge, 0.0, scale)
        at = pl.ds(pl.multiple_of(t * width, width), width)
        for slot in range(slots):
            near = slot < near_slots
            lane = (slot if near else slot - near_slots) * width
            value = total[slot] * (scale if near else far_scale)
            (near_out if near else far_out)[at, lane : lane + width] = value.astype(BF16)

    def loads(n, t):
        cut = lambda p: pl.ds(p * piece, piece)
        return [
            pltpu.make_async_copy(blocks.at[t, cut(p)], raw.at[n, cut(p)], sems.at[n, p])
            for p in range(parts)
        ]

    if held:
        @pl.when(keep)
        def _():
            for n, row in enumerate(held):
                for copy in loads(n, place(*row)):
                    copy.start()

            def one(n, carry):
                steps = sum(jnp.where(n == at, step, 0) for at, (step, _) in enumerate(held))
                direct = sum(jnp.where(n == at, int(direct), 0) for at, (_, direct) in enumerate(held))
                t = place(steps, direct)
                for copy in loads(n, t):
                    copy.wait()
                build(lambda k: raw[n, k], t)
                return carry

            lax.fori_loop(0, len(held), one, 0)

    @pl.when(jnp.logical_not(keep))
    def _():
        for step, direct, pieces in lot:
            arrays = [moved.pop(0) for _ in range(pieces)]
            each = nblk // pieces
            build(lambda k: arrays[k // each][0, k % each], place(step, direct))


def gather_kernel(counts, cols, lists, out):
    out[0] = counts[0]
    at = 1
    for t in range(cols.shape[0]):
        for k in range(cols.shape[1]):
            out[at] = cols[t, k]
            at += 1
    for way in range(lists.shape[1]):
        for i in range(lists.shape[2]):
            out[at] = lists[0, way, i]
            at += 1


def tables_kernel(own, moved, info, send_lists):
    role, keep = here()[:2]
    get = lambda i: jnp.where(keep, own[i], moved[i])
    slots = info.shape[0]
    for i in range(slots):
        info[i] = get(i)
    edge = send_lists.shape[0] // 2
    for i in range(edge):
        up, down = get(slots + i), get(slots + edge + i)
        send_lists[i] = jnp.where(role == 0, up, down)
        send_lists[edge + i] = jnp.where(role == 0, down, up)


def row_of(half, step, direct, cap):
    flip = jnp.where(direct == 1, half, 1 - half)
    return jnp.where(flip == 1, cap - 1 - step, step)


def stage_kernel(cuts, cap, blocks, *refs):
    outs, sems = refs[:-1], refs[-1]
    half = here()[2]
    copies = []
    for n, ((step, first, count), out) in enumerate(zip(cuts, outs)):
        piece = count // 2
        for p in range(2):
            copies.append(
                pltpu.make_async_copy(
                    blocks.at[row_of(half, step, 1, cap), pl.ds(first + p * piece, piece)],
                    out.at[0, pl.ds(p * piece, piece)], sems.at[n, p],
                )
            )
    for copy in copies:
        copy.start()
    for copy in copies:
        copy.wait()


def slot_place(slot, role, cap, slots):
    edge = (slots - cap) // 2
    first = jnp.where(slot < edge, slot + slots - edge, slot - edge)
    second = jnp.where(slot < edge, slot + cap, jnp.where(slot < edge + cap, slot - edge, slot))
    return jnp.where(role == 0, first, second)


def pick(lists, first, edge, width):
    return [pl.ds(pl.multiple_of(lists[first + i] * width, width), width) for i in range(edge)]


def pack_kernel(width, edge, lists, own, moved, field, near_send, far_send):
    keep = here()[1]

    @pl.when(keep)
    def _():
        field[...] = own[...]

    @pl.when(jnp.logical_not(keep))
    def _():
        field[...] = moved[...]

    for first, send in ((0, near_send), (edge, far_send)):
        for i, rows in enumerate(pick(lists, first, edge, width)):
            send[i * width : (i + 1) * width, :] = field[rows, :]


def fetch(lists, table, sem):
    return pltpu.make_async_copy(lists, table, sem)


def local_kernel(width, edge, less, gives, lists, near_op, field, near, *refs):
    table, sem = refs[-2:]
    refs = list(refs[:-2])
    copy = fetch(lists, table, sem)
    copy.start()
    rows = field.shape[0]
    older = refs.pop(0) if less else None
    far_op = refs.pop(0) if gives == "both" else None
    acc = refs.pop(0)
    total = jnp.dot(near_op[:, :rows], field[...], preferred_element_type=F32) + jnp.dot(
        near_op[:, rows:], near[...], preferred_element_type=F32
    )
    acc[...] = total - older[...].astype(F32) if less else total
    copy.wait()
    if not gives:
        return
    part = refs.pop(0)
    for i, at in enumerate(pick(table, edge, edge, width)):
        part[i * width : (i + 1) * width, :] = acc[at, :].astype(part.dtype)
        if gives == "both":
            half, place = divmod(i, edge // 2)
            refs[half][place * width : (place + 1) * width, :] = far_op[at, :]


def result_of(first, acc, far_op, far):
    total = acc[...] + jnp.dot(far_op[...], far, preferred_element_type=F32)
    return 0.5 * total if first else total


def ahead_kernel(first, acc, low, high, far, out):
    far_op = jnp.concatenate([low[...], high[...]], axis=0)
    total = acc[...] + jnp.dot(far_op, far[...], preferred_element_type=F32)
    out[...] = (0.5 * total if first else total).astype(BF16)


def far_rows(part, low, high, sent):
    op = jnp.concatenate([low[...], high[...]], axis=0)
    total = part[...].astype(F32) + jnp.dot(op, sent[...], preferred_element_type=F32)
    return total.astype(BF16)


def finish_kernel(first, apart, wants, width, edge, lists, acc, far_op, *refs):
    table, sem = refs[-2:]
    refs = list(refs[:-2])
    copy = fetch(lists, table, sem)
    copy.start()
    if apart:
        far = far_rows(*refs[:4])
        refs = refs[4:]
    else:
        far = refs.pop(0)[...]
    total = result_of(first, acc, far_op, far)
    value, part = wants
    if value:
        refs.pop(0)[...] = total
    field, near_send = refs[:2]
    field[...] = total.astype(BF16)
    copy.wait()
    sends = [(0, near_send)] + ([(edge, refs[2])] if part else [])
    for begin, send in sends:
        for i, rows in enumerate(pick(table, begin, edge, width)):
            send[i * width : (i + 1) * width, :] = field[rows, :]


def last_kernel(begin, acc, far_op, part, low, high, sent, out):
    rows = pl.ds(begin, out.shape[1])
    far = far_rows(part, low, high, sent)
    total = acc[rows, :] + jnp.dot(far_op[rows, :], far, preferred_element_type=F32)
    out[...] = total.T.astype(BF16)


def merge_kernel(begin, own, moved, *refs):
    out, wide, sem = refs[-3:]
    keep = here()[1]

    @pl.when(keep)
    def _():
        wide[...] = own[...].astype(F32)

    @pl.when(jnp.logical_not(keep))
    def _():
        wide[...] = moved[...].astype(F32)

    copy = pltpu.make_async_copy(wide, out.at[:, pl.ds(begin, wide.shape[1])], sem)
    copy.start()
    copy.wait()


def body(vectors, rotation, blocks, cols, lists, counts):
    rows, columns = lax.axis_size("row"), lax.axis_size("col")
    ways = patterns(rows, columns)

    def send(x, way):
        return lax.ppermute(x, AXES, ways[way])

    cap, nblk, width = blocks.shape[0], blocks.shape[1], blocks.shape[2]
    edge = lists.shape[2]
    panel = rotation.shape[1]
    height = cap * width
    slots = cap + 2 * edge
    sds = jax.ShapeDtypeStruct

    ints = lambda n: sds((n,), jnp.int32)

    pieces = {0: vectors.astype(BF16)}
    bit = columns // 2
    while bit:
        for place in list(pieces):
            pieces[place ^ bit] = lax.ppermute(
                pieces[place], "col", [(k, k ^ bit) for k in range(columns)]
            )
        bit //= 2

    held = pltpu.with_memory_space_constraint(blocks, pltpu.HBM)
    middle, part_blocks = cap // 2, nblk // 2
    block_rows = lambda count: sds((1, count, width, width), BF16)

    def stage(*cuts):
        return call(
            functools.partial(stage_kernel, cuts, cap), tuple(block_rows(cut[2]) for cut in cuts),
            [HBM], (VMEM,) * len(cuts), scratch=(pltpu.SemaphoreType.DMA((len(cuts), 2)),),
        )(held)

    staged = stage((0, 0, nblk))
    staged += stage(
        *((k, 0, nblk) for k in range(1, middle - 1)),
        (middle - 1, part_blocks, part_blocks), (middle - 1, 0, part_blocks), (middle, 0, part_blocks),
    )
    direct = [send(x, "trade") for x in staged]
    relayed = [send(x, "across") for x in direct[:middle]]

    n_slots = 1 + cap * nblk
    own = call(gather_kernel, ints(n_slots + 2 * edge), [SMEM] * 3, SMEM)(counts, cols, lists)
    info, send_lists = call(
        tables_kernel, (ints(n_slots), ints(2 * edge)), [SMEM] * 2, (SMEM, SMEM)
    )(own, send(own, "trade"))

    field = call(
        functools.partial(rotate_kernel, tuple(pieces), width),
        sds((height, panel), BF16), [SMEM, VMEM] + [VMEM] * len(pieces), VMEM,
    )(counts, rotation, *pieces.values())
    moved_field = send(field, "trade")

    ops = ()
    op_shapes = (sds((height, height + edge * width), BF16), sds((height, edge * width), BF16))
    low, high, extra = direct[middle], direct[middle - 1], direct[middle + 1]
    cut = middle // 2
    lots = [
        [(k, 1, (direct[k],)) for k in range(cut)],
        [(k, 1, (direct[k],)) for k in range(cut, middle - 1)],
        [(k, 0, (relayed[k],)) for k in range(middle - 2)],
        [(middle - 2, 0, (relayed[middle - 2],)), (middle - 1, 1, (low, high))],
        [(middle, 1, (extra, relayed[middle - 1]))],
    ]
    whole = sum([[row[:2] for row in lot] for lot in lots], [])
    holds = [whole[: cap // 2], whole[cap // 2 :], [], [], []]
    for lot, hold in zip(lots, holds):
        given = [x for row in lot for x in row[2]]
        n = len(given)
        ops = call(
            functools.partial(build_kernel, [(*row[:2], len(row[2])) for row in lot], hold, cap, nblk, width),
            op_shapes, [SMEM, HBM] + [VMEM] * (n + len(ops)), (VMEM, VMEM),
            scratch=(
                pltpu.VMEM((max(1, len(hold)), nblk, width, width), BF16),
                pltpu.VMEM((slots, width, width), F32),
                pltpu.SemaphoreType.DMA((max(1, len(hold)), 4)),
            ),
            aliases={2 + n: 0, 3 + n: 1} if ops else {}, mib=20,
        )(info, held, *given, *ops)
    near_op, far_op = ops

    sent = sds((edge * width, panel), BF16)
    wide = lambda kind: sds((height, panel), kind)
    field, near_send, far_send = call(
        functools.partial(pack_kernel, width, edge), (wide(BF16), sent, sent),
        [SMEM, VMEM, VMEM], (VMEM,) * 3,
    )(send_lists, field, moved_field)
    older, newer = (), field
    part = lambda kind: sds((edge * width, panel), kind)
    square = sds((edge // 2 * width, edge * width), BF16)
    table = (pltpu.SMEM((2 * edge,), jnp.int32), pltpu.SemaphoreType.DMA)
    lists_at = pltpu.with_memory_space_constraint(send_lists, pltpu.HBM)
    moved_part, sent_rows, theirs = None, {}, []
    for step in range(STEPS):
        plain = step <= PLAIN
        first, last = step == 0, step == STEPS - 1
        near = send(near_send, "near")
        if plain:
            far = send(far_send, "far")
            sent_rows[step] = far_send
        if step == 1:
            theirs = [send(x, "far") for x in far_part]
        gives = "both" if first else "" if last else "one"
        kind = F32 if step < PLAIN else BF16
        outs = (wide(F32),) + ((part(kind),) if gives else ()) + ((square,) * 2 if first else ())
        given = (lists_at, near_op, field, near) + older + ((far_op,) if first else ())
        mine = call(
            functools.partial(local_kernel, width, edge, not first, gives), outs,
            [HBM] + [VMEM] * (len(given) - 1), (VMEM,) * len(outs), scratch=table,
        )(*given)
        acc = mine[0]
        if first:
            far_part = mine[2:]
        arrived_part, moved_part = moved_part, None
        if PLAIN <= step and not last:
            moved_part = send(mine[1], "far")
        if last:
            cut = height // 2
            ends = [
                call(
                    functools.partial(last_kernel, begin), sds((panel, cut), BF16), [VMEM] * 6, VMEM
                )(acc, far_op, arrived_part, *theirs, sent_rows[step - 1])
                for begin in (0, cut)
            ]
            backs = [send(x, "trade") for x in ends]
            out = ()
            for at, (own, back) in enumerate(zip(ends, backs)):
                out = (
                    call(
                        functools.partial(merge_kernel, at * cut), sds((panel, height), F32),
                        [VMEM] * 2 + [HBM] * len(out), HBM,
                        scratch=(pltpu.VMEM((panel, cut), F32), pltpu.SemaphoreType.DMA),
                        aliases={2: 0} if out else {},
                    )(own, back, *out),
                )
            return out[0]
        if step < PLAIN:
            far_send = call(functools.partial(ahead_kernel, first), sent, [VMEM] * 4, VMEM)(mine[1], *far_part, far)
        wants = (step < STEPS - 2, PLAIN <= step < STEPS - 2)
        outs = ((wide(F32),) if wants[0] else ()) + (wide(BF16), sent) + ((sent,) if wants[1] else ())
        given = (far,) if plain else (arrived_part, *theirs, sent_rows[step - 1])
        result = call(
            functools.partial(finish_kernel, first, not plain, wants, width, edge), outs,
            [HBM] + [VMEM] * (2 + len(given)), (VMEM,) * len(outs), scratch=table,
        )(lists_at, acc, far_op, *given)
        result = list(result)
        older, newer = (newer,), result.pop(0) if wants[0] else None
        field, near_send = result[:2]
        if wants[1]:
            sent_rows[step + 1] = result[2]


def solution(mesh):
    return jax.shard_map(
        body,
        mesh=mesh,
        in_specs=(
            P(("row", "col"), None),
            P(None, "col"),
            P("row", None, None, None),
            P("row", None),
            P("row", None, None),
            P("row"),
        ),
        out_specs=P("col", "row"),
        check_vma=False,
    )
```

```python
import functools

import jax
import jax.numpy as jnp
from jax import lax
from jax.experimental import pallas as pl
from jax.experimental.pallas import tpu as pltpu
from jax.sharding import PartitionSpec as P


STEPS = 10
PLAIN = 2
AXES = ("row", "col")
F32, BF16 = jnp.float32, jnp.bfloat16
VMEM = pl.BlockSpec(memory_space=pltpu.VMEM)
SMEM = pl.BlockSpec(memory_space=pltpu.SMEM)
HBM = pl.BlockSpec(memory_space=pltpu.HBM)
ANY = pl.BlockSpec(memory_space=pl.ANY)


def patterns(rows, cols):
    every = [(r, c) for r in range(rows) for c in range(cols)]
    keeps = lambda r, c: r % 2 == c % 2

    def far(r, c):
        to = r + 2 if c % 2 else r - 2
        return (to, c ^ 1) if 0 <= to < rows else (r ^ 1, c)

    ways = {
        "trade": lambda r, c: (r ^ 2, c) if keeps(r, c) else (r ^ 1, c ^ 1),
        "across": lambda r, c: (r, c ^ 2),
        "near": lambda r, c: (r, c ^ 1),
        "far": far,
    }
    at = lambda place: place[0] * cols + place[1]
    pairs = {name: [(at(p), at(way(*p))) for p in every] for name, way in ways.items()}
    pairs["across"] = [(at(p), at(ways["across"](*p))) for p in every if not keeps(*p)]
    return pairs


def call(kernel, outs, in_specs, out_specs, scratch=(), aliases={}, mib=12):
    return pl.pallas_call(
        kernel,
        out_shape=outs,
        in_specs=in_specs,
        out_specs=out_specs,
        scratch_shapes=scratch,
        input_output_aliases=aliases,
        compiler_params=pltpu.CompilerParams(vmem_limit_bytes=mib << 20),
    )


def here():
    r, c = lax.axis_index("row"), lax.axis_index("col")
    role = lax.rem(c, 2)
    keep = role == lax.rem(r, 2)
    half = lax.rem(lax.div(c, 2), 2)
    edge = jnp.where(role == 0, r < 2, r >= lax.axis_size("row") - 2)
    return role, keep, half, edge, c


def rotate_kernel(places, width, counts, rotation, *refs):
    pieces, out = refs[: len(places)], refs[len(places)]
    rot = rotation[...]
    high = rot.astype(BF16)
    low = (rot - high.astype(F32)).astype(BF16)
    mine, used = here()[4], counts[0] * width
    for place, piece in zip(places, pieces):
        rows = piece.shape[0]
        first = pl.multiple_of((mine ^ place) * rows, rows)
        x = piece[...]
        y = jnp.dot(x, high, preferred_element_type=F32) + jnp.dot(x, low, preferred_element_type=F32)
        at = first + lax.broadcasted_iota(jnp.int32, y.shape, 0)
        out[pl.ds(first, rows), :] = jnp.where(at < used, y, 0.0).astype(BF16)


def build_kernel(lot, held, cap, nblk, width, info, blocks, *refs):
    count = sum(pieces for _, _, pieces in lot)
    moved, refs = list(refs[:count]), refs[count:]
    near_out, far_out, raw, total, sems = refs[-5:]
    role, keep, half, at_edge, _ = here()
    slots = total.shape[0]
    near_slots = near_out.shape[1] // width
    parts = 4
    piece = nblk // parts
    place = lambda step, direct: row_of(half, step, direct, cap)

    def build(source, t):
        total[...] = jnp.zeros_like(total)
        for k in range(nblk):
            slot = slot_place(info[1 + t * nblk + k], role, cap, slots)
            total[slot] = total[slot] + source(k).astype(F32)
        scale = jnp.where(t < info[0], 2.0, 0.0).astype(F32)
        far_scale = jnp.where(at_edge, 0.0, scale)
        at = pl.ds(pl.multiple_of(t * width, width), width)
        for slot in range(slots):
            near = slot < near_slots
            lane = (slot if near else slot - near_slots) * width
            value = total[slot] * (scale if near else far_scale)
            (near_out if near else far_out)[at, lane : lane + width] = value.astype(BF16)

    def loads(n, t):
        cut = lambda p: pl.ds(p * piece, piece)
        return [
            pltpu.make_async_copy(blocks.at[t, cut(p)], raw.at[n, cut(p)], sems.at[n, p])
            for p in range(parts)
        ]

    if held:
        @pl.when(keep)
        def _():
            for n, row in enumerate(held):
                for copy in loads(n, place(*row)):
                    copy.start()

            def one(n, carry):
                steps = sum(jnp.where(n == at, step, 0) for at, (step, _) in enumerate(held))
                direct = sum(jnp.where(n == at, int(direct), 0) for at, (_, direct) in enumerate(held))
                t = place(steps, direct)
                for copy in loads(n, t):
                    copy.wait()
                build(lambda k: raw[n, k], t)
                return carry

            lax.fori_loop(0, len(held), one, 0)

    @pl.when(jnp.logical_not(keep))
    def _():
        for step, direct, pieces in lot:
            arrays = [moved.pop(0) for _ in range(pieces)]
            each = nblk // pieces
            build(lambda k: arrays[k // each][0, k % each], place(step, direct))


def gather_kernel(counts, cols, lists, out):
    out[0] = counts[0]
    at = 1
    for t in range(cols.shape[0]):
        for k in range(cols.shape[1]):
            out[at] = cols[t, k]
            at += 1
    for way in range(lists.shape[1]):
        for i in range(lists.shape[2]):
            out[at] = lists[0, way, i]
            at += 1


def tables_kernel(own, moved, info, send_lists):
    role, keep = here()[:2]
    get = lambda i: jnp.where(keep, own[i], moved[i])
    slots = info.shape[0]
    for i in range(slots):
        info[i] = get(i)
    edge = send_lists.shape[0] // 2
    for i in range(edge):
        up, down = get(slots + i), get(slots + edge + i)
        send_lists[i] = jnp.where(role == 0, up, down)
        send_lists[edge + i] = jnp.where(role == 0, down, up)


def row_of(half, step, direct, cap):
    flip = jnp.where(direct == 1, half, 1 - half)
    return jnp.where(flip == 1, cap - 1 - step, step)


def stage_kernel(cuts, cap, blocks, *refs):
    outs, sems = refs[:-1], refs[-1]
    half = here()[2]
    copies = []
    for n, ((step, first, count), out) in enumerate(zip(cuts, outs)):
        piece = count // 2
        for p in range(2):
            copies.append(
                pltpu.make_async_copy(
                    blocks.at[row_of(half, step, 1, cap), pl.ds(first + p * piece, piece)],
                    out.at[0, pl.ds(p * piece, piece)], sems.at[n, p],
                )
            )
    for copy in copies:
        copy.start()
    for copy in copies:
        copy.wait()


def slot_place(slot, role, cap, slots):
    edge = (slots - cap) // 2
    first = jnp.where(slot < edge, slot + slots - edge, slot - edge)
    second = jnp.where(slot < edge, slot + cap, jnp.where(slot < edge + cap, slot - edge, slot))
    return jnp.where(role == 0, first, second)


def pick(lists, first, edge, width):
    return [pl.ds(pl.multiple_of(lists[first + i] * width, width), width) for i in range(edge)]


def pack_kernel(width, edge, lists, own, moved, field, near_send, far_send):
    keep = here()[1]

    @pl.when(keep)
    def _():
        field[...] = own[...]

    @pl.when(jnp.logical_not(keep))
    def _():
        field[...] = moved[...]

    for first, send in ((0, near_send), (edge, far_send)):
        for i, rows in enumerate(pick(lists, first, edge, width)):
            send[i * width : (i + 1) * width, :] = field[rows, :]


def fetch(lists, table, sem):
    return pltpu.make_async_copy(lists, table, sem)


def local_kernel(width, edge, less, gives, lists, near_op, field, near, *refs):
    table, sem = refs[-2:]
    refs = list(refs[:-2])
    copy = fetch(lists, table, sem)
    copy.start()
    rows = field.shape[0]
    older = refs.pop(0) if less else None
    far_op = refs.pop(0) if gives == "both" else None
    acc = refs.pop(0)
    total = jnp.dot(near_op[:, :rows], field[...], preferred_element_type=F32) + jnp.dot(
        near_op[:, rows:], near[...], preferred_element_type=F32
    )
    acc[...] = total - older[...].astype(F32) if less else total
    copy.wait()
    if not gives:
        return
    part, near_part = refs[:2]
    ats = pick(table, edge, edge, width), pick(table, 0, edge, width)
    for out, places in zip((part, near_part), ats):
        for i, at in enumerate(places):
            out[i * width : (i + 1) * width, :] = acc[at, :].astype(out.dtype)
    if gives == "both":
        for i, at in enumerate(ats[0]):
            half, place = divmod(i, edge // 2)
            refs[2 + half][place * width : (place + 1) * width, :] = far_op[at, :]
        for i, at in enumerate(ats[1]):
            refs[4][i * width : (i + 1) * width, :] = far_op[at, :]


def result_of(first, acc, far_op, far):
    total = acc[...] + jnp.dot(far_op[...], far, preferred_element_type=F32)
    return 0.5 * total if first else total


def ahead_kernel(first, acc, low, high, far, out):
    far_op = jnp.concatenate([low[...], high[...]], axis=0)
    total = acc[...] + jnp.dot(far_op, far[...], preferred_element_type=F32)
    out[...] = (0.5 * total if first else total).astype(BF16)


def far_rows(part, low, high, sent):
    op = jnp.concatenate([low[...], high[...]], axis=0)
    total = part[...].astype(F32) + jnp.dot(op, sent[...], preferred_element_type=F32)
    return total.astype(BF16)


def near_kernel(first, apart, acc, far_op, *refs):
    if apart:
        far = far_rows(*refs[:4])
        refs[5][...] = far
        out = refs[4]
    else:
        far, out = refs[0][...], refs[1]
    out[...] = result_of(first, acc, far_op, far).astype(BF16)


def finish_kernel(first, wants, width, edge, lists, acc, far_op, far, *refs):
    table, sem = refs[-2:]
    refs = list(refs[:-2])
    copy = fetch(lists, table, sem)
    copy.start()
    total = result_of(first, acc, far_op, far[...])
    value, part = wants
    if value:
        refs.pop(0)[...] = total
    field = refs[0]
    field[...] = total.astype(BF16)
    copy.wait()
    if part:
        for i, rows in enumerate(pick(table, edge, edge, width)):
            refs[1][i * width : (i + 1) * width, :] = field[rows, :]


def last_kernel(begin, acc, far_op, part, low, high, sent, out):
    rows = pl.ds(begin, out.shape[1])
    far = far_rows(part, low, high, sent)
    total = acc[rows, :] + jnp.dot(far_op[rows, :], far, preferred_element_type=F32)
    out[...] = total.T.astype(BF16)


def merge_kernel(begin, own, moved, *refs):
    out, wide, sem = refs[-3:]
    keep = here()[1]

    @pl.when(keep)
    def _():
        wide[...] = own[...].astype(F32)

    @pl.when(jnp.logical_not(keep))
    def _():
        wide[...] = moved[...].astype(F32)

    copy = pltpu.make_async_copy(wide, out.at[:, pl.ds(begin, wide.shape[1])], sem)
    copy.start()
    copy.wait()


def body(vectors, rotation, blocks, cols, lists, counts):
    rows, columns = lax.axis_size("row"), lax.axis_size("col")
    ways = patterns(rows, columns)

    def send(x, way):
        return lax.ppermute(x, AXES, ways[way])

    cap, nblk, width = blocks.shape[0], blocks.shape[1], blocks.shape[2]
    edge = lists.shape[2]
    panel = rotation.shape[1]
    height = cap * width
    slots = cap + 2 * edge
    sds = jax.ShapeDtypeStruct

    ints = lambda n: sds((n,), jnp.int32)

    pieces = {0: vectors.astype(BF16)}
    bit = columns // 2
    while bit:
        for place in list(pieces):
            pieces[place ^ bit] = lax.ppermute(
                pieces[place], "col", [(k, k ^ bit) for k in range(columns)]
            )
        bit //= 2

    held = pltpu.with_memory_space_constraint(blocks, pltpu.HBM)
    middle, part_blocks = cap // 2, nblk // 2
    block_rows = lambda count: sds((1, count, width, width), BF16)

    def stage(*cuts):
        return call(
            functools.partial(stage_kernel, cuts, cap), tuple(block_rows(cut[2]) for cut in cuts),
            [HBM], (VMEM,) * len(cuts), scratch=(pltpu.SemaphoreType.DMA((len(cuts), 2)),),
        )(held)

    staged = stage((0, 0, nblk))
    staged += stage(
        *((k, 0, nblk) for k in range(1, middle - 1)),
        (middle - 1, part_blocks, part_blocks), (middle - 1, 0, part_blocks), (middle, 0, part_blocks),
    )
    direct = [send(x, "trade") for x in staged]
    relayed = [send(x, "across") for x in direct[:middle]]

    n_slots = 1 + cap * nblk
    own = call(gather_kernel, ints(n_slots + 2 * edge), [SMEM] * 3, SMEM)(counts, cols, lists)
    info, send_lists = call(
        tables_kernel, (ints(n_slots), ints(2 * edge)), [SMEM] * 2, (SMEM, SMEM)
    )(own, send(own, "trade"))

    field = call(
        functools.partial(rotate_kernel, tuple(pieces), width),
        sds((height, panel), BF16), [SMEM, VMEM] + [VMEM] * len(pieces), VMEM,
    )(counts, rotation, *pieces.values())
    moved_field = send(field, "trade")

    ops = ()
    op_shapes = (sds((height, height + edge * width), BF16), sds((height, edge * width), BF16))
    low, high, extra = direct[middle], direct[middle - 1], direct[middle + 1]
    cut = middle // 2
    lots = [
        [(k, 1, (direct[k],)) for k in range(cut)],
        [(k, 1, (direct[k],)) for k in range(cut, middle - 1)],
        [(k, 0, (relayed[k],)) for k in range(middle - 2)],
        [(middle - 2, 0, (relayed[middle - 2],)), (middle - 1, 1, (low, high))],
        [(middle, 1, (extra, relayed[middle - 1]))],
    ]
    whole = sum([[row[:2] for row in lot] for lot in lots], [])
    holds = [whole[: cap // 2], whole[cap // 2 :], [], [], []]
    for lot, hold in zip(lots, holds):
        given = [x for row in lot for x in row[2]]
        n = len(given)
        ops = call(
            functools.partial(build_kernel, [(*row[:2], len(row[2])) for row in lot], hold, cap, nblk, width),
            op_shapes, [SMEM, HBM] + [VMEM] * (n + len(ops)), (VMEM, VMEM),
            scratch=(
                pltpu.VMEM((max(1, len(hold)), nblk, width, width), BF16),
                pltpu.VMEM((slots, width, width), F32),
                pltpu.SemaphoreType.DMA((max(1, len(hold)), 4)),
            ),
            aliases={2 + n: 0, 3 + n: 1} if ops else {}, mib=20,
        )(info, held, *given, *ops)
    near_op, far_op = ops

    sent = sds((edge * width, panel), BF16)
    wide = lambda kind: sds((height, panel), kind)
    field, near_send, far_send = call(
        functools.partial(pack_kernel, width, edge), (wide(BF16), sent, sent),
        [SMEM, VMEM, VMEM], (VMEM,) * 3,
    )(send_lists, field, moved_field)
    older, newer = (), field
    part = lambda kind: sds((edge * width, panel), kind)
    square = sds((edge // 2 * width, edge * width), BF16)
    table = (pltpu.SMEM((2 * edge,), jnp.int32), pltpu.SemaphoreType.DMA)
    lists_at = pltpu.with_memory_space_constraint(send_lists, pltpu.HBM)
    moved_part, sent_rows, theirs = None, {}, []
    for step in range(STEPS):
        plain = step <= PLAIN
        first, last = step == 0, step == STEPS - 1
        near = send(near_send, "near")
        if plain:
            far = send(far_send, "far")
            sent_rows[step] = far_send
        if 0 < step <= 2:
            theirs.append(send(far_part[step - 1], "far"))
        gives = "both" if first else "" if last else "one"
        kind = F32 if step < PLAIN else BF16
        outs = (wide(F32),) + ((part(kind), part(F32)) if gives else ())
        outs += (square, square, sds((edge * width, edge * width), BF16)) if first else ()
        given = (lists_at, near_op, field, near) + older + ((far_op,) if first else ())
        mine = call(
            functools.partial(local_kernel, width, edge, not first, gives), outs,
            [HBM] + [VMEM] * (len(given) - 1), (VMEM,) * len(outs), scratch=table,
        )(*given)
        acc = mine[0]
        if first:
            far_part, near_far = mine[3:5], mine[5]
        arrived_part, moved_part = moved_part, None
        if PLAIN <= step and not last:
            moved_part = send(mine[1], "far")
        if last:
            cut = height // 2
            ends = [
                call(
                    functools.partial(last_kernel, begin), sds((panel, cut), BF16), [VMEM] * 6, VMEM
                )(acc, far_op, arrived_part, *theirs, sent_rows[step - 1])
                for begin in (0, cut)
            ]
            backs = [send(x, "trade") for x in ends]
            out = ()
            for at, (own, back) in enumerate(zip(ends, backs)):
                out = (
                    call(
                        functools.partial(merge_kernel, at * cut), sds((panel, height), F32),
                        [VMEM] * 2 + [HBM] * len(out), HBM,
                        scratch=(pltpu.VMEM((panel, cut), F32), pltpu.SemaphoreType.DMA),
                        aliases={2: 0} if out else {},
                    )(own, back, *out),
                )
            return out[0]
        if step < PLAIN:
            far_send = call(
                functools.partial(ahead_kernel, first), sent, [VMEM] * 4, VMEM
            )(mine[1], *far_part, far)
        given = (far,) if plain else (arrived_part, *theirs, sent_rows[step - 1])
        outs = (sent,) if plain else (sent, sent)
        ready = call(
            functools.partial(near_kernel, first, not plain), outs,
            [VMEM] * (2 + len(given)), (VMEM,) * len(outs),
        )(mine[2], near_far, *given)
        near_send = ready[0]
        far = far if plain else ready[1]
        wants = (step < STEPS - 2, PLAIN <= step < STEPS - 2)
        outs = ((wide(F32),) if wants[0] else ()) + (wide(BF16),) + ((sent,) if wants[1] else ())
        result = call(
            functools.partial(finish_kernel, first, wants, width, edge), outs,
            [HBM] + [VMEM] * 3, (VMEM,) * len(outs), scratch=table,
        )(lists_at, acc, far_op, far)
        result = list(result)
        older, newer = (newer,), result.pop(0) if wants[0] else None
        field = result[0]
        if wants[1]:
            sent_rows[step + 1] = result[1]


def solution(mesh):
    return jax.shard_map(
        body,
        mesh=mesh,
        in_specs=(
            P(("row", "col"), None),
            P(None, "col"),
            P("row", None, None, None),
            P("row", None),
            P("row", None, None),
            P("row"),
        ),
        out_specs=P("col", "row"),
        check_vma=False,
    )
```

```python
import functools

import jax
import jax.numpy as jnp
from jax import lax
from jax.experimental import pallas as pl
from jax.experimental.pallas import tpu as pltpu
from jax.sharding import PartitionSpec as P


STEPS = 10
PLAIN = 2
AXES = ("row", "col")
F32, BF16 = jnp.float32, jnp.bfloat16
VMEM = pl.BlockSpec(memory_space=pltpu.VMEM)
SMEM = pl.BlockSpec(memory_space=pltpu.SMEM)
HBM = pl.BlockSpec(memory_space=pltpu.HBM)
ANY = pl.BlockSpec(memory_space=pl.ANY)


def patterns(rows, cols):
    every = [(r, c) for r in range(rows) for c in range(cols)]
    keeps = lambda r, c: r % 2 == c % 2

    def far(r, c):
        to = r + 2 if c % 2 else r - 2
        return (to, c ^ 1) if 0 <= to < rows else (r ^ 1, c)

    ways = {
        "trade": lambda r, c: (r ^ 2, c) if keeps(r, c) else (r ^ 1, c ^ 1),
        "across": lambda r, c: (r, c ^ 2),
        "near": lambda r, c: (r, c ^ 1),
        "far": far,
    }
    at = lambda place: place[0] * cols + place[1]
    pairs = {name: [(at(p), at(way(*p))) for p in every] for name, way in ways.items()}
    pairs["across"] = [(at(p), at(ways["across"](*p))) for p in every if not keeps(*p)]
    return pairs


def call(kernel, outs, in_specs, out_specs, scratch=(), aliases={}, mib=12):
    return pl.pallas_call(
        kernel,
        out_shape=outs,
        in_specs=in_specs,
        out_specs=out_specs,
        scratch_shapes=scratch,
        input_output_aliases=aliases,
        compiler_params=pltpu.CompilerParams(vmem_limit_bytes=mib << 20),
    )


def here():
    r, c = lax.axis_index("row"), lax.axis_index("col")
    role = lax.rem(c, 2)
    keep = role == lax.rem(r, 2)
    half = lax.rem(lax.div(c, 2), 2)
    edge = jnp.where(role == 0, r < 2, r >= lax.axis_size("row") - 2)
    return role, keep, half, edge, c


def rotate_kernel(places, width, counts, rotation, *refs):
    pieces, out = refs[: len(places)], refs[len(places)]
    rot = rotation[...]
    high = rot.astype(BF16)
    low = (rot - high.astype(F32)).astype(BF16)
    mine, used = here()[4], counts[0] * width
    for place, piece in zip(places, pieces):
        rows = piece.shape[0]
        first = pl.multiple_of((mine ^ place) * rows, rows)
        x = piece[...]
        y = jnp.dot(x, high, preferred_element_type=F32) + jnp.dot(x, low, preferred_element_type=F32)
        at = first + lax.broadcasted_iota(jnp.int32, y.shape, 0)
        out[pl.ds(first, rows), :] = jnp.where(at < used, y, 0.0).astype(BF16)


def build_kernel(lot, held, cap, nblk, width, info, blocks, *refs):
    count = sum(pieces for _, _, pieces in lot)
    moved, refs = list(refs[:count]), refs[count:]
    near_out, far_out, raw, total, sems = refs[-5:]
    role, keep, half, at_edge, _ = here()
    slots = total.shape[0]
    near_slots = near_out.shape[1] // width
    parts = 4
    piece = nblk // parts
    place = lambda step, direct: row_of(half, step, direct, cap)

    def build(source, t):
        total[...] = jnp.zeros_like(total)
        for k in range(nblk):
            slot = slot_place(info[1 + t * nblk + k], role, cap, slots)
            total[slot] = total[slot] + source(k).astype(F32)
        scale = jnp.where(t < info[0], 2.0, 0.0).astype(F32)
        far_scale = jnp.where(at_edge, 0.0, scale)
        at = pl.ds(pl.multiple_of(t * width, width), width)
        for slot in range(slots):
            near = slot < near_slots
            lane = (slot if near else slot - near_slots) * width
            value = total[slot] * (scale if near else far_scale)
            (near_out if near else far_out)[at, lane : lane + width] = value.astype(BF16)

    def loads(n, t):
        cut = lambda p: pl.ds(p * piece, piece)
        return [
            pltpu.make_async_copy(blocks.at[t, cut(p)], raw.at[n, cut(p)], sems.at[n, p])
            for p in range(parts)
        ]

    if held:
        @pl.when(keep)
        def _():
            for n, row in enumerate(held):
                for copy in loads(n, place(*row)):
                    copy.start()

            def one(n, carry):
                steps = sum(jnp.where(n == at, step, 0) for at, (step, _) in enumerate(held))
                direct = sum(jnp.where(n == at, int(direct), 0) for at, (_, direct) in enumerate(held))
                t = place(steps, direct)
                for copy in loads(n, t):
                    copy.wait()
                build(lambda k: raw[n, k], t)
                return carry

            lax.fori_loop(0, len(held), one, 0)

    @pl.when(jnp.logical_not(keep))
    def _():
        for step, direct, pieces in lot:
            arrays = [moved.pop(0) for _ in range(pieces)]
            each = nblk // pieces
            build(lambda k: arrays[k // each][0, k % each], place(step, direct))


def gather_kernel(counts, cols, lists, out):
    out[0] = counts[0]
    at = 1
    for t in range(cols.shape[0]):
        for k in range(cols.shape[1]):
            out[at] = cols[t, k]
            at += 1
    for way in range(lists.shape[1]):
        for i in range(lists.shape[2]):
            out[at] = lists[0, way, i]
            at += 1


def tables_kernel(own, moved, info, send_lists, spread):
    role, keep = here()[:2]
    get = lambda i: jnp.where(keep, own[i], moved[i])
    slots = info.shape[0]
    for i in range(slots):
        info[i] = get(i)
    edge = send_lists.shape[0] // 2
    for i in range(edge):
        up, down = get(slots + i), get(slots + edge + i)
        send_lists[i] = jnp.where(role == 0, up, down)
        send_lists[edge + i] = jnp.where(role == 0, down, up)
    for i in range(2 * edge):
        spread[i : i + 1, :] = jnp.full((1, spread.shape[1]), send_lists[i].astype(F32), F32)


def row_of(half, step, direct, cap):
    flip = jnp.where(direct == 1, half, 1 - half)
    return jnp.where(flip == 1, cap - 1 - step, step)


def stage_kernel(cuts, cap, blocks, *refs):
    outs, sems = refs[:-1], refs[-1]
    half = here()[2]
    copies = []
    for n, ((step, first, count), out) in enumerate(zip(cuts, outs)):
        piece = count // 2
        for p in range(2):
            copies.append(
                pltpu.make_async_copy(
                    blocks.at[row_of(half, step, 1, cap), pl.ds(first + p * piece, piece)],
                    out.at[0, pl.ds(p * piece, piece)], sems.at[n, p],
                )
            )
    for copy in copies:
        copy.start()
    for copy in copies:
        copy.wait()


def slot_place(slot, role, cap, slots):
    edge = (slots - cap) // 2
    first = jnp.where(slot < edge, slot + slots - edge, slot - edge)
    second = jnp.where(slot < edge, slot + cap, jnp.where(slot < edge + cap, slot - edge, slot))
    return jnp.where(role == 0, first, second)


def pick(lists, first, edge, width):
    return [pl.ds(pl.multiple_of(lists[first + i] * width, width), width) for i in range(edge)]


def pack_kernel(width, edge, lists, own, moved, field, near_send, far_send):
    keep = here()[1]

    @pl.when(keep)
    def _():
        field[...] = own[...]

    @pl.when(jnp.logical_not(keep))
    def _():
        field[...] = moved[...]

    for first, send in ((0, near_send), (edge, far_send)):
        for i, rows in enumerate(pick(lists, first, edge, width)):
            send[i * width : (i + 1) * width, :] = field[rows, :]


def picked(spread, first, edge, width):
    index = lambda i: jnp.max(spread[i : i + 1, :]).astype(jnp.int32)
    return [pl.ds(pl.multiple_of(index(first + i) * width, width), width) for i in range(edge)]


def local_kernel(width, edge, less, gives, lists, near_op, field, near, *refs):
    refs = list(refs)
    ats = picked(lists, edge, edge, width), picked(lists, 0, edge, width)
    rows = field.shape[0]
    older = refs.pop(0) if less else None
    far_op = refs.pop(0) if gives == "both" else None
    acc = refs.pop(0)
    total = jnp.dot(near_op[:, :rows], field[...], preferred_element_type=F32) + jnp.dot(
        near_op[:, rows:], near[...], preferred_element_type=F32
    )
    acc[...] = total - older[...].astype(F32) if less else total
    if not gives:
        return
    part, near_part = refs[:2]
    for out, places in zip((part, near_part), ats):
        for i, at in enumerate(places):
            out[i * width : (i + 1) * width, :] = acc[at, :].astype(out.dtype)
    if gives == "both":
        for i, at in enumerate(ats[0]):
            half, place = divmod(i, edge // 2)
            refs[2 + half][place * width : (place + 1) * width, :] = far_op[at, :]
        for i, at in enumerate(ats[1]):
            refs[4][i * width : (i + 1) * width, :] = far_op[at, :]


def result_of(first, acc, far_op, far):
    total = acc[...] + jnp.dot(far_op[...], far, preferred_element_type=F32)
    return 0.5 * total if first else total


def ahead_kernel(first, acc, low, high, far, out):
    far_op = jnp.concatenate([low[...], high[...]], axis=0)
    total = acc[...] + jnp.dot(far_op, far[...], preferred_element_type=F32)
    out[...] = (0.5 * total if first else total).astype(BF16)


def far_rows(part, low, high, sent):
    op = jnp.concatenate([low[...], high[...]], axis=0)
    total = part[...].astype(F32) + jnp.dot(op, sent[...], preferred_element_type=F32)
    return total.astype(BF16)


def near_kernel(first, apart, acc, far_op, *refs):
    if apart:
        far = far_rows(*refs[:4])
        refs[5][...] = far
        out = refs[4]
    else:
        far, out = refs[0][...], refs[1]
    out[...] = result_of(first, acc, far_op, far).astype(BF16)


def finish_kernel(first, wants, width, edge, lists, acc, far_op, far, *refs):
    refs = list(refs)
    total = result_of(first, acc, far_op, far[...])
    value, part = wants
    if value:
        refs.pop(0)[...] = total
    field = refs[0]
    field[...] = total.astype(BF16)
    if part:
        for i, rows in enumerate(picked(lists, edge, edge, width)):
            refs[1][i * width : (i + 1) * width, :] = field[rows, :]


def last_kernel(begin, acc, far_op, part, low, high, sent, out):
    rows = pl.ds(begin, out.shape[1])
    far = far_rows(part, low, high, sent)
    total = acc[rows, :] + jnp.dot(far_op[rows, :], far, preferred_element_type=F32)
    out[...] = total.T.astype(BF16)


def merge_kernel(begin, own, moved, *refs):
    out, wide, sem = refs[-3:]
    keep = here()[1]

    @pl.when(keep)
    def _():
        wide[...] = own[...].astype(F32)

    @pl.when(jnp.logical_not(keep))
    def _():
        wide[...] = moved[...].astype(F32)

    copy = pltpu.make_async_copy(wide, out.at[:, pl.ds(begin, wide.shape[1])], sem)
    copy.start()
    copy.wait()


def body(vectors, rotation, blocks, cols, lists, counts):
    rows, columns = lax.axis_size("row"), lax.axis_size("col")
    ways = patterns(rows, columns)

    def send(x, way):
        return lax.ppermute(x, AXES, ways[way])

    cap, nblk, width = blocks.shape[0], blocks.shape[1], blocks.shape[2]
    edge = lists.shape[2]
    panel = rotation.shape[1]
    height = cap * width
    slots = cap + 2 * edge
    sds = jax.ShapeDtypeStruct

    ints = lambda n: sds((n,), jnp.int32)

    pieces = {0: vectors.astype(BF16)}
    bit = columns // 2
    while bit:
        for place in list(pieces):
            pieces[place ^ bit] = lax.ppermute(
                pieces[place], "col", [(k, k ^ bit) for k in range(columns)]
            )
        bit //= 2

    held = pltpu.with_memory_space_constraint(blocks, pltpu.HBM)
    middle, part_blocks = cap // 2, nblk // 2
    block_rows = lambda count: sds((1, count, width, width), BF16)

    def stage(*cuts):
        return call(
            functools.partial(stage_kernel, cuts, cap), tuple(block_rows(cut[2]) for cut in cuts),
            [HBM], (VMEM,) * len(cuts), scratch=(pltpu.SemaphoreType.DMA((len(cuts), 2)),),
        )(held)

    staged = stage((0, 0, nblk))
    staged += stage(
        *((k, 0, nblk) for k in range(1, middle - 1)),
        (middle - 1, part_blocks, part_blocks), (middle - 1, 0, part_blocks), (middle, 0, part_blocks),
    )
    direct = [send(x, "trade") for x in staged]
    relayed = [send(x, "across") for x in direct[:middle]]

    n_slots = 1 + cap * nblk
    own = call(gather_kernel, ints(n_slots + 2 * edge), [SMEM] * 3, SMEM)(counts, cols, lists)
    info, send_lists, spread = call(
        tables_kernel, (ints(n_slots), ints(2 * edge), sds((2 * edge, width), F32)),
        [SMEM] * 2, (SMEM, SMEM, VMEM),
    )(own, send(own, "trade"))

    field = call(
        functools.partial(rotate_kernel, tuple(pieces), width),
        sds((height, panel), BF16), [SMEM, VMEM] + [VMEM] * len(pieces), VMEM,
    )(counts, rotation, *pieces.values())
    moved_field = send(field, "trade")

    ops = ()
    op_shapes = (sds((height, height + edge * width), BF16), sds((height, edge * width), BF16))
    low, high, extra = direct[middle], direct[middle - 1], direct[middle + 1]
    cut = middle // 2
    lots = [
        [(k, 1, (direct[k],)) for k in range(cut)],
        [(k, 1, (direct[k],)) for k in range(cut, middle - 1)],
        [(k, 0, (relayed[k],)) for k in range(middle - 2)],
        [(middle - 2, 0, (relayed[middle - 2],)), (middle - 1, 1, (low, high))],
        [(middle, 1, (extra, relayed[middle - 1]))],
    ]
    whole = sum([[row[:2] for row in lot] for lot in lots], [])
    holds = [whole[: cap // 2], whole[cap // 2 :], [], [], []]
    for lot, hold in zip(lots, holds):
        given = [x for row in lot for x in row[2]]
        n = len(given)
        ops = call(
            functools.partial(build_kernel, [(*row[:2], len(row[2])) for row in lot], hold, cap, nblk, width),
            op_shapes, [SMEM, HBM] + [VMEM] * (n + len(ops)), (VMEM, VMEM),
            scratch=(
                pltpu.VMEM((max(1, len(hold)), nblk, width, width), BF16),
                pltpu.VMEM((slots, width, width), F32),
                pltpu.SemaphoreType.DMA((max(1, len(hold)), 4)),
            ),
            aliases={2 + n: 0, 3 + n: 1} if ops else {}, mib=20,
        )(info, held, *given, *ops)
    near_op, far_op = ops

    sent = sds((edge * width, panel), BF16)
    wide = lambda kind: sds((height, panel), kind)
    field, near_send, far_send = call(
        functools.partial(pack_kernel, width, edge), (wide(BF16), sent, sent),
        [SMEM, VMEM, VMEM], (VMEM,) * 3,
    )(send_lists, field, moved_field)
    older, newer = (), field
    part = lambda kind: sds((edge * width, panel), kind)
    square = sds((edge // 2 * width, edge * width), BF16)
    moved_part, sent_rows, theirs = None, {}, []
    for step in range(STEPS):
        plain = step <= PLAIN
        first, last = step == 0, step == STEPS - 1
        near = send(near_send, "near")
        if plain:
            far = send(far_send, "far")
            sent_rows[step] = far_send
        if 0 < step <= 2:
            theirs.append(send(far_part[step - 1], "far"))
        gives = "both" if first else "" if last else "one"
        kind = F32 if step < PLAIN else BF16
        outs = (wide(F32),) + ((part(kind), part(F32)) if gives else ())
        outs += (square, square, sds((edge * width, edge * width), BF16)) if first else ()
        given = (spread, near_op, field, near) + older + ((far_op,) if first else ())
        mine = call(
            functools.partial(local_kernel, width, edge, not first, gives), outs,
            [VMEM] * len(given), (VMEM,) * len(outs),
        )(*given)
        acc = mine[0]
        if first:
            far_part, near_far = mine[3:5], mine[5]
        arrived_part, moved_part = moved_part, None
        if PLAIN <= step and not last:
            moved_part = send(mine[1], "far")
        if last:
            cut = height // 2
            ends = [
                call(
                    functools.partial(last_kernel, begin), sds((panel, cut), BF16), [VMEM] * 6, VMEM
                )(acc, far_op, arrived_part, *theirs, sent_rows[step - 1])
                for begin in (0, cut)
            ]
            backs = [send(x, "trade") for x in ends]
            out = ()
            for at, (own, back) in enumerate(zip(ends, backs)):
                out = (
                    call(
                        functools.partial(merge_kernel, at * cut), sds((panel, height), F32),
                        [VMEM] * 2 + [HBM] * len(out), HBM,
                        scratch=(pltpu.VMEM((panel, cut), F32), pltpu.SemaphoreType.DMA),
                        aliases={2: 0} if out else {},
                    )(own, back, *out),
                )
            return out[0]
        if step < PLAIN:
            far_send = call(
                functools.partial(ahead_kernel, first), sent, [VMEM] * 4, VMEM
            )(mine[1], *far_part, far)
        given = (far,) if plain else (arrived_part, *theirs, sent_rows[step - 1])
        outs = (sent,) if plain else (sent, sent)
        ready = call(
            functools.partial(near_kernel, first, not plain), outs,
            [VMEM] * (2 + len(given)), (VMEM,) * len(outs),
        )(mine[2], near_far, *given)
        near_send = ready[0]
        far = far if plain else ready[1]
        wants = (step < STEPS - 2, PLAIN <= step < STEPS - 2)
        outs = ((wide(F32),) if wants[0] else ()) + (wide(BF16),) + ((sent,) if wants[1] else ())
        result = call(
            functools.partial(finish_kernel, first, wants, width, edge), outs,
            [VMEM] * 4, (VMEM,) * len(outs),
        )(spread, acc, far_op, far)
        result = list(result)
        older, newer = (newer,), result.pop(0) if wants[0] else None
        field = result[0]
        if wants[1]:
            sent_rows[step + 1] = result[1]


def solution(mesh):
    return jax.shard_map(
        body,
        mesh=mesh,
        in_specs=(
            P(("row", "col"), None),
            P(None, "col"),
            P("row", None, None, None),
            P("row", None),
            P("row", None, None),
            P("row"),
        ),
        out_specs=P("col", "row"),
        check_vma=False,
    )
```

```python
import functools

import jax
import jax.numpy as jnp
from jax import lax
from jax.experimental import pallas as pl
from jax.experimental.pallas import tpu as pltpu
from jax.sharding import PartitionSpec as P


STEPS = 10
PLAIN = 2
AXES = ("row", "col")
F32, BF16 = jnp.float32, jnp.bfloat16
VMEM = pl.BlockSpec(memory_space=pltpu.VMEM)
SMEM = pl.BlockSpec(memory_space=pltpu.SMEM)
HBM = pl.BlockSpec(memory_space=pltpu.HBM)
ANY = pl.BlockSpec(memory_space=pl.ANY)


def patterns(rows, cols):
    every = [(r, c) for r in range(rows) for c in range(cols)]
    keeps = lambda r, c: r % 2 == c % 2

    def far(r, c):
        to = r + 2 if c % 2 else r - 2
        return (to, c ^ 1) if 0 <= to < rows else (r ^ 1, c)

    ways = {
        "trade": lambda r, c: (r ^ 2, c) if keeps(r, c) else (r ^ 1, c ^ 1),
        "across": lambda r, c: (r, c ^ 2),
        "near": lambda r, c: (r, c ^ 1),
        "far": far,
    }
    at = lambda place: place[0] * cols + place[1]
    pairs = {name: [(at(p), at(way(*p))) for p in every] for name, way in ways.items()}
    pairs["across"] = [(at(p), at(ways["across"](*p))) for p in every if not keeps(*p)]
    return pairs


def call(kernel, outs, in_specs, out_specs, scratch=(), aliases={}, mib=12):
    return pl.pallas_call(
        kernel,
        out_shape=outs,
        in_specs=in_specs,
        out_specs=out_specs,
        scratch_shapes=scratch,
        input_output_aliases=aliases,
        compiler_params=pltpu.CompilerParams(vmem_limit_bytes=mib << 20),
    )


def here():
    r, c = lax.axis_index("row"), lax.axis_index("col")
    role = lax.rem(c, 2)
    keep = role == lax.rem(r, 2)
    half = lax.rem(lax.div(c, 2), 2)
    edge = jnp.where(role == 0, r < 2, r >= lax.axis_size("row") - 2)
    return role, keep, half, edge, c


def rotate_kernel(places, width, counts, rotation, *refs):
    pieces, out = refs[: len(places)], refs[len(places)]
    rot = rotation[...]
    high = rot.astype(BF16)
    low = (rot - high.astype(F32)).astype(BF16)
    mine, used = here()[4], counts[0] * width
    for place, piece in zip(places, pieces):
        rows = piece.shape[0]
        first = pl.multiple_of((mine ^ place) * rows, rows)
        x = piece[...]
        y = jnp.dot(x, high, preferred_element_type=F32) + jnp.dot(x, low, preferred_element_type=F32)
        at = first + lax.broadcasted_iota(jnp.int32, y.shape, 0)
        out[pl.ds(first, rows), :] = jnp.where(at < used, y, 0.0).astype(BF16)


def build_kernel(lot, held, cap, nblk, width, info, blocks, *refs):
    count = sum(pieces for _, _, pieces in lot)
    moved, refs = list(refs[:count]), refs[count:]
    near_out, far_out, raw, total, sems = refs[-5:]
    role, keep, half, at_edge, _ = here()
    slots = total.shape[0]
    near_slots = near_out.shape[1] // width
    parts = 4
    piece = nblk // parts
    place = lambda step, direct: row_of(half, step, direct, cap)

    def build(source, t):
        total[...] = jnp.zeros_like(total)
        for k in range(nblk):
            slot = slot_place(info[1 + t * nblk + k], role, cap, slots)
            total[slot] = total[slot] + source(k).astype(F32)
        scale = jnp.where(t < info[0], 2.0, 0.0).astype(F32)
        far_scale = jnp.where(at_edge, 0.0, scale)
        at = pl.ds(pl.multiple_of(t * width, width), width)
        for slot in range(slots):
            near = slot < near_slots
            lane = (slot if near else slot - near_slots) * width
            value = total[slot] * (scale if near else far_scale)
            (near_out if near else far_out)[at, lane : lane + width] = value.astype(BF16)

    def loads(n, t):
        cut = lambda p: pl.ds(p * piece, piece)
        return [
            pltpu.make_async_copy(blocks.at[t, cut(p)], raw.at[n, cut(p)], sems.at[n, p])
            for p in range(parts)
        ]

    if held:
        @pl.when(keep)
        def _():
            for n, row in enumerate(held):
                for copy in loads(n, place(*row)):
                    copy.start()

            def one(n, carry):
                steps = sum(jnp.where(n == at, step, 0) for at, (step, _) in enumerate(held))
                direct = sum(jnp.where(n == at, int(direct), 0) for at, (_, direct) in enumerate(held))
                t = place(steps, direct)
                for copy in loads(n, t):
                    copy.wait()
                build(lambda k: raw[n, k], t)
                return carry

            lax.fori_loop(0, len(held), one, 0)

    @pl.when(jnp.logical_not(keep))
    def _():
        for step, direct, pieces in lot:
            arrays = [moved.pop(0) for _ in range(pieces)]
            each = nblk // pieces
            build(lambda k: arrays[k // each][0, k % each], place(step, direct))


def gather_kernel(counts, cols, lists, out):
    out[0] = counts[0]
    at = 1
    for t in range(cols.shape[0]):
        for k in range(cols.shape[1]):
            out[at] = cols[t, k]
            at += 1
    for way in range(lists.shape[1]):
        for i in range(lists.shape[2]):
            out[at] = lists[0, way, i]
            at += 1


def tables_kernel(own, moved, info, send_lists, spread):
    role, keep = here()[:2]
    get = lambda i: jnp.where(keep, own[i], moved[i])
    slots = info.shape[0]
    for i in range(slots):
        info[i] = get(i)
    edge = send_lists.shape[0] // 2
    for i in range(edge):
        up, down = get(slots + i), get(slots + edge + i)
        send_lists[i] = jnp.where(role == 0, up, down)
        send_lists[edge + i] = jnp.where(role == 0, down, up)
    for i in range(2 * edge):
        spread[i : i + 1, :] = jnp.full((1, spread.shape[1]), send_lists[i].astype(F32), F32)


def row_of(half, step, direct, cap):
    flip = jnp.where(direct == 1, half, 1 - half)
    return jnp.where(flip == 1, cap - 1 - step, step)


def stage_kernel(cuts, cap, blocks, *refs):
    outs, sems = refs[:-1], refs[-1]
    half = here()[2]
    copies = []
    for n, ((step, first, count), out) in enumerate(zip(cuts, outs)):
        piece = count // 2
        for p in range(2):
            copies.append(
                pltpu.make_async_copy(
                    blocks.at[row_of(half, step, 1, cap), pl.ds(first + p * piece, piece)],
                    out.at[0, pl.ds(p * piece, piece)], sems.at[n, p],
                )
            )
    for copy in copies:
        copy.start()
    for copy in copies:
        copy.wait()


def slot_place(slot, role, cap, slots):
    edge = (slots - cap) // 2
    first = jnp.where(slot < edge, slot + slots - edge, slot - edge)
    second = jnp.where(slot < edge, slot + cap, jnp.where(slot < edge + cap, slot - edge, slot))
    return jnp.where(role == 0, first, second)


def pick(lists, first, edge, width):
    return [pl.ds(pl.multiple_of(lists[first + i] * width, width), width) for i in range(edge)]


def pack_kernel(width, edge, lists, own, moved, field, near_send, far_send):
    keep = here()[1]

    @pl.when(keep)
    def _():
        field[...] = own[...]

    @pl.when(jnp.logical_not(keep))
    def _():
        field[...] = moved[...]

    for first, send in ((0, near_send), (edge, far_send)):
        for i, rows in enumerate(pick(lists, first, edge, width)):
            send[i * width : (i + 1) * width, :] = field[rows, :]


def picked(spread, first, edge, width):
    index = lambda i: jnp.max(spread[i : i + 1, :]).astype(jnp.int32)
    return [pl.ds(pl.multiple_of(index(first + i) * width, width), width) for i in range(edge)]


def local_kernel(width, edge, less, gives, lists, near_op, field, near, *refs):
    refs = list(refs)
    ats = picked(lists, edge, edge, width), picked(lists, 0, edge, width)
    rows = field.shape[0]
    older = refs.pop(0) if less else None
    far_op = refs.pop(0) if gives == "both" else None
    acc = refs.pop(0)
    total = jnp.dot(near_op[:, :rows], field[...], preferred_element_type=F32) + jnp.dot(
        near_op[:, rows:], near[...], preferred_element_type=F32
    )
    acc[...] = total - older[...].astype(F32) if less else total
    if not gives:
        return
    part, near_part = refs[:2]
    for out, places in zip((part, near_part), ats):
        for i, at in enumerate(places):
            out[i * width : (i + 1) * width, :] = acc[at, :].astype(out.dtype)
    if gives == "both":
        for i, at in enumerate(ats[0]):
            half, place = divmod(i, edge // 2)
            refs[2 + half][place * width : (place + 1) * width, :] = far_op[at, :]
        for i, at in enumerate(ats[1]):
            refs[4][i * width : (i + 1) * width, :] = far_op[at, :]


def result_of(first, acc, far_op, far):
    total = acc[...] + jnp.dot(far_op[...], far, preferred_element_type=F32)
    return 0.5 * total if first else total


def ahead_kernel(first, acc, low, high, far, out):
    half = low.shape[0]
    for at, op in ((0, low), (half, high)):
        rows = pl.ds(at, half)
        total = acc[rows, :] + jnp.dot(op[...], far[...], preferred_element_type=F32)
        out[rows, :] = (0.5 * total if first else total).astype(BF16)


def far_rows(part, low, high, sent, out):
    half = low.shape[0]
    for at, op in ((0, low), (half, high)):
        rows = pl.ds(at, half)
        total = part[rows, :].astype(F32) + jnp.dot(op[...], sent[...], preferred_element_type=F32)
        out[rows, :] = total.astype(BF16)


def mix_kernel(far_op, low, high, out):
    half = low.shape[0]
    total = jnp.dot(far_op[:, :half], low[...], preferred_element_type=F32) + jnp.dot(
        far_op[:, half:], high[...], preferred_element_type=F32
    )
    out[...] = total.astype(BF16)


def before_kernel(near_part, mixed, sent, out):
    out[...] = near_part[...] + jnp.dot(mixed[...], sent[...], preferred_element_type=F32)


def near_kernel(first, acc, far_op, far, out):
    out[...] = result_of(first, acc, far_op, far[...]).astype(BF16)


def finish_kernel(first, apart, wants, width, edge, spread, acc, far_op, *refs):
    refs = list(refs)
    if apart:
        far = refs.pop()
        far_rows(*refs[:4], far)
        refs = refs[4:]
    else:
        far = refs.pop(0)
    total = result_of(first, acc, far_op, far[...])
    value, part = wants
    if value:
        refs.pop(0)[...] = total
    field = refs[0]
    field[...] = total.astype(BF16)
    if part:
        for i, rows in enumerate(picked(spread, edge, edge, width)):
            refs[1][i * width : (i + 1) * width, :] = field[rows, :]


def last_kernel(begin, acc, far_op, part, low, high, sent, out, far):
    rows = pl.ds(begin, out.shape[1])
    far_rows(part, low, high, sent, far)
    total = acc[rows, :] + jnp.dot(far_op[rows, :], far[...], preferred_element_type=F32)
    out[...] = total.T.astype(BF16)


def merge_kernel(begin, own, moved, *refs):
    out, wide, sem = refs[-3:]
    keep = here()[1]

    @pl.when(keep)
    def _():
        wide[...] = own[...].astype(F32)

    @pl.when(jnp.logical_not(keep))
    def _():
        wide[...] = moved[...].astype(F32)

    copy = pltpu.make_async_copy(wide, out.at[:, pl.ds(begin, wide.shape[1])], sem)
    copy.start()
    copy.wait()


def body(vectors, rotation, blocks, cols, lists, counts):
    rows, columns = lax.axis_size("row"), lax.axis_size("col")
    ways = patterns(rows, columns)

    def send(x, way):
        return lax.ppermute(x, AXES, ways[way])

    cap, nblk, width = blocks.shape[0], blocks.shape[1], blocks.shape[2]
    edge = lists.shape[2]
    panel = rotation.shape[1]
    height = cap * width
    slots = cap + 2 * edge
    sds = jax.ShapeDtypeStruct

    ints = lambda n: sds((n,), jnp.int32)

    pieces = {0: vectors.astype(BF16)}
    bit = columns // 2
    while bit:
        for place in list(pieces):
            pieces[place ^ bit] = lax.ppermute(
                pieces[place], "col", [(k, k ^ bit) for k in range(columns)]
            )
        bit //= 2

    held = pltpu.with_memory_space_constraint(blocks, pltpu.HBM)
    middle, part_blocks = cap // 2, nblk // 2
    block_rows = lambda count: sds((1, count, width, width), BF16)

    def stage(*cuts):
        return call(
            functools.partial(stage_kernel, cuts, cap), tuple(block_rows(cut[2]) for cut in cuts),
            [HBM], (VMEM,) * len(cuts), scratch=(pltpu.SemaphoreType.DMA((len(cuts), 2)),),
        )(held)

    staged = stage((0, 0, nblk))
    staged += stage(
        *((k, 0, nblk) for k in range(1, middle - 1)),
        (middle - 1, part_blocks, part_blocks), (middle - 1, 0, part_blocks), (middle, 0, part_blocks),
    )
    direct = [send(x, "trade") for x in staged]
    relayed = [send(x, "across") for x in direct[:middle]]

    n_slots = 1 + cap * nblk
    own = call(gather_kernel, ints(n_slots + 2 * edge), [SMEM] * 3, SMEM)(counts, cols, lists)
    info, send_lists, spread = call(
        tables_kernel, (ints(n_slots), ints(2 * edge), sds((2 * edge, width), F32)),
        [SMEM] * 2, (SMEM, SMEM, VMEM),
    )(own, send(own, "trade"))

    field = call(
        functools.partial(rotate_kernel, tuple(pieces), width),
        sds((height, panel), BF16), [SMEM, VMEM] + [VMEM] * len(pieces), VMEM,
    )(counts, rotation, *pieces.values())
    moved_field = send(field, "trade")

    ops = ()
    op_shapes = (sds((height, height + edge * width), BF16), sds((height, edge * width), BF16))
    low, high, extra = direct[middle], direct[middle - 1], direct[middle + 1]
    cut = middle // 2
    lots = [
        [(k, 1, (direct[k],)) for k in range(cut)],
        [(k, 1, (direct[k],)) for k in range(cut, middle - 1)],
        [(k, 0, (relayed[k],)) for k in range(middle - 2)],
        [(middle - 2, 0, (relayed[middle - 2],)), (middle - 1, 1, (low, high))],
        [(middle, 1, (extra, relayed[middle - 1]))],
    ]
    whole = sum([[row[:2] for row in lot] for lot in lots], [])
    holds = [whole[: cap // 2], whole[cap // 2 :], [], [], []]
    for lot, hold in zip(lots, holds):
        given = [x for row in lot for x in row[2]]
        n = len(given)
        ops = call(
            functools.partial(build_kernel, [(*row[:2], len(row[2])) for row in lot], hold, cap, nblk, width),
            op_shapes, [SMEM, HBM] + [VMEM] * (n + len(ops)), (VMEM, VMEM),
            scratch=(
                pltpu.VMEM((max(1, len(hold)), nblk, width, width), BF16),
                pltpu.VMEM((slots, width, width), F32),
                pltpu.SemaphoreType.DMA((max(1, len(hold)), 4)),
            ),
            aliases={2 + n: 0, 3 + n: 1} if ops else {}, mib=20,
        )(info, held, *given, *ops)
    near_op, far_op = ops

    sent = sds((edge * width, panel), BF16)
    wide = lambda kind: sds((height, panel), kind)
    field, near_send, far_send = call(
        functools.partial(pack_kernel, width, edge), (wide(BF16), sent, sent),
        [SMEM, VMEM, VMEM], (VMEM,) * 3,
    )(send_lists, field, moved_field)
    older, newer = (), field
    part = lambda kind: sds((edge * width, panel), kind)
    square = sds((edge // 2 * width, edge * width), BF16)
    moved_part, sent_rows, theirs, mixed = None, {}, [], None
    for step in range(STEPS):
        plain = step <= PLAIN
        first, last = step == 0, step == STEPS - 1
        near = send(near_send, "near")
        if plain:
            far = send(far_send, "far")
            sent_rows[step] = far_send
        if 0 < step <= 2:
            theirs.append(send(far_part[step - 1], "far"))
        gives = "both" if first else "" if last else "one"
        kind = F32 if step < PLAIN else BF16
        outs = (wide(F32),) + ((part(kind), part(F32)) if gives else ())
        outs += (square, square, sds((edge * width, edge * width), BF16)) if first else ()
        given = (spread, near_op, field, near) + older + ((far_op,) if first else ())
        mine = call(
            functools.partial(local_kernel, width, edge, not first, gives), outs,
            [VMEM] * len(given), (VMEM,) * len(outs),
        )(*given)
        acc = mine[0]
        if first:
            far_part, near_far = mine[3:5], mine[5]
        arrived_part, moved_part = moved_part, None
        if PLAIN <= step and not last:
            moved_part = send(mine[1], "far")
        if last:
            cut = height // 2
            ends = [
                call(
                    functools.partial(last_kernel, begin), sds((panel, cut), BF16), [VMEM] * 6, VMEM,
                    scratch=(pltpu.VMEM((edge * width, panel), BF16),),
                )(acc, far_op, arrived_part, *theirs, sent_rows[step - 1])
                for begin in (0, cut)
            ]
            backs = [send(x, "trade") for x in ends]
            out = ()
            for at, (own, back) in enumerate(zip(ends, backs)):
                out = (
                    call(
                        functools.partial(merge_kernel, at * cut), sds((panel, height), F32),
                        [VMEM] * 2 + [HBM] * len(out), HBM,
                        scratch=(pltpu.VMEM((panel, cut), F32), pltpu.SemaphoreType.DMA),
                        aliases={2: 0} if out else {},
                    )(own, back, *out),
                )
            return out[0]
        if step < PLAIN:
            far_send = call(
                functools.partial(ahead_kernel, first), sent, [VMEM] * 4, VMEM
            )(mine[1], *far_part, far)
        ready, given, scratch = mine[2], (far,), ()
        if not plain:
            if mixed is None:
                mixed = call(
                    mix_kernel, sds((edge * width,) * 2, BF16), [VMEM] * 3, VMEM
                )(near_far, *theirs)
            ready = call(before_kernel, part(F32), [VMEM] * 3, VMEM)(
                mine[2], mixed, sent_rows[step - 1]
            )
            given = (arrived_part, *theirs, sent_rows[step - 1])
            scratch = (pltpu.VMEM((edge * width, panel), BF16),)
        near_send = call(
            functools.partial(near_kernel, first), sent, [VMEM] * 3, VMEM
        )(ready, near_far, given[0])
        wants = (step < STEPS - 2, PLAIN <= step < STEPS - 2)
        outs = ((wide(F32),) if wants[0] else ()) + (wide(BF16),) + ((sent,) if wants[1] else ())
        result = call(
            functools.partial(finish_kernel, first, not plain, wants, width, edge), outs,
            [VMEM] * (3 + len(given)), (VMEM,) * len(outs), scratch=scratch,
        )(spread, acc, far_op, *given)
        result = list(result)
        older, newer = (newer,), result.pop(0) if wants[0] else None
        field = result[0]
        if wants[1]:
            sent_rows[step + 1] = result[1]


def solution(mesh):
    return jax.shard_map(
        body,
        mesh=mesh,
        in_specs=(
            P(("row", "col"), None),
            P(None, "col"),
            P("row", None, None, None),
            P("row", None),
            P("row", None, None),
            P("row"),
        ),
        out_specs=P("col", "row"),
        check_vma=False,
    )
```

```python
import functools

import jax
import jax.numpy as jnp
from jax import lax
from jax.experimental import pallas as pl
from jax.experimental.pallas import tpu as pltpu
from jax.sharding import PartitionSpec as P


STEPS = 10
PLAIN = 2
AXES = ("row", "col")
F32, BF16 = jnp.float32, jnp.bfloat16
VMEM = pl.BlockSpec(memory_space=pltpu.VMEM)
SMEM = pl.BlockSpec(memory_space=pltpu.SMEM)
HBM = pl.BlockSpec(memory_space=pltpu.HBM)
ANY = pl.BlockSpec(memory_space=pl.ANY)


def patterns(rows, cols):
    every = [(r, c) for r in range(rows) for c in range(cols)]
    keeps = lambda r, c: r % 2 == c % 2

    def far(r, c):
        to = r + 2 if c % 2 else r - 2
        return (to, c ^ 1) if 0 <= to < rows else (r ^ 1, c)

    ways = {
        "trade": lambda r, c: (r ^ 2, c) if keeps(r, c) else (r ^ 1, c ^ 1),
        "across": lambda r, c: (r, c ^ 2),
        "near": lambda r, c: (r, c ^ 1),
        "far": far,
    }
    at = lambda place: place[0] * cols + place[1]
    pairs = {name: [(at(p), at(way(*p))) for p in every] for name, way in ways.items()}
    pairs["across"] = [(at(p), at(ways["across"](*p))) for p in every if not keeps(*p)]
    return pairs


def call(kernel, outs, in_specs, out_specs, scratch=(), aliases={}, mib=12):
    return pl.pallas_call(
        kernel,
        out_shape=outs,
        in_specs=in_specs,
        out_specs=out_specs,
        scratch_shapes=scratch,
        input_output_aliases=aliases,
        compiler_params=pltpu.CompilerParams(vmem_limit_bytes=mib << 20),
    )


def here():
    r, c = lax.axis_index("row"), lax.axis_index("col")
    role = lax.rem(c, 2)
    keep = role == lax.rem(r, 2)
    half = lax.rem(lax.div(c, 2), 2)
    edge = jnp.where(role == 0, r < 2, r >= lax.axis_size("row") - 2)
    return role, keep, half, edge, c


def rotate_kernel(places, width, counts, rotation, *refs):
    pieces, out = refs[: len(places)], refs[len(places)]
    rot = rotation[...]
    high = rot.astype(BF16)
    low = (rot - high.astype(F32)).astype(BF16)
    mine, used = here()[4], counts[0] * width
    for place, piece in zip(places, pieces):
        rows = piece.shape[0]
        first = pl.multiple_of((mine ^ place) * rows, rows)
        x = piece[...]
        y = jnp.dot(x, high, preferred_element_type=F32) + jnp.dot(x, low, preferred_element_type=F32)
        at = first + lax.broadcasted_iota(jnp.int32, y.shape, 0)
        out[pl.ds(first, rows), :] = jnp.where(at < used, y, 0.0).astype(BF16)


def build_kernel(lot, held, cap, nblk, width, info, blocks, *refs):
    count = 1 + max(which for _, _, sources in lot for which, _ in sources)
    moved, refs = list(refs[:count]), refs[count:]
    near_out, far_out, raw, total, sems = refs[-5:]
    role, keep, half, at_edge, _ = here()
    slots = total.shape[0]
    near_slots = near_out.shape[1] // width
    parts = 4
    piece = nblk // parts
    place = lambda step, direct: row_of(half, step, direct, cap)

    def build(source, t):
        total[...] = jnp.zeros_like(total)
        for k in range(nblk):
            slot = slot_place(info[1 + t * nblk + k], role, cap, slots)
            total[slot] = total[slot] + source(k).astype(F32)
        scale = jnp.where(t < info[0], 2.0, 0.0).astype(F32)
        far_scale = jnp.where(at_edge, 0.0, scale)
        at = pl.ds(pl.multiple_of(t * width, width), width)
        for slot in range(slots):
            near = slot < near_slots
            lane = (slot if near else slot - near_slots) * width
            value = total[slot] * (scale if near else far_scale)
            (near_out if near else far_out)[at, lane : lane + width] = value.astype(BF16)

    def loads(n, t):
        cut = lambda p: pl.ds(p * piece, piece)
        return [
            pltpu.make_async_copy(blocks.at[t, cut(p)], raw.at[n, cut(p)], sems.at[n, p])
            for p in range(parts)
        ]

    if held:
        @pl.when(keep)
        def _():
            for n, row in enumerate(held):
                for copy in loads(n, place(*row)):
                    copy.start()

            def one(n, carry):
                steps = sum(jnp.where(n == at, step, 0) for at, (step, _) in enumerate(held))
                direct = sum(jnp.where(n == at, int(direct), 0) for at, (_, direct) in enumerate(held))
                t = place(steps, direct)
                for copy in loads(n, t):
                    copy.wait()
                build(lambda k: raw[n, k], t)
                return carry

            lax.fori_loop(0, len(held), one, 0)

    @pl.when(jnp.logical_not(keep))
    def _():
        for step, direct, sources in lot:
            each = nblk // len(sources)

            def source(k):
                which, first = sources[k // each]
                return moved[which][0, first + k % each]

            build(source, place(step, direct))


def gather_kernel(counts, cols, lists, out):
    out[0] = counts[0]
    at = 1
    for t in range(cols.shape[0]):
        for k in range(cols.shape[1]):
            out[at] = cols[t, k]
            at += 1
    for way in range(lists.shape[1]):
        for i in range(lists.shape[2]):
            out[at] = lists[0, way, i]
            at += 1


def tables_kernel(own, moved, info, send_lists, spread):
    role, keep = here()[:2]
    get = lambda i: jnp.where(keep, own[i], moved[i])
    slots = info.shape[0]
    for i in range(slots):
        info[i] = get(i)
    edge = send_lists.shape[0] // 2
    for i in range(edge):
        up, down = get(slots + i), get(slots + edge + i)
        send_lists[i] = jnp.where(role == 0, up, down)
        send_lists[edge + i] = jnp.where(role == 0, down, up)
    for i in range(2 * edge):
        spread[i : i + 1, :] = jnp.full((1, spread.shape[1]), send_lists[i].astype(F32), F32)


def row_of(half, step, direct, cap):
    flip = jnp.where(direct == 1, half, 1 - half)
    return jnp.where(flip == 1, cap - 1 - step, step)


def stage_kernel(cuts, cap, blocks, *refs):
    outs, sems = refs[:-1], refs[-1]
    half = here()[2]
    copies = []
    for n, (pieces, out) in enumerate(zip(cuts, outs)):
        at = 0
        for p, (step, first, count) in enumerate(pieces):
            src = blocks.at[row_of(half, step, 1, cap), pl.ds(first, count)]
            copies.append(pltpu.make_async_copy(src, out.at[0, pl.ds(at, count)], sems.at[n, p]))
            at += count
    for copy in copies:
        copy.start()
    for copy in copies:
        copy.wait()


def slot_place(slot, role, cap, slots):
    edge = (slots - cap) // 2
    first = jnp.where(slot < edge, slot + slots - edge, slot - edge)
    second = jnp.where(slot < edge, slot + cap, jnp.where(slot < edge + cap, slot - edge, slot))
    return jnp.where(role == 0, first, second)


def pick(lists, first, edge, width):
    return [pl.ds(pl.multiple_of(lists[first + i] * width, width), width) for i in range(edge)]


def pack_kernel(width, edge, lists, own, moved, field, near_send, far_send):
    keep = here()[1]

    @pl.when(keep)
    def _():
        field[...] = own[...]

    @pl.when(jnp.logical_not(keep))
    def _():
        field[...] = moved[...]

    for first, send in ((0, near_send), (edge, far_send)):
        for i, rows in enumerate(pick(lists, first, edge, width)):
            send[i * width : (i + 1) * width, :] = field[rows, :]


def picked(spread, first, edge, width):
    index = lambda i: jnp.max(spread[i : i + 1, :]).astype(jnp.int32)
    return [pl.ds(pl.multiple_of(index(first + i) * width, width), width) for i in range(edge)]


def local_kernel(width, edge, less, gives, lists, near_op, field, near, *refs):
    refs = list(refs)
    ats = picked(lists, edge, edge, width), picked(lists, 0, edge, width)
    rows = field.shape[0]
    older = refs.pop(0) if less else None
    far_op = refs.pop(0) if gives == "both" else None
    acc = refs.pop(0)
    total = jnp.dot(near_op[:, :rows], field[...], preferred_element_type=F32) + jnp.dot(
        near_op[:, rows:], near[...], preferred_element_type=F32
    )
    acc[...] = total - older[...].astype(F32) if less else total
    if not gives:
        return
    part, near_part = refs[:2]
    for out, places in zip((part, near_part), ats):
        for i, at in enumerate(places):
            out[i * width : (i + 1) * width, :] = acc[at, :].astype(out.dtype)
    if gives == "both":
        for i, at in enumerate(ats[0]):
            half, place = divmod(i, edge // 2)
            refs[2 + half][place * width : (place + 1) * width, :] = far_op[at, :]
        for i, at in enumerate(ats[1]):
            refs[4][i * width : (i + 1) * width, :] = far_op[at, :]


def result_of(first, acc, far_op, far):
    total = acc[...] + jnp.dot(far_op[...], far, preferred_element_type=F32)
    return 0.5 * total if first else total


def ahead_kernel(first, acc, low, high, far, out):
    half = low.shape[0]
    for at, op in ((0, low), (half, high)):
        rows = pl.ds(at, half)
        total = acc[rows, :] + jnp.dot(op[...], far[...], preferred_element_type=F32)
        out[rows, :] = (0.5 * total if first else total).astype(BF16)


def far_rows(part, low, high, sent, out):
    half = low.shape[0]
    for at, op in ((0, low), (half, high)):
        rows = pl.ds(at, half)
        total = part[rows, :].astype(F32) + jnp.dot(op[...], sent[...], preferred_element_type=F32)
        out[rows, :] = total.astype(BF16)


def mix_kernel(far_op, low, high, out):
    half = low.shape[0]
    total = jnp.dot(far_op[:, :half], low[...], preferred_element_type=F32) + jnp.dot(
        far_op[:, half:], high[...], preferred_element_type=F32
    )
    out[...] = total.astype(BF16)


def before_kernel(near_part, mixed, sent, out):
    out[...] = near_part[...] + jnp.dot(mixed[...], sent[...], preferred_element_type=F32)


def near_kernel(first, acc, far_op, far, out):
    out[...] = result_of(first, acc, far_op, far[...]).astype(BF16)


def finish_kernel(first, apart, wants, width, edge, spread, acc, far_op, *refs):
    refs = list(refs)
    if apart:
        far = refs.pop()
        far_rows(*refs[:4], far)
        refs = refs[4:]
    else:
        far = refs.pop(0)
    total = result_of(first, acc, far_op, far[...])
    value, part = wants
    if value:
        refs.pop(0)[...] = total
    field = refs[0]
    field[...] = total.astype(BF16)
    if part:
        for i, rows in enumerate(picked(spread, edge, edge, width)):
            refs[1][i * width : (i + 1) * width, :] = field[rows, :]


def last_kernel(begin, acc, far_op, part, low, high, sent, out, far):
    rows = pl.ds(begin, out.shape[1])
    far_rows(part, low, high, sent, far)
    total = acc[rows, :] + jnp.dot(far_op[rows, :], far[...], preferred_element_type=F32)
    out[...] = total.T.astype(BF16)


def merge_kernel(begin, own, moved, *refs):
    out, wide, sem = refs[-3:]
    keep = here()[1]

    @pl.when(keep)
    def _():
        wide[...] = own[...].astype(F32)

    @pl.when(jnp.logical_not(keep))
    def _():
        wide[...] = moved[...].astype(F32)

    copy = pltpu.make_async_copy(wide, out.at[:, pl.ds(begin, wide.shape[1])], sem)
    copy.start()
    copy.wait()


def body(vectors, rotation, blocks, cols, lists, counts):
    rows, columns = lax.axis_size("row"), lax.axis_size("col")
    ways = patterns(rows, columns)

    def send(x, way):
        return lax.ppermute(x, AXES, ways[way])

    cap, nblk, width = blocks.shape[0], blocks.shape[1], blocks.shape[2]
    edge = lists.shape[2]
    panel = rotation.shape[1]
    height = cap * width
    slots = cap + 2 * edge
    sds = jax.ShapeDtypeStruct

    ints = lambda n: sds((n,), jnp.int32)

    pieces = {0: vectors.astype(BF16)}
    bit = columns // 2
    while bit:
        for place in list(pieces):
            pieces[place ^ bit] = lax.ppermute(
                pieces[place], "col", [(k, k ^ bit) for k in range(columns)]
            )
        bit //= 2

    held = pltpu.with_memory_space_constraint(blocks, pltpu.HBM)
    middle, hb = cap // 2, nblk // 2
    block_rows = lambda count: sds((1, count, width, width), BF16)

    def stage(*cuts):
        return call(
            functools.partial(stage_kernel, cuts, cap),
            tuple(block_rows(sum(count for _, _, count in pieces)) for pieces in cuts),
            [HBM], (VMEM,) * len(cuts), scratch=(pltpu.SemaphoreType.DMA((len(cuts), 4)),),
        )(held)

    full = lambda k: ((k, 0, hb), (k, hb, hb))
    staged = stage(full(0))
    staged += stage(
        *(full(k) for k in range(1, middle - 2)),
        full(middle - 2) + ((middle - 1, hb, hb),), ((middle - 1, 0, hb),), ((middle, 0, hb),),
    )
    direct = [send(x, "trade") for x in staged]
    relayed = [send(x, "across") for x in direct[: middle - 1]]

    n_slots = 1 + cap * nblk
    own = call(gather_kernel, ints(n_slots + 2 * edge), [SMEM] * 3, SMEM)(counts, cols, lists)
    info, send_lists, spread = call(
        tables_kernel, (ints(n_slots), ints(2 * edge), sds((2 * edge, width), F32)),
        [SMEM] * 2, (SMEM, SMEM, VMEM),
    )(own, send(own, "trade"))

    field = call(
        functools.partial(rotate_kernel, tuple(pieces), width),
        sds((height, panel), BF16), [SMEM, VMEM] + [VMEM] * len(pieces), VMEM,
    )(counts, rotation, *pieces.values())
    moved_field = send(field, "trade")

    ops = ()
    op_shapes = (sds((height, height + edge * width), BF16), sds((height, edge * width), BF16))
    joint, low, extra = direct[middle - 2], direct[middle - 1], direct[middle]
    lots = [
        [(k, 1, ((k, 0),)) for k in range(middle - 2)],
        [(middle - 2, 1, ((0, 0),))],
        [(k, 0, ((k, 0),)) for k in range(middle - 2)],
        [(middle - 1, 1, ((0, 0), (1, nblk)))],
        [(middle - 2, 0, ((0, 0),)), (middle, 1, ((1, 0), (0, nblk)))],
    ]
    arrays = [direct[: middle - 2], [joint], relayed[: middle - 2], [low, joint], [relayed[-1], extra]]
    whole = sum([[row[:2] for row in lot] for lot in lots], [])
    holds = [whole[: cap // 2], whole[cap // 2 :], [], [], []]
    for lot, given, hold in zip(lots, arrays, holds):
        n = len(given)
        ops = call(
            functools.partial(build_kernel, lot, hold, cap, nblk, width),
            op_shapes, [SMEM, HBM] + [VMEM] * (n + len(ops)), (VMEM, VMEM),
            scratch=(
                pltpu.VMEM((max(1, len(hold)), nblk, width, width), BF16),
                pltpu.VMEM((slots, width, width), F32),
                pltpu.SemaphoreType.DMA((max(1, len(hold)), 4)),
            ),
            aliases={2 + n: 0, 3 + n: 1} if ops else {}, mib=20,
        )(info, held, *given, *ops)
    near_op, far_op = ops

    sent = sds((edge * width, panel), BF16)
    wide = lambda kind: sds((height, panel), kind)
    field, near_send, far_send = call(
        functools.partial(pack_kernel, width, edge), (wide(BF16), sent, sent),
        [SMEM, VMEM, VMEM], (VMEM,) * 3,
    )(send_lists, field, moved_field)
    older, newer = (), field
    part = lambda kind: sds((edge * width, panel), kind)
    square = sds((edge // 2 * width, edge * width), BF16)
    moved_part, sent_rows, theirs, mixed = None, {}, [], None
    for step in range(STEPS):
        plain = step <= PLAIN
        first, last = step == 0, step == STEPS - 1
        near = send(near_send, "near")
        if plain:
            far = send(far_send, "far")
            sent_rows[step] = far_send
        if 0 < step <= 2:
            theirs.append(send(far_part[step - 1], "far"))
        gives = "both" if first else "" if last else "one"
        kind = F32 if step < PLAIN else BF16
        outs = (wide(F32),) + ((part(kind), part(F32)) if gives else ())
        outs += (square, square, sds((edge * width, edge * width), BF16)) if first else ()
        given = (spread, near_op, field, near) + older + ((far_op,) if first else ())
        mine = call(
            functools.partial(local_kernel, width, edge, not first, gives), outs,
            [VMEM] * len(given), (VMEM,) * len(outs),
        )(*given)
        acc = mine[0]
        if first:
            far_part, near_far = mine[3:5], mine[5]
        arrived_part, moved_part = moved_part, None
        if PLAIN <= step and not last:
            moved_part = send(mine[1], "far")
        if last:
            cut = height // 2
            ends = [
                call(
                    functools.partial(last_kernel, begin), sds((panel, cut), BF16), [VMEM] * 6, VMEM,
                    scratch=(pltpu.VMEM((edge * width, panel), BF16),),
                )(acc, far_op, arrived_part, *theirs, sent_rows[step - 1])
                for begin in (0, cut)
            ]
            backs = [send(x, "trade") for x in ends]
            out = ()
            for at, (own, back) in enumerate(zip(ends, backs)):
                out = (
                    call(
                        functools.partial(merge_kernel, at * cut), sds((panel, height), F32),
                        [VMEM] * 2 + [HBM] * len(out), HBM,
                        scratch=(pltpu.VMEM((panel, cut), F32), pltpu.SemaphoreType.DMA),
                        aliases={2: 0} if out else {},
                    )(own, back, *out),
                )
            return out[0]
        if step < PLAIN:
            far_send = call(
                functools.partial(ahead_kernel, first), sent, [VMEM] * 4, VMEM
            )(mine[1], *far_part, far)
        ready, given, scratch = mine[2], (far,), ()
        if not plain:
            if mixed is None:
                mixed = call(
                    mix_kernel, sds((edge * width,) * 2, BF16), [VMEM] * 3, VMEM
                )(near_far, *theirs)
            ready = call(before_kernel, part(F32), [VMEM] * 3, VMEM)(
                mine[2], mixed, sent_rows[step - 1]
            )
            given = (arrived_part, *theirs, sent_rows[step - 1])
            scratch = (pltpu.VMEM((edge * width, panel), BF16),)
        near_send = call(
            functools.partial(near_kernel, first), sent, [VMEM] * 3, VMEM
        )(ready, near_far, given[0])
        wants = (step < STEPS - 2, PLAIN <= step < STEPS - 2)
        outs = ((wide(F32),) if wants[0] else ()) + (wide(BF16),) + ((sent,) if wants[1] else ())
        result = call(
            functools.partial(finish_kernel, first, not plain, wants, width, edge), outs,
            [VMEM] * (3 + len(given)), (VMEM,) * len(outs), scratch=scratch,
        )(spread, acc, far_op, *given)
        result = list(result)
        older, newer = (newer,), result.pop(0) if wants[0] else None
        field = result[0]
        if wants[1]:
            sent_rows[step + 1] = result[1]


def solution(mesh):
    return jax.shard_map(
        body,
        mesh=mesh,
        in_specs=(
            P(("row", "col"), None),
            P(None, "col"),
            P("row", None, None, None),
            P("row", None),
            P("row", None, None),
            P("row"),
        ),
        out_specs=P("col", "row"),
        check_vma=False,
    )
```

```python
import functools

import jax
import jax.numpy as jnp
from jax import lax
from jax.experimental import pallas as pl
from jax.experimental.pallas import tpu as pltpu
from jax.sharding import PartitionSpec as P


STEPS = 10
PLAIN = 2
AXES = ("row", "col")
F32, BF16 = jnp.float32, jnp.bfloat16
VMEM = pl.BlockSpec(memory_space=pltpu.VMEM)
SMEM = pl.BlockSpec(memory_space=pltpu.SMEM)
HBM = pl.BlockSpec(memory_space=pltpu.HBM)
ANY = pl.BlockSpec(memory_space=pl.ANY)


def patterns(rows, cols):
    every = [(r, c) for r in range(rows) for c in range(cols)]
    keeps = lambda r, c: r % 2 == c % 2

    def far(r, c):
        to = r + 2 if c % 2 else r - 2
        return (to, c ^ 1) if 0 <= to < rows else (r ^ 1, c)

    ways = {
        "trade": lambda r, c: (r ^ 2, c) if keeps(r, c) else (r ^ 1, c ^ 1),
        "across": lambda r, c: (r, c ^ 2),
        "near": lambda r, c: (r, c ^ 1),
        "far": far,
    }
    at = lambda place: place[0] * cols + place[1]
    pairs = {name: [(at(p), at(way(*p))) for p in every] for name, way in ways.items()}
    pairs["across"] = [(at(p), at(ways["across"](*p))) for p in every if not keeps(*p)]
    return pairs


def call(kernel, outs, in_specs, out_specs, scratch=(), aliases={}, mib=12):
    return pl.pallas_call(
        kernel,
        out_shape=outs,
        in_specs=in_specs,
        out_specs=out_specs,
        scratch_shapes=scratch,
        input_output_aliases=aliases,
        compiler_params=pltpu.CompilerParams(vmem_limit_bytes=mib << 20),
    )


def here():
    r, c = lax.axis_index("row"), lax.axis_index("col")
    role = lax.rem(c, 2)
    keep = role == lax.rem(r, 2)
    half = lax.rem(lax.div(c, 2), 2)
    edge = jnp.where(role == 0, r < 2, r >= lax.axis_size("row") - 2)
    return role, keep, half, edge, c


def rotate_kernel(places, width, counts, rotation, *refs):
    pieces, out = refs[: len(places)], refs[len(places)]
    rot = rotation[...]
    high = rot.astype(BF16)
    low = (rot - high.astype(F32)).astype(BF16)
    mine, used = here()[4], counts[0] * width
    for place, piece in zip(places, pieces):
        rows = piece.shape[0]
        first = pl.multiple_of((mine ^ place) * rows, rows)
        x = piece[...]
        y = jnp.dot(x, high, preferred_element_type=F32) + jnp.dot(x, low, preferred_element_type=F32)
        at = first + lax.broadcasted_iota(jnp.int32, y.shape, 0)
        out[pl.ds(first, rows), :] = jnp.where(at < used, y, 0.0).astype(BF16)


def build_kernel(lot, held, cap, nblk, width, info, blocks, *refs):
    count = sum(pieces for _, _, pieces in lot)
    moved, refs = list(refs[:count]), refs[count:]
    near_out, far_out, raw, total, sems = refs[-5:]
    role, keep, half, at_edge, _ = here()
    slots = total.shape[0]
    near_slots = near_out.shape[1] // width
    parts = 4
    piece = nblk // parts
    place = lambda step, direct: row_of(half, step, direct, cap)

    def build(source, t):
        total[...] = jnp.zeros_like(total)
        for k in range(nblk):
            slot = slot_place(info[1 + t * nblk + k], role, cap, slots)
            total[slot] = total[slot] + source(k).astype(F32)
        scale = jnp.where(t < info[0], 2.0, 0.0).astype(F32)
        far_scale = jnp.where(at_edge, 0.0, scale)
        at = pl.ds(pl.multiple_of(t * width, width), width)
        for slot in range(slots):
            near = slot < near_slots
            lane = (slot if near else slot - near_slots) * width
            value = total[slot] * (scale if near else far_scale)
            (near_out if near else far_out)[at, lane : lane + width] = value.astype(BF16)

    def loads(n, t):
        cut = lambda p: pl.ds(p * piece, piece)
        return [
            pltpu.make_async_copy(blocks.at[t, cut(p)], raw.at[n, cut(p)], sems.at[n, p])
            for p in range(parts)
        ]

    if held:
        @pl.when(keep)
        def _():
            for n, row in enumerate(held):
                for copy in loads(n, place(*row)):
                    copy.start()

            def one(n, carry):
                steps = sum(jnp.where(n == at, step, 0) for at, (step, _) in enumerate(held))
                direct = sum(jnp.where(n == at, int(direct), 0) for at, (_, direct) in enumerate(held))
                t = place(steps, direct)
                for copy in loads(n, t):
                    copy.wait()
                build(lambda k: raw[n, k], t)
                return carry

            lax.fori_loop(0, len(held), one, 0)

    @pl.when(jnp.logical_not(keep))
    def _():
        for step, direct, pieces in lot:
            arrays = [moved.pop(0) for _ in range(pieces)]
            each = nblk // pieces
            build(lambda k: arrays[k // each][0, k % each], place(step, direct))


def gather_kernel(counts, cols, lists, out):
    out[0] = counts[0]
    at = 1
    for t in range(cols.shape[0]):
        for k in range(cols.shape[1]):
            out[at] = cols[t, k]
            at += 1
    for way in range(lists.shape[1]):
        for i in range(lists.shape[2]):
            out[at] = lists[0, way, i]
            at += 1


def tables_kernel(own, moved, info, send_lists, spread):
    role, keep = here()[:2]
    get = lambda i: jnp.where(keep, own[i], moved[i])
    slots = info.shape[0]
    for i in range(slots):
        info[i] = get(i)
    edge = send_lists.shape[0] // 2
    for i in range(edge):
        up, down = get(slots + i), get(slots + edge + i)
        send_lists[i] = jnp.where(role == 0, up, down)
        send_lists[edge + i] = jnp.where(role == 0, down, up)
    for i in range(2 * edge):
        spread[i : i + 1, :] = jnp.full((1, spread.shape[1]), send_lists[i].astype(F32), F32)


def row_of(half, step, direct, cap):
    flip = jnp.where(direct == 1, half, 1 - half)
    return jnp.where(flip == 1, cap - 1 - step, step)


def stage_kernel(cuts, cap, blocks, *refs):
    outs, sems = refs[:-1], refs[-1]
    half = here()[2]
    copies = []
    for n, ((step, first, count), out) in enumerate(zip(cuts, outs)):
        piece = count // 2
        for p in range(2):
            copies.append(
                pltpu.make_async_copy(
                    blocks.at[row_of(half, step, 1, cap), pl.ds(first + p * piece, piece)],
                    out.at[0, pl.ds(p * piece, piece)], sems.at[n, p],
                )
            )
    for copy in copies:
        copy.start()
    for copy in copies:
        copy.wait()


def slot_place(slot, role, cap, slots):
    edge = (slots - cap) // 2
    first = jnp.where(slot < edge, slot + slots - edge, slot - edge)
    second = jnp.where(slot < edge, slot + cap, jnp.where(slot < edge + cap, slot - edge, slot))
    return jnp.where(role == 0, first, second)


def pick(lists, first, edge, width):
    return [pl.ds(pl.multiple_of(lists[first + i] * width, width), width) for i in range(edge)]


def pack_kernel(width, edge, lists, own, moved, field, near_send, far_send):
    keep = here()[1]

    @pl.when(keep)
    def _():
        field[...] = own[...]

    @pl.when(jnp.logical_not(keep))
    def _():
        field[...] = moved[...]

    for first, send in ((0, near_send), (edge, far_send)):
        for i, rows in enumerate(pick(lists, first, edge, width)):
            send[i * width : (i + 1) * width, :] = field[rows, :]


def picked(spread, first, edge, width):
    index = lambda i: jnp.max(spread[i : i + 1, :]).astype(jnp.int32)
    return [pl.ds(pl.multiple_of(index(first + i) * width, width), width) for i in range(edge)]


def local_kernel(width, edge, less, gives, lists, near_op, field, near, *refs):
    refs = list(refs)
    ats = picked(lists, edge, edge, width), picked(lists, 0, edge, width)
    rows = field.shape[0]
    older = refs.pop(0) if less else None
    far_op = refs.pop(0) if gives == "both" else None
    acc = refs.pop(0)
    total = jnp.dot(near_op[:, :rows], field[...], preferred_element_type=F32) + jnp.dot(
        near_op[:, rows:], near[...], preferred_element_type=F32
    )
    acc[...] = total - older[...].astype(F32) if less else total
    if not gives:
        return
    part, near_part = refs[:2]
    for out, places in zip((part, near_part), ats):
        for i, at in enumerate(places):
            out[i * width : (i + 1) * width, :] = acc[at, :].astype(out.dtype)
    if gives == "both":
        for i, at in enumerate(ats[0]):
            half, place = divmod(i, edge // 2)
            refs[2 + half][place * width : (place + 1) * width, :] = far_op[at, :]
        for i, at in enumerate(ats[1]):
            refs[4][i * width : (i + 1) * width, :] = far_op[at, :]


def result_of(first, acc, far_op, far):
    total = acc[...] + jnp.dot(far_op[...], far, preferred_element_type=F32)
    return 0.5 * total if first else total


def ahead_kernel(first, acc, low, high, far, out):
    half = low.shape[0]
    for at, op in ((0, low), (half, high)):
        rows = pl.ds(at, half)
        total = acc[rows, :] + jnp.dot(op[...], far[...], preferred_element_type=F32)
        out[rows, :] = (0.5 * total if first else total).astype(BF16)


def far_rows(part, low, high, sent, out):
    half = low.shape[0]
    for at, op in ((0, low), (half, high)):
        rows = pl.ds(at, half)
        total = part[rows, :].astype(F32) + jnp.dot(op[...], sent[...], preferred_element_type=F32)
        out[rows, :] = total.astype(BF16)


def mix_kernel(far_op, low, high, out):
    half = low.shape[0]
    total = jnp.dot(far_op[:, :half], low[...], preferred_element_type=F32) + jnp.dot(
        far_op[:, half:], high[...], preferred_element_type=F32
    )
    out[...] = total.astype(BF16)


def before_kernel(near_part, mixed, sent, out):
    out[...] = near_part[...] + jnp.dot(mixed[...], sent[...], preferred_element_type=F32)


def near_kernel(first, acc, far_op, far, out):
    out[...] = result_of(first, acc, far_op, far[...]).astype(BF16)


def finish_kernel(first, apart, wants, width, edge, spread, acc, far_op, *refs):
    refs = list(refs)
    if apart:
        far = refs.pop()
        far_rows(*refs[:4], far)
        refs = refs[4:]
    else:
        far = refs.pop(0)
    total = result_of(first, acc, far_op, far[...])
    value, part = wants
    if value:
        refs.pop(0)[...] = total
    field = refs[0]
    field[...] = total.astype(BF16)
    if part:
        for i, rows in enumerate(picked(spread, edge, edge, width)):
            refs[1][i * width : (i + 1) * width, :] = field[rows, :]


def last_kernel(begin, acc, far_op, part, low, high, sent, out, far):
    rows = pl.ds(begin, out.shape[1])
    far_rows(part, low, high, sent, far)
    total = acc[rows, :] + jnp.dot(far_op[rows, :], far[...], preferred_element_type=F32)
    out[...] = total.T.astype(BF16)


def merge_kernel(begin, own, moved, *refs):
    out, wide, sems = refs[-3:]
    keep = here()[1]
    pieces = 4
    piece = wide.shape[0] // pieces
    copies = []
    for n in range(pieces):
        rows = pl.ds(n * piece, piece)
        value = jnp.where(keep, own[rows, :], moved[rows, :])
        wide[rows, :] = value.astype(F32)
        copies.append(
            pltpu.make_async_copy(
                wide.at[rows, :], out.at[rows, pl.ds(begin, wide.shape[1])], sems.at[n]
            )
        )
        copies[-1].start()
    for copy in copies:
        copy.wait()


def body(vectors, rotation, blocks, cols, lists, counts):
    rows, columns = lax.axis_size("row"), lax.axis_size("col")
    ways = patterns(rows, columns)

    def send(x, way):
        return lax.ppermute(x, AXES, ways[way])

    cap, nblk, width = blocks.shape[0], blocks.shape[1], blocks.shape[2]
    edge = lists.shape[2]
    panel = rotation.shape[1]
    height = cap * width
    slots = cap + 2 * edge
    sds = jax.ShapeDtypeStruct

    ints = lambda n: sds((n,), jnp.int32)

    pieces = {0: vectors.astype(BF16)}
    bit = columns // 2
    while bit:
        for place in list(pieces):
            pieces[place ^ bit] = lax.ppermute(
                pieces[place], "col", [(k, k ^ bit) for k in range(columns)]
            )
        bit //= 2

    held = pltpu.with_memory_space_constraint(blocks, pltpu.HBM)
    middle, part_blocks = cap // 2, nblk // 2
    block_rows = lambda count: sds((1, count, width, width), BF16)

    def stage(*cuts):
        return call(
            functools.partial(stage_kernel, cuts, cap), tuple(block_rows(cut[2]) for cut in cuts),
            [HBM], (VMEM,) * len(cuts), scratch=(pltpu.SemaphoreType.DMA((len(cuts), 2)),),
        )(held)

    staged = stage((0, 0, nblk))
    staged += stage(
        *((k, 0, nblk) for k in range(1, middle - 1)),
        (middle - 1, part_blocks, part_blocks), (middle - 1, 0, part_blocks), (middle, 0, part_blocks),
    )
    direct = [send(x, "trade") for x in staged]
    relayed = [send(x, "across") for x in direct[:middle]]

    n_slots = 1 + cap * nblk
    own = call(gather_kernel, ints(n_slots + 2 * edge), [SMEM] * 3, SMEM)(counts, cols, lists)
    info, send_lists, spread = call(
        tables_kernel, (ints(n_slots), ints(2 * edge), sds((2 * edge, width), F32)),
        [SMEM] * 2, (SMEM, SMEM, VMEM),
    )(own, send(own, "trade"))

    field = call(
        functools.partial(rotate_kernel, tuple(pieces), width),
        sds((height, panel), BF16), [SMEM, VMEM] + [VMEM] * len(pieces), VMEM,
    )(counts, rotation, *pieces.values())
    moved_field = send(field, "trade")

    ops = ()
    op_shapes = (sds((height, height + edge * width), BF16), sds((height, edge * width), BF16))
    low, high, extra = direct[middle], direct[middle - 1], direct[middle + 1]
    cut = middle // 2
    lots = [
        [(k, 1, (direct[k],)) for k in range(cut)],
        [(k, 1, (direct[k],)) for k in range(cut, middle - 1)],
        [(k, 0, (relayed[k],)) for k in range(middle - 2)],
        [(middle - 2, 0, (relayed[middle - 2],)), (middle - 1, 1, (low, high))],
        [(middle, 1, (extra, relayed[middle - 1]))],
    ]
    whole = sum([[row[:2] for row in lot] for lot in lots], [])
    holds = [whole[: cap // 2], whole[cap // 2 :], [], [], []]
    for lot, hold in zip(lots, holds):
        given = [x for row in lot for x in row[2]]
        n = len(given)
        ops = call(
            functools.partial(build_kernel, [(*row[:2], len(row[2])) for row in lot], hold, cap, nblk, width),
            op_shapes, [SMEM, HBM] + [VMEM] * (n + len(ops)), (VMEM, VMEM),
            scratch=(
                pltpu.VMEM((max(1, len(hold)), nblk, width, width), BF16),
                pltpu.VMEM((slots, width, width), F32),
                pltpu.SemaphoreType.DMA((max(1, len(hold)), 4)),
            ),
            aliases={2 + n: 0, 3 + n: 1} if ops else {}, mib=20,
        )(info, held, *given, *ops)
    near_op, far_op = ops

    sent = sds((edge * width, panel), BF16)
    wide = lambda kind: sds((height, panel), kind)
    field, near_send, far_send = call(
        functools.partial(pack_kernel, width, edge), (wide(BF16), sent, sent),
        [SMEM, VMEM, VMEM], (VMEM,) * 3,
    )(send_lists, field, moved_field)
    older, newer = (), field
    part = lambda kind: sds((edge * width, panel), kind)
    square = sds((edge // 2 * width, edge * width), BF16)
    moved_part, sent_rows, theirs, mixed = None, {}, [], None
    for step in range(STEPS):
        plain = step <= PLAIN
        first, last = step == 0, step == STEPS - 1
        near = send(near_send, "near")
        if plain:
            far = send(far_send, "far")
            sent_rows[step] = far_send
        if 0 < step <= 2:
            theirs.append(send(far_part[step - 1], "far"))
        gives = "both" if first else "" if last else "one"
        kind = F32 if step < PLAIN else BF16
        outs = (wide(F32),) + ((part(kind), part(F32)) if gives else ())
        outs += (square, square, sds((edge * width, edge * width), BF16)) if first else ()
        given = (spread, near_op, field, near) + older + ((far_op,) if first else ())
        mine = call(
            functools.partial(local_kernel, width, edge, not first, gives), outs,
            [VMEM] * len(given), (VMEM,) * len(outs),
        )(*given)
        acc = mine[0]
        if first:
            far_part, near_far = mine[3:5], mine[5]
        arrived_part, moved_part = moved_part, None
        if PLAIN <= step and not last:
            moved_part = send(mine[1], "far")
        if last:
            cut = height // 2
            ends = [
                call(
                    functools.partial(last_kernel, begin), sds((panel, cut), BF16), [VMEM] * 6, VMEM,
                    scratch=(pltpu.VMEM((edge * width, panel), BF16),),
                )(acc, far_op, arrived_part, *theirs, sent_rows[step - 1])
                for begin in (0, cut)
            ]
            backs = [send(x, "trade") for x in ends]
            out = ()
            for at, (own, back) in enumerate(zip(ends, backs)):
                out = (
                    call(
                        functools.partial(merge_kernel, at * cut), sds((panel, height), F32),
                        [VMEM] * 2 + [HBM] * len(out), HBM,
                        scratch=(pltpu.VMEM((panel, cut), F32), pltpu.SemaphoreType.DMA((4,))),
                        aliases={2: 0} if out else {},
                    )(own, back, *out),
                )
            return out[0]
        if step < PLAIN:
            far_send = call(
                functools.partial(ahead_kernel, first), sent, [VMEM] * 4, VMEM
            )(mine[1], *far_part, far)
        ready, given, scratch = mine[2], (far,), ()
        if not plain:
            if mixed is None:
                mixed = call(
                    mix_kernel, sds((edge * width,) * 2, BF16), [VMEM] * 3, VMEM
                )(near_far, *theirs)
            ready = call(before_kernel, part(F32), [VMEM] * 3, VMEM)(
                mine[2], mixed, sent_rows[step - 1]
            )
            given = (arrived_part, *theirs, sent_rows[step - 1])
            scratch = (pltpu.VMEM((edge * width, panel), BF16),)
        near_send = call(
            functools.partial(near_kernel, first), sent, [VMEM] * 3, VMEM
        )(ready, near_far, given[0])
        wants = (step < STEPS - 2, PLAIN <= step < STEPS - 2)
        outs = ((wide(F32),) if wants[0] else ()) + (wide(BF16),) + ((sent,) if wants[1] else ())
        result = call(
            functools.partial(finish_kernel, first, not plain, wants, width, edge), outs,
            [VMEM] * (3 + len(given)), (VMEM,) * len(outs), scratch=scratch,
        )(spread, acc, far_op, *given)
        result = list(result)
        older, newer = (newer,), result.pop(0) if wants[0] else None
        field = result[0]
        if wants[1]:
            sent_rows[step + 1] = result[1]


def solution(mesh):
    return jax.shard_map(
        body,
        mesh=mesh,
        in_specs=(
            P(("row", "col"), None),
            P(None, "col"),
            P("row", None, None, None),
            P("row", None),
            P("row", None, None),
            P("row"),
        ),
        out_specs=P("col", "row"),
        check_vma=False,
    )
```
